32 devices in a mesh: dp: 16 (over z, y, core), tensor: 2 (over x).
Axes of the slice: x: 2, y: 2, z: 4, core: 2. Of those that a mesh axis runs over, the one named last changes fastest.
Arguments:
- inputs: float32 [16384, 768], P(('dp', 'tensor')), may hold values from -6 to 6
- seq_ids: int32 [16, 1024], P('dp'), may hold values from 0 to 15, never falling along the last dimension, each value on 1 to 128 neighbouring positions
- norm1_gain: bfloat16 [768], P(('dp', 'tensor')), may hold values from 0.5 to 1.5
- norm1_shift: bfloat16 [768], P(('dp', 'tensor')), may hold values from -3 to 3
- qkv_weight: bfloat16 [3, 768, 768], P(None, 'dp', 'tensor'), may hold values from -0.21875 to 0.21875
- qv_bias: bfloat16 [2, 12, 64], P(None, 'tensor', 'dp'), may hold values from -3 to 3
- out_weight: bfloat16 [768, 768], P('tensor', 'dp'), may hold values from -0.875 to 0.875
- out_bias: bfloat16 [768], P(('dp', 'tensor')), may hold values from -3 to 3
- norm2_gain: bfloat16 [768], P(('dp', 'tensor')), may hold values from 0.5 to 1.5
- norm2_shift: bfloat16 [768], P(('dp', 'tensor')), may hold values from -3 to 3
- up_weight: bfloat16 [768, 3072], P('dp', 'tensor'), may hold values from -0.21875 to 0.21875
- up_bias: bfloat16 [48, 64], P('tensor', 'dp'), may hold values from -3 to 3
- down_weight: bfloat16 [3072, 768], P('tensor', 'dp'), may hold values from -0.109375 to 0.109375
- down_bias: bfloat16 [768], P(('dp', 'tensor')), may hold values from -3 to 3
- out_cotangent: float32 [16384, 768], P(('dp', 'tensor')), may hold values from -6 to 6
Outputs:
- layer_out: float32 [16384, 768], P(('dp', 'tensor'))
- input_grad: float32 [16384, 768], P(('dp', 'tensor'))
- norm1_gain_grad: float32 [768], P(('dp', 'tensor'))
- norm1_shift_grad: float32 [768], P(('dp', 'tensor'))
- qkv_weight_grad: float32 [3, 768, 768], P(None, 'dp', 'tensor')
- qv_bias_grad: float32 [2, 12, 64], P(None, 'tensor', 'dp')
- out_weight_grad: float32 [768, 768], P('tensor', 'dp')
- out_bias_grad: float32 [768], P(('dp', 'tensor'))
- norm2_gain_grad: float32 [768], P(('dp', 'tensor'))
- norm2_shift_grad: float32 [768], P(('dp', 'tensor'))
- up_weight_grad: float32 [768, 3072], P('dp', 'tensor')
- up_bias_grad: float32 [48, 64], P('tensor', 'dp')
- down_weight_grad: float32 [3072, 768], P('tensor', 'dp')
- down_bias_grad: float32 [768], P(('dp', 'tensor'))
The draws below stay inside these ranges and needn't reach their ends.
Inputs may be any that keep to these rules, and one draw needn't show every extreme that they name: In each row of seq_ids (one data group of 1024 tokens) the numbers never fall; each number marks one sequence of consecutive tokens, of 1 to 128 tokens, and at least one sequence has exactly 128 tokens.
All inputs are finite; a program needn't handle non-finite values.
Results may differ from the reference program's by a relative error of at most 0.012.
Values may be sent and summed in bfloat16 or wider, within the bound.
A program may use at most 128 MiB of HBM per device.

```python
import math
import jax
import jax.numpy as jnp
import numpy as np
from jax import lax

D = 768
H = 12
HD = 64
FF = 3072
TOK_DEV = 1024
SEQ_MAX = 128
SEQS = 16
GROUPS = 16
TOKENS = 16384


def strengthened(entries, own_key, source, target, shards_of, factor):
    def block_of(position):
        return (jnp.arange(entries.shape[position]) // (entries.shape[position] // shards_of)).reshape((-1,) + (1,) * (entries.ndim - 1 - position))

    first = jax.random.permutation(own_key, shards_of)[block_of(target)]
    far = (block_of(target) + shards_of // 2) % shards_of
    return jnp.where((block_of(source) == first) | (block_of(source) == far), factor * entries, entries)


def block_levels(key, shape, pieces, smallest, high):
    def one(axis_at, blocks):
        heights = jax.random.uniform(jax.random.fold_in(jax.random.fold_in(key, 6), axis_at), (blocks,), jnp.float32, smallest / len(pieces), high / len(pieces))
        return jnp.repeat(jnp.exp(heights), shape[axis_at] // blocks).reshape((-1,) + (1,) * (len(shape) - axis_at - 1))

    factor_of = one(*pieces[0])
    for cut in pieces[1:]:
        factor_of = factor_of * one(*cut)
    return factor_of


def split_up(number_of, total, bound, slope):
    portions = [(1 << 20) // math.isqrt(rank ** slope) + 1 for rank in range(2, number_of + 1)]
    surplus, counts = total - bound - (number_of - 1), [1] * (number_of - 1)
    while surplus > 0:
        free = [i for i in range(number_of - 1) if counts[i] < bound]
        whole, budget = sum([portions[i] for i in free]), surplus
        for i in free:
            extra = min(bound - counts[i], max(1, budget * portions[i] // whole), surplus)
            counts[i] = counts[i] + extra
            surplus = surplus - extra
    return np.array([bound] + counts)


def ragged_sizes(rng, count, total, bound, lean):
    if count == 2:
        one = jax.random.randint(rng, (), max(1, total - bound), min(bound, total - 1) + 1)
        return jnp.stack([one, total - one])
    lengths = jnp.asarray(split_up(count, total, bound, lean), jnp.int32)
    twos = (count - 1) // 2
    giver, receiver = lengths[1:1 + 2 * twos:2], lengths[2:2 + 2 * twos:2]
    slack = jnp.minimum(giver - 1, bound - receiver)
    moved = jax.random.randint(jax.random.fold_in(rng, 1), (twos,), 0, 1 << 20) % (slack + 1)
    lengths = lengths.at[1:1 + 2 * twos:2].set(giver - moved).at[2:2 + 2 * twos:2].set(receiver + moved)
    return lengths[jax.random.permutation(jax.random.fold_in(rng, 2), count)]


def noise(key, dims, scale, reach, shards=(), held_as=jnp.bfloat16):
    factor_of = block_levels(key, dims, shards, -0.22, 0.18) if shards else 1.0
    array = jax.random.normal(key, dims, jnp.float32) * scale * factor_of
    return jnp.minimum(jnp.maximum(array, -reach), reach).astype(held_as)


def gaussian_with(key, dims, spread, limit, cuts, heavy, held_as=jnp.bfloat16):
    array = spread * jax.random.normal(key, dims, jnp.float32)
    if cuts:
        array = array * block_levels(key, dims, cuts, -0.22, 0.18)
    return jnp.clip(strengthened(array, jax.random.fold_in(key, 3), *heavy), -limit, limit).astype(held_as)


def setup_inputs(seed: int = 0) -> dict:
    keys = jax.random.split(jax.random.key(seed), 16)
    inputs = gaussian_with(keys[0], (TOKENS, D), 1.0, 6.0, ((0, 32),), (0, 1, 32, 2.75), jnp.float32)
    seq_ids = jax.vmap(lambda own: jnp.searchsorted(jnp.cumsum(ragged_sizes(own, SEQS, TOK_DEV, SEQ_MAX, 2)), jnp.arange(TOK_DEV), side="right"))(jax.random.split(keys[1], GROUPS)).reshape((GROUPS, TOK_DEV)).astype(jnp.int32)
    norm1_gain = jnp.clip(1.0 + 0.1 * jax.random.normal(keys[2], (D,), jnp.float32), 0.5, 1.5).astype(jnp.bfloat16)
    norm1_shift = noise(keys[3], (D,), 0.5, 3.0, ((0, 32),))
    qkv_weight = noise(keys[4], (3, D, D), D ** -0.5, 0.21875, ((1, 16), (2, 2)))
    qv_bias = noise(keys[5], (2, H, HD), 0.5, 3.0, ((1, 2), (2, 16)))
    out_weight = noise(keys[6], (D, D), (D // 16) ** -0.5, 0.875, ((0, 2), (1, 16)))
    out_bias = noise(keys[7], (D,), 0.5, 3.0, ((0, 32),))
    norm2_gain = jnp.clip(1.0 + 0.1 * jax.random.normal(keys[8], (D,), jnp.float32), 0.5, 1.5).astype(jnp.bfloat16)
    norm2_shift = noise(keys[9], (D,), 0.5, 3.0, ((0, 32),))
    up_weight = noise(keys[10], (D, FF), D ** -0.5, 0.21875, ((0, 16), (1, 2)))
    up_bias = noise(keys[11], (FF // HD, HD), 0.5, 3.0, ((0, 2), (1, 16)))
    down_weight = noise(keys[12], (FF, D), FF ** -0.5, 0.109375, ((0, 2), (1, 16)))
    down_bias = noise(keys[13], (D,), 0.5, 3.0, ((0, 32),))
    out_cotangent = gaussian_with(keys[14], (TOKENS, D), 1.0, 6.0, ((0, 32),), (0, 1, 32, 2.75), jnp.float32)
    return dict(inputs=inputs, seq_ids=seq_ids, norm1_gain=norm1_gain, norm1_shift=norm1_shift, qkv_weight=qkv_weight, qv_bias=qv_bias, out_weight=out_weight, out_bias=out_bias, norm2_gain=norm2_gain, norm2_shift=norm2_shift, up_weight=up_weight, up_bias=up_bias, down_weight=down_weight, down_bias=down_bias, out_cotangent=out_cotangent)


eps = 1e-05
scale_factor = 0.125

def gelu_forward(pre_act):
    return jax.nn.gelu(pre_act, approximate=True)

def gelu_backward(pre_act, cotangent):
    return jax.vjp(gelu_forward, pre_act)[1](cotangent)[0]

def norm_forward(row_data, gain_vec, shift_vec):
    row_mean = lax.optimization_barrier(jnp.mean(row_data, axis=-1, keepdims=True))
    centred = row_data - row_mean
    inv_std = lax.rsqrt(lax.optimization_barrier(jnp.mean(centred * centred, axis=-1, keepdims=True)) + eps)
    normed = centred * inv_std
    scaled = normed * gain_vec.astype(jnp.float32) + shift_vec.astype(jnp.float32)
    return (normed, inv_std, scaled.astype(jnp.bfloat16))

def norm_backward(grad_norm, normed, inv_std, gain_vec):
    scaled = grad_norm * gain_vec.astype(jnp.float32)
    first_mean = lax.optimization_barrier(jnp.mean(scaled, axis=-1, keepdims=True))
    second_mean = lax.optimization_barrier(jnp.mean(scaled * normed, axis=-1, keepdims=True))
    return inv_std * (scaled - first_mean - normed * second_mean)

def group_pass(params, row_data, seq_row, cotangent):
    gain_one, shift_one, qkv_full, qv_full, out_full, bias_out, gain_two, shift_two, up_full, up_bias_full, down_full, bias_down = params
    row_count = row_data.shape[0]
    normed_one, inv_one, ln_one = norm_forward(row_data, gain_one, shift_one)
    projected = jnp.einsum('rd,cdk->crk', ln_one.astype(jnp.float32), qkv_full.astype(jnp.float32))
    bias_rows = qv_full.astype(jnp.float32).reshape(2, D)
    query_heads = (projected[0] + bias_rows[0]).astype(jnp.bfloat16).reshape(row_count, H, HD)
    key_heads = projected[1].astype(jnp.bfloat16).reshape(row_count, H, HD)
    value_heads = (projected[2] + bias_rows[1]).astype(jnp.bfloat16).reshape(row_count, H, HD)
    scores = jnp.einsum('qhe,khe->hqk', query_heads.astype(jnp.float32), key_heads.astype(jnp.float32)) * scale_factor
    positions = lax.iota(jnp.int32, row_count)
    allowed = ((seq_row[:, None] == seq_row[None, :]) & (positions[None, :] <= positions[:, None]))[None]
    log_total = jnp.log(lax.optimization_barrier(jnp.sum(jnp.where(allowed, jnp.exp(scores), 0.0), axis=-1)))
    probs_full = jnp.where(allowed, jnp.exp(scores - log_total[:, :, None]), 0.0)
    attn_probs = probs_full.astype(jnp.bfloat16)
    mixed_heads = jnp.einsum('hqk,khe->qhe', attn_probs.astype(jnp.float32), value_heads.astype(jnp.float32)).astype(jnp.bfloat16)
    mixed_flat = mixed_heads.reshape(row_count, D)
    middle = row_data + jnp.dot(mixed_flat, out_full, preferred_element_type=jnp.float32) + bias_out.astype(jnp.float32)
    normed_two, inv_two, ln_two = norm_forward(middle, gain_two, shift_two)
    pre_act = jnp.dot(ln_two, up_full, preferred_element_type=jnp.float32) + up_bias_full.astype(jnp.float32).reshape(FF)
    hidden = gelu_forward(pre_act).astype(jnp.bfloat16)
    layer_out = middle + jnp.dot(hidden, down_full, preferred_element_type=jnp.float32) + bias_down.astype(jnp.float32)
    cot_bf = cotangent.astype(jnp.bfloat16)
    down_grad = jnp.dot(hidden.T, cot_bf, preferred_element_type=jnp.float32)
    grad_pre = gelu_backward(pre_act, jnp.dot(cot_bf, down_full.T, preferred_element_type=jnp.float32))
    grad_pre_bf = grad_pre.astype(jnp.bfloat16)
    up_grad = jnp.dot(ln_two.T, grad_pre_bf, preferred_element_type=jnp.float32)
    up_bias_grad = lax.optimization_barrier(jnp.sum(grad_pre, axis=0)).reshape(FF // HD, HD)
    grad_ln_two = jnp.dot(grad_pre_bf, up_full.T, preferred_element_type=jnp.float32)
    gain_two_grad = lax.optimization_barrier(jnp.sum(grad_ln_two * normed_two, axis=0))
    shift_two_grad = lax.optimization_barrier(jnp.sum(grad_ln_two, axis=0))
    grad_middle = cotangent + norm_backward(grad_ln_two, normed_two, inv_two, gain_two)
    bias_down_grad = lax.optimization_barrier(jnp.sum(cotangent, axis=0))
    bias_out_grad = lax.optimization_barrier(jnp.sum(grad_middle, axis=0))
    mid_bf = grad_middle.astype(jnp.bfloat16)
    out_grad = jnp.dot(mixed_flat.T, mid_bf, preferred_element_type=jnp.float32)
    grad_mixed = jnp.dot(mid_bf, out_full.T, preferred_element_type=jnp.float32).astype(jnp.bfloat16).reshape(row_count, H, HD)
    row_delta = lax.optimization_barrier(jnp.sum(grad_mixed.astype(jnp.float32) * mixed_heads.astype(jnp.float32), axis=-1))
    value_grad = jnp.einsum('hqk,qhe->khe', attn_probs.astype(jnp.float32), grad_mixed.astype(jnp.float32))
    grad_probs = jnp.einsum('qhe,khe->hqk', grad_mixed.astype(jnp.float32), value_heads.astype(jnp.float32))
    grad_scores = (probs_full * (grad_probs - row_delta.T[:, :, None]) * scale_factor).astype(jnp.bfloat16)
    query_grad = jnp.einsum('hqk,khe->qhe', grad_scores.astype(jnp.float32), key_heads.astype(jnp.float32))
    key_grad = jnp.einsum('hqk,qhe->khe', grad_scores.astype(jnp.float32), query_heads.astype(jnp.float32))
    grad_qkv = jnp.stack([query_grad, key_grad, value_grad]).astype(jnp.bfloat16).reshape(3, row_count, D)
    qkv_grad = jnp.einsum('rd,crk->cdk', ln_one.astype(jnp.float32), grad_qkv.astype(jnp.float32))
    qv_grad = jnp.stack([lax.optimization_barrier(jnp.sum(query_grad, axis=0)), lax.optimization_barrier(jnp.sum(value_grad, axis=0))])
    grad_ln_one = jnp.einsum('crk,cdk->rd', grad_qkv.astype(jnp.float32), qkv_full.astype(jnp.float32))
    gain_one_grad = lax.optimization_barrier(jnp.sum(grad_ln_one * normed_one, axis=0))
    shift_one_grad = lax.optimization_barrier(jnp.sum(grad_ln_one, axis=0))
    input_grad = grad_middle + norm_backward(grad_ln_one, normed_one, inv_one, gain_one)
    grads = (gain_one_grad, shift_one_grad, qkv_grad, qv_grad, out_grad, bias_out_grad, gain_two_grad, shift_two_grad, up_grad, up_bias_grad, down_grad, bias_down_grad)
    return (layer_out, input_grad, grads)

def reference(inputs, seq_ids, norm1_gain, norm1_shift, qkv_weight, qv_bias, out_weight, out_bias, norm2_gain, norm2_shift, up_weight, up_bias, down_weight, down_bias, out_cotangent):
    params = (norm1_gain, norm1_shift, qkv_weight, qv_bias, out_weight, out_bias, norm2_gain, norm2_shift, up_weight, up_bias, down_weight, down_bias)
    grouped_rows = inputs.reshape(GROUPS, TOK_DEV, D)
    grouped_cot = out_cotangent.reshape(GROUPS, TOK_DEV, D)

    def group_step(grad_total, scan_inputs):
        row_data, seq_row, cotangent = scan_inputs
        layer_out, input_grad, grads = group_pass(params, row_data, seq_row, cotangent)
        return (jax.tree.map(jnp.add, grad_total, grads), (layer_out, input_grad))
    zero_grads = (jnp.zeros((D,), jnp.float32), jnp.zeros((D,), jnp.float32), jnp.zeros((3, D, D), jnp.float32), jnp.zeros((2, H, HD), jnp.float32), jnp.zeros((D, D), jnp.float32), jnp.zeros((D,), jnp.float32), jnp.zeros((D,), jnp.float32), jnp.zeros((D,), jnp.float32), jnp.zeros((D, FF), jnp.float32), jnp.zeros((FF // HD, HD), jnp.float32), jnp.zeros((FF, D), jnp.float32), jnp.zeros((D,), jnp.float32))
    grad_total, (outputs, input_grads) = lax.scan(group_step, zero_grads, (grouped_rows, seq_ids, grouped_cot))
    return (outputs.reshape(TOKENS, D), input_grads.reshape(TOKENS, D), grad_total[0], grad_total[1], grad_total[2], grad_total[3], grad_total[4], grad_total[5], grad_total[6], grad_total[7], grad_total[8], grad_total[9], grad_total[10], grad_total[11])
```

```python
import functools

import jax
import jax.numpy as jnp
from jax import lax
from jax.experimental import pallas as pl
from jax.experimental.pallas import tpu as pltpu
from jax.sharding import PartitionSpec as P

HD = 64
SEQ_MAX = 128
LANES = 128
VMEM_BYTES = 60 * 1024 * 1024

eps = 1e-05
scale_factor = 0.125
MESH = pl.DeviceIdType.MESH


def gelu_forward(pre_act):
    return jax.nn.gelu(pre_act, approximate=True)


def gelu_backward(pre_act, cotangent):
    return jax.vjp(gelu_forward, pre_act)[1](cotangent)[0]


def norm_forward(row_data, gain_vec, shift_vec):
    row_mean = jnp.mean(row_data, axis=-1, keepdims=True)
    centred = row_data - row_mean
    inv_std = lax.rsqrt(jnp.mean(centred * centred, axis=-1, keepdims=True) + eps)
    normed = centred * inv_std
    scaled = normed * gain_vec.astype(jnp.float32) + shift_vec.astype(jnp.float32)
    return (normed, inv_std, scaled.astype(jnp.bfloat16))


def norm_backward(grad_norm, normed, inv_std, gain_vec):
    scaled = grad_norm * gain_vec.astype(jnp.float32)
    first_mean = jnp.mean(scaled, axis=-1, keepdims=True)
    second_mean = jnp.mean(scaled * normed, axis=-1, keepdims=True)
    return inv_std * (scaled - first_mean - normed * second_mean)


def contract_rows(left_mat, right_mat):
    return lax.dot_general(
        left_mat, right_mat, (((0,), (0,)), ((), ())), preferred_element_type=jnp.float32
    )


def times_transposed(left_mat, right_mat):
    return lax.dot_general(
        left_mat, right_mat, (((1,), (1,)), ((), ())), preferred_element_type=jnp.float32
    )


class Place:
    def __init__(self, far_count):
        index = lax.axis_index("dp")
        self.far_count = far_count
        self.tensor = lax.axis_index("tensor")
        self.core = lax.rem(index, 2)
        self.near = lax.rem(index // 2, 2)
        self.far = index // 4

    def index(self, far, near, core):
        return (far * 2 + near) * 2 + core

    def far_at(self, step):
        return lax.rem(self.far + step + self.far_count, self.far_count)

    def peer(self, kind, step=0):
        far, near, core, tensor = self.far, self.near, self.core, self.tensor
        if kind == "far":
            far = self.far_at(step)
        if kind == "near":
            near = 1 - near
        if kind == "core":
            core = 1 - core
        if kind == "tensor":
            tensor = 1 - tensor
        return {"dp": self.index(far, near, core), "tensor": tensor}

    def greet(self):
        barrier = pltpu.get_barrier_semaphore()
        peers = [self.peer("far", step) for step in range(1, self.far_count)]
        peers += [self.peer("near"), self.peer("core"), self.peer("tensor")]
        for peer in peers:
            pl.semaphore_signal(barrier, inc=1, device_id=peer, device_id_type=MESH)
        pl.semaphore_wait(barrier, len(peers))


def columns_at(tensor, width, start=0, size=None):
    return pl.ds(pl.multiple_of(tensor * width + start, LANES), width if size is None else size)


def gather_kernel(far_count, array_count, pieces, *refs):
    group_count = len(pieces)
    own_arrays = refs[:array_count]
    tail_ref = refs[array_count]
    full_refs = refs[array_count + 1 : 2 * array_count + 1]
    halo_ref = refs[2 * array_count + 1]
    local_sem, tail_sem, far_sem, x_sem, y_sem, diag_sem, core_sem = refs[2 * array_count + 2 :]
    own_refs = []
    for array, lead, first, _, size in pieces:
        own = own_arrays[array]
        own_refs.append(own.at[:, pl.ds(first, size)] if lead is None else own.at[lead])
    at = Place(far_count)
    at.greet()
    sent, arrivals = [], []

    def slot(group, tensor, far, near, core):
        array, _, _, start, size = pieces[group]
        block_width = full_refs[array].shape[2] // 2
        columns = columns_at(tensor, block_width, start, size)
        return full_refs[array].at[at.index(far, near, core), :, columns]

    def send(source, target, sems, place, peer):
        copy = pltpu.make_async_remote_copy(
            src_ref=source,
            dst_ref=target,
            send_sem=sems.at[(0,) + place],
            recv_sem=sems.at[(1,) + place],
            device_id=peer,
            device_id_type=MESH,
        )
        copy.start()
        sent.append(copy)

    def arrived(target, sems, place, peer):
        pltpu.make_async_remote_copy(
            src_ref=target,
            dst_ref=target,
            send_sem=sems.at[(0,) + place],
            recv_sem=sems.at[(1,) + place],
            device_id=peer,
            device_id_type=MESH,
        ).wait_recv()

    groups = range(group_count)
    x_first, loads = [], [0, 0]
    for piece in pieces:
        x_first.append(loads[0] <= loads[1])
        loads[0 if x_first[-1] else 1] += piece[4]
    x_peer, y_peer, core_peer = at.peer("tensor"), at.peer("near"), at.peer("core")
    local = []
    for group in groups:
        own_slot = slot(group, at.tensor, at.far, at.near, at.core)
        for step in range(1, far_count):
            send(own_refs[group], own_slot, far_sem, (group, step), at.peer("far", step))
        send(own_refs[group], own_slot, x_sem, (group, 0), x_peer)
        send(own_refs[group], own_slot, y_sem, (group, 0), y_peer)
        send(own_refs[group], own_slot, core_sem, (group, 0, 0), core_peer)
        if group == 0:
            copy = pltpu.make_async_remote_copy(
                src_ref=tail_ref,
                dst_ref=halo_ref,
                send_sem=tail_sem.at[0],
                recv_sem=tail_sem.at[1],
                device_id=x_peer,
                device_id_type=MESH,
            )
            copy.start()
            tail_copy = copy
        keep = pltpu.make_async_copy(own_refs[group], own_slot, local_sem.at[group])
        keep.start()
        local.append(keep)

    def spread(group, step):
        far = at.far_at(-step)
        here = slot(group, at.tensor, far, at.near, at.core)
        arrived(here, far_sem, (group, step), x_peer)
        send(here, here, x_sem, (group, step), x_peer)
        send(here, here, y_sem, (group, step), y_peer)
        send(here, here, core_sem, (group, 0, step), core_peer)

    def relay(group, step):
        far = at.far_at(-step)
        from_x = slot(group, 1 - at.tensor, far, at.near, at.core)
        arrived(from_x, x_sem, (group, step), x_peer)
        if x_first[group]:
            send(from_x, from_x, diag_sem, (group, step), y_peer)
        send(from_x, from_x, core_sem, (group, 1, step), core_peer)
        from_y = slot(group, at.tensor, far, 1 - at.near, at.core)
        arrived(from_y, y_sem, (group, step), y_peer)
        if not x_first[group]:
            send(from_y, from_y, diag_sem, (group, step), x_peer)
        send(from_y, from_y, core_sem, (group, 2, step), core_peer)

    def corner(group, step):
        far = at.far_at(-step)
        diag = slot(group, 1 - at.tensor, far, 1 - at.near, at.core)
        arrived(diag, diag_sem, (group, step), y_peer if x_first[group] else x_peer)
        send(diag, diag, core_sem, (group, 3, step), core_peer)

    for group in groups:
        relay(group, 0)
        for step in range(1, far_count):
            spread(group, step)
            if group:
                corner(group - 1, step - 1)
        if group:
            corner(group - 1, far_count - 1)
        for step in range(1, far_count):
            relay(group, step)
    for step in range(far_count):
        corner(group_count - 1, step)
    for group in groups:
        for step in range(far_count):
            far = at.far_at(-step)
            for kind, (flip_x, flip_y) in enumerate(((0, 0), (1, 0), (0, 1), (1, 1))):
                tensor = 1 - at.tensor if flip_x else at.tensor
                near = 1 - at.near if flip_y else at.near
                arrived(
                    slot(group, tensor, far, near, 1 - at.core),
                    core_sem,
                    (group, kind, step),
                    core_peer,
                )
    for copy in sent:
        copy.wait_send()
    tail_copy.wait()
    for keep in local:
        keep.wait()


def gather_weights(own_blocks, tail):
    dp_size, tensor_size = lax.axis_size("dp"), lax.axis_size("tensor")
    far_count = dp_size // 4
    array_count = len(own_blocks)
    shapes, pieces = [], []
    for array, own in enumerate(own_blocks):
        size = own.shape[-1]
        lead_count = own.shape[0] if own.ndim == 3 else 1
        block_width = lead_count * size
        shapes.append(
            jax.ShapeDtypeStruct((dp_size, own.shape[-2], tensor_size * block_width), own.dtype)
        )
        if own.ndim == 3:
            pieces += [(array, lead, 0, lead * size, size) for lead in range(lead_count)]
        elif size < 8 * LANES:
            pieces.append((array, None, 0, 0, size))
        else:
            cut = size // 2
            pieces += [(array, None, first, first, cut) for first in (0, cut)]
    shapes.append(jax.ShapeDtypeStruct(tail.shape, tail.dtype))
    count = len(pieces)
    dma = pltpu.SemaphoreType.DMA
    return pl.pallas_call(
        functools.partial(gather_kernel, far_count, array_count, tuple(pieces)),
        out_shape=shapes,
        in_specs=[pl.BlockSpec(memory_space=pltpu.VMEM)] * (array_count + 1),
        out_specs=[pl.BlockSpec(memory_space=pl.ANY)] * (array_count + 1),
        scratch_shapes=[
            dma((count,)),
            dma((2,)),
            dma((2, count, far_count)),
            dma((2, count, far_count)),
            dma((2, count, far_count)),
            dma((2, count, far_count)),
            dma((2, count, 4, far_count)),
        ],
        compiler_params=pltpu.CompilerParams(
            collective_id=0, has_side_effects=True, vmem_limit_bytes=VMEM_BYTES
        ),
        name="gather_weights",
    )(*own_blocks, tail)


def scatter_kernel(far_count, group_count, *refs):
    part_refs = refs[:group_count]
    out_refs = refs[group_count : 2 * group_count]
    (
        result,
        total,
        core_in,
        x_in,
        y_in,
        diag_in,
        far_in,
        core_sem,
        x_sem,
        y_sem,
        diag_x_sem,
        diag_y_sem,
        far_sem,
    ) = refs[2 * group_count :]
    at = Place(far_count)
    at.greet()
    sent = []
    tensor_size = 2
    widths = [ref.shape[2] // tensor_size for ref in part_refs]
    offsets = [sum(widths[:group]) for group in range(group_count)]
    all_columns = sum(widths)
    half = all_columns // 2 // LANES * LANES
    low, high = pl.ds(0, half), pl.ds(half, all_columns - half)
    x_peer, y_peer, core_peer = at.peer("tensor"), at.peer("near"), at.peer("core")
    order = list(range(1, far_count)) + [0]
    own, by_x, by_y, diag = range(4)
    flips = ((0, 0), (1, 0), (0, 1), (1, 1))

    def make(source, target, sems, place, peer):
        return pltpu.make_async_remote_copy(
            src_ref=source,
            dst_ref=target,
            send_sem=sems.at[(0,) + place],
            recv_sem=sems.at[(1,) + place],
            device_id=peer,
            device_id_type=MESH,
        )

    def send(*args):
        copy = make(*args)
        copy.start()
        sent.append(copy)

    def slot(group, kind, step, core):
        flip_x, flip_y = flips[kind]
        tensor = 1 - at.tensor if flip_x else at.tensor
        near = 1 - at.near if flip_y else at.near
        index = at.index(at.far_at(step), near, core)
        return part_refs[group].at[index, :, columns_at(tensor, widths[group])]

    def core_slot(group, kind, step):
        return core_in.at[kind, step, :, pl.ds(offsets[group], widths[group])]

    kinds = (diag, by_x, by_y, own)
    for step in order:
        for kind in kinds:
            for group in range(group_count):
                send(
                    slot(group, kind, step, 1 - at.core),
                    core_slot(group, kind, step),
                    core_sem,
                    (group, kind, step),
                    core_peer,
                )

    def meet(kind, step):
        for group in range(group_count):
            target = core_slot(group, kind, step)
            make(target, target, core_sem, (group, kind, step), core_peer).wait_recv()
            columns = pl.ds(offsets[group], widths[group])
            mine = slot(group, kind, step, at.core)
            total[kind, step, :, columns] = (
                mine[...].astype(jnp.float32) + target[...].astype(jnp.float32)
            ).astype(jnp.bfloat16)

    def add_to(kind, step, columns, source):
        total[kind, step, :, columns] = (
            total[kind, step, :, columns].astype(jnp.float32) + source[...].astype(jnp.float32)
        ).astype(jnp.bfloat16)

    for step in order:
        meet(diag, step)
        corner = total.at[diag, step]
        send(corner.at[:, low], diag_in.at[step, :, low], diag_y_sem, (step,), y_peer)
        send(corner.at[:, high], diag_in.at[step, :, high], diag_x_sem, (step,), x_peer)
        meet(by_x, step)
        meet(by_y, step)
        meet(own, step)

    for step in order:
        from_y = diag_in.at[step, :, low]
        make(from_y, from_y, diag_y_sem, (step,), y_peer).wait_recv()
        add_to(by_x, step, low, from_y)
        send(total.at[by_x, step], x_in.at[step], x_sem, (step,), x_peer)
        from_x = diag_in.at[step, :, high]
        make(from_x, from_x, diag_x_sem, (step,), x_peer).wait_recv()
        add_to(by_y, step, high, from_x)
        send(total.at[by_y, step], y_in.at[step], y_sem, (step,), y_peer)

    for step in order:
        make(x_in.at[step], x_in.at[step], x_sem, (step,), x_peer).wait_recv()
        make(y_in.at[step], y_in.at[step], y_sem, (step,), y_peer).wait_recv()
        merged = (
            total[own, step].astype(jnp.float32)
            + x_in[step].astype(jnp.float32)
            + y_in[step].astype(jnp.float32)
        )
        if step:
            total[own, step] = merged.astype(jnp.bfloat16)
            send(total.at[own, step], far_in.at[step], far_sem, (step,), at.peer("far", step))
        else:
            result[...] = merged
    for step in range(1, far_count):
        make(far_in.at[step], far_in.at[step], far_sem, (step,), at.peer("far", step)).wait_recv()
        if step < far_count - 1:
            result[...] += far_in[step].astype(jnp.float32)
    for group in range(group_count):
        out_ref = out_refs[group]
        width = out_ref.shape[-1]
        for lead in range(widths[group] // width):
            columns = pl.ds(offsets[group] + lead * width, width)
            held = result[:, columns]
            if far_count > 1:
                held += far_in[far_count - 1, :, columns].astype(jnp.float32)
            if len(out_ref.shape) == 3:
                out_ref[lead] = held
            else:
                out_ref[...] = held
    for copy in sent:
        copy.wait_send()


def scatter_grads(parts, out_shapes):
    dp_size, tensor_size = lax.axis_size("dp"), lax.axis_size("tensor")
    far_count = dp_size // 4
    count = len(parts)
    rows = parts[0].shape[1]
    all_columns = sum(part.shape[2] for part in parts) // tensor_size
    dma = pltpu.SemaphoreType.DMA
    block = (rows, all_columns)
    return pl.pallas_call(
        functools.partial(scatter_kernel, far_count, count),
        out_shape=[jax.ShapeDtypeStruct(shape, jnp.float32) for shape in out_shapes],
        in_specs=[pl.BlockSpec(memory_space=pltpu.VMEM)] * count,
        out_specs=[pl.BlockSpec(memory_space=pltpu.VMEM)] * count,
        scratch_shapes=[
            pltpu.VMEM(block, jnp.float32),
            pltpu.VMEM((4, far_count) + block, jnp.bfloat16),
            pltpu.VMEM((4, far_count) + block, jnp.bfloat16),
            pltpu.VMEM((far_count,) + block, jnp.bfloat16),
            pltpu.VMEM((far_count,) + block, jnp.bfloat16),
            pltpu.VMEM((far_count,) + block, jnp.bfloat16),
            pltpu.VMEM((far_count,) + block, jnp.bfloat16),
            dma((2, count, 4, far_count)),
            dma((2, far_count)),
            dma((2, far_count)),
            dma((2, far_count)),
            dma((2, far_count)),
            dma((2, far_count)),
        ],
        compiler_params=pltpu.CompilerParams(
            collective_id=1, has_side_effects=True, vmem_limit_bytes=VMEM_BYTES
        ),
        name="scatter_grads",
    )(*parts)


def head_blocks(q_ref, k_ref, v_ref, id_row, id_col, halo):
    query_rows = id_col.shape[0]
    lane = lax.broadcasted_iota(jnp.int32, (halo, LANES), 1)
    window = 2 * halo
    row = lax.broadcasted_iota(jnp.int32, (halo, window), 0)
    column = lax.broadcasted_iota(jnp.int32, (halo, window), 1)
    causal = column <= row + halo
    for block in range(query_rows // halo):
        first = block * halo
        query = q_ref[first + halo : first + 2 * halo, :]
        keys = k_ref[first : first + window, :]
        values = v_ref[first : first + window, :]
        same = id_col[first : first + halo, :] == id_row[:, first : first + window]
        allowed = causal & same
        for head in range(LANES // HD):
            mine = (lane >= head * HD) & (lane < (head + 1) * HD)
            query_head = jnp.where(mine, query, jnp.zeros_like(query))
            scores = times_transposed(query_head, keys) * scale_factor
            weight = jnp.where(allowed, jnp.exp(scores), 0.0)
            probs = weight / jnp.sum(weight, axis=-1, keepdims=True)
            yield first, head, mine, query_head, keys, values, probs


def attend_kernel(halo, q_ref, k_ref, v_ref, id_row, id_col, mixed_ref):
    held = None
    for first, head, mine, _, _, values, probs in head_blocks(
        q_ref, k_ref, v_ref, id_row, id_col, halo
    ):
        part = jnp.dot(probs.astype(jnp.bfloat16), values, preferred_element_type=jnp.float32)
        held = part if head == 0 else jnp.where(mine, part, held)
        if head == LANES // HD - 1:
            mixed_ref[first : first + halo, :] = held.astype(jnp.bfloat16)


def attend_back_kernel(
    halo, q_ref, k_ref, v_ref, id_row, id_col, mixed_ref, grad_ref, dq_ref, dk_ref, dv_ref
):
    dk_ref[...] = jnp.zeros_like(dk_ref)
    dv_ref[...] = jnp.zeros_like(dv_ref)
    for first, head, mine, query_head, keys, values, probs in head_blocks(
        q_ref, k_ref, v_ref, id_row, id_col, halo
    ):
        window = keys.shape[0]
        grad = grad_ref[first : first + halo, :]
        grad_head = jnp.where(mine, grad, jnp.zeros_like(grad))
        mixed = mixed_ref[first : first + halo, :]
        delta = jnp.sum(
            grad_head.astype(jnp.float32) * mixed.astype(jnp.float32), axis=-1, keepdims=True
        )
        grad_probs = times_transposed(grad_head, values)
        grad_scores = (probs * (grad_probs - delta) * scale_factor).astype(jnp.bfloat16)
        dv_ref[first : first + window, :] += contract_rows(probs.astype(jnp.bfloat16), grad_head)
        dk_ref[first : first + window, :] += contract_rows(grad_scores, query_head)
        part = jnp.dot(grad_scores, keys, preferred_element_type=jnp.float32)
        if head == 0:
            dq_ref[first : first + halo, :] = part
        else:
            dq_ref[first : first + halo, :] = jnp.where(
                mine, part, dq_ref[first : first + halo, :]
            )


def attend_specs(qkv, halo, tensor_size, parts=None):
    ext_rows = qkv.shape[0]
    pairs = qkv.shape[1] // 3 // (parts or tensor_size) // LANES

    def part_of(which):
        return pl.BlockSpec(
            (ext_rows, LANES), lambda pair: (0, pair // pairs * 3 * pairs + which * pairs + pair % pairs)
        )

    ids = [
        pl.BlockSpec((1, ext_rows), lambda pair: (0, 0)),
        pl.BlockSpec((ext_rows - halo, 1), lambda pair: (0, 0)),
    ]
    return pairs * (parts or tensor_size), [part_of(0), part_of(1), part_of(2)] + ids


def attend(qkv, id_row, id_col, halo, tensor_size):
    steps, specs = attend_specs(qkv, halo, tensor_size)
    rows = qkv.shape[0] - halo
    return pl.pallas_call(
        functools.partial(attend_kernel, halo),
        grid=(steps,),
        in_specs=specs,
        out_specs=pl.BlockSpec((rows, LANES), lambda pair: (0, pair)),
        out_shape=jax.ShapeDtypeStruct((rows, steps * LANES), jnp.bfloat16),
        name="attend",
    )(qkv, qkv, qkv, id_row, id_col)


def attend_back(qkv, id_row, id_col, mixed, grad_mixed, halo, tensor_size, parts=None):
    steps, specs = attend_specs(qkv, halo, tensor_size, parts)
    ext_rows = qkv.shape[0]
    rows = ext_rows - halo
    short = pl.BlockSpec((rows, LANES), lambda pair: (0, pair))
    tall = pl.BlockSpec((ext_rows, LANES), lambda pair: (0, pair))
    width = steps * LANES
    return pl.pallas_call(
        functools.partial(attend_back_kernel, halo),
        grid=(steps,),
        in_specs=specs + [short, short],
        out_specs=[short, tall, tall],
        out_shape=[
            jax.ShapeDtypeStruct((rows, width), jnp.float32),
            jax.ShapeDtypeStruct((ext_rows, width), jnp.float32),
            jax.ShapeDtypeStruct((ext_rows, width), jnp.float32),
        ],
        name="attend_back",
    )(qkv, qkv, qkv, id_row, id_col, mixed, grad_mixed)


GELU_C = 0.7978845608028654
GELU_A = 0.044715
ROWS_AT = {"gain_one": 0, "shift_one": 1, "out_bias": 2, "gain_two": 3, "shift_two": 4, "down_bias": 5}
Q_BIAS, V_BIAS, UP_BIAS = 6, 7, 8
SMALL_ROWS = 16
TILE = 256


def loop(count, body):
    lax.fori_loop(0, count, lambda i, carry: (body(i), carry)[1], 0)


def lanes(start, size=TILE):
    return pl.ds(pl.multiple_of(start, LANES), size)


def forward_kernel(far_count, halo, *refs):
    (
        own_qkv,
        own_out,
        own_up,
        own_down,
        own_small,
        x_hbm,
        cot_hbm,
        ids_ref,
        qkv_w_out,
        out_w_out,
        up_w_out,
        ln1_out,
        qkv_out,
        mixed_out,
        middle_out,
        ln2_out,
        hidden_out,
        grad_pre_out,
        layer_out,
        params,
        up_grad,
        w_qkv,
        w_out,
        w_up,
        w_down,
        small_all,
        x_ref,
        cot_ref,
        cot_bf,
        ln1,
        qkv,
        mixed,
        middle,
        total,
        ln2,
        hidden,
        slope,
        grad_pre,
        id_ref,
        mask_ref,
        load_sem,
        out_sem,
        local_sem,
        tail_sem,
        far_sem,
        x_sem,
        y_sem,
        diag_sem,
        core_sem,
    ) = refs
    f32, bf16 = jnp.float32, jnp.bfloat16
    rows, width = x_ref.shape
    own_rows = own_out.shape[0]
    attn = own_out.shape[1]
    hid = own_up.shape[1]
    cut = hid // 2
    at = Place(far_count)
    at.greet()
    sent, keeps = [], {}
    x_load = pltpu.make_async_copy(x_hbm, x_ref, load_sem.at[0])
    cot_load = pltpu.make_async_copy(cot_hbm, cot_ref, load_sem.at[1])
    x_load.start()
    cot_load.start()

    def block_of(full, width_of, start, size):
        def place(index, tensor):
            row = pl.multiple_of(index * own_rows, 16)
            return full.at[pl.ds(row, own_rows), lanes(tensor * width_of + start, size)]

        return place

    groups = [(own_small, lambda index, tensor: small_all.at[index * 2 + tensor], 0)]
    for lead in range(3):
        def place(index, tensor, lead=lead):
            row = pl.multiple_of(index * own_rows, 16)
            return w_qkv.at[pl.ds(row, own_rows), lanes(lead * width + tensor * attn, attn)]

        groups.append((own_qkv.at[lead], place, attn))
    groups.append((own_out, block_of(w_out, attn, 0, attn), attn))
    for half in range(2):
        columns = pl.ds(half * cut, cut)
        groups.append((own_up.at[:, columns], block_of(w_up, hid, half * cut, cut), cut))
        groups.append((own_down.at[:, columns], block_of(w_down, hid, half * cut, cut), cut))
    count = len(groups)
    x_first, loads = [], [attn, 0]
    for _, _, size in groups:
        x_first.append(loads[0] >= loads[1])
        loads[1 if x_first[-1] else 0] += size

    def slot(group, tensor, far, near, core):
        return groups[group][1](at.index(far, near, core), tensor)

    def remote(source, target, sems, place, peer):
        return pltpu.make_async_remote_copy(
            src_ref=source,
            dst_ref=target,
            send_sem=sems.at[(0,) + place],
            recv_sem=sems.at[(1,) + place],
            device_id=peer,
            device_id_type=MESH,
        )

    def send(*args):
        copy = remote(*args)
        copy.start()
        sent.append(copy)

    def arrived(target, sems, place, peer):
        remote(target, target, sems, place, peer).wait_recv()

    x_peer, y_peer, core_peer = at.peer("tensor"), at.peer("near"), at.peer("core")

    def own(group):
        source = groups[group][0]
        target = slot(group, at.tensor, at.far, at.near, at.core)
        for step in range(1, far_count):
            send(source, target, far_sem, (group, step), at.peer("far", step))
        send(source, target, x_sem, (group, 0), x_peer)
        send(source, target, y_sem, (group, 0), y_peer)
        send(source, target, core_sem, (group, 0, 0), core_peer)
        keep = pltpu.make_async_copy(source, target, local_sem.at[group])
        keep.start()
        keeps[group] = keep

    def spread(group, step):
        here = slot(group, at.tensor, at.far_at(-step), at.near, at.core)
        arrived(here, far_sem, (group, step), x_peer)
        send(here, here, x_sem, (group, step), x_peer)
        send(here, here, y_sem, (group, step), y_peer)
        send(here, here, core_sem, (group, 0, step), core_peer)

    def relay(group, step):
        far = at.far_at(-step)
        from_x = slot(group, 1 - at.tensor, far, at.near, at.core)
        arrived(from_x, x_sem, (group, step), x_peer)
        if x_first[group]:
            send(from_x, from_x, diag_sem, (group, step), y_peer)
        send(from_x, from_x, core_sem, (group, 1, step), core_peer)
        from_y = slot(group, at.tensor, far, 1 - at.near, at.core)
        arrived(from_y, y_sem, (group, step), y_peer)
        if not x_first[group]:
            send(from_y, from_y, diag_sem, (group, step), x_peer)
        send(from_y, from_y, core_sem, (group, 2, step), core_peer)

    def corner(group, step):
        diag = slot(group, 1 - at.tensor, at.far_at(-step), 1 - at.near, at.core)
        arrived(diag, diag_sem, (group, step), y_peer if x_first[group] else x_peer)
        send(diag, diag, core_sem, (group, 3, step), core_peer)

    def finish(group):
        for step in range(far_count):
            far = at.far_at(-step)
            for kind, (flip_x, flip_y) in enumerate(((0, 0), (1, 0), (0, 1), (1, 1))):
                tensor = 1 - at.tensor if flip_x else at.tensor
                near = 1 - at.near if flip_y else at.near
                place = slot(group, tensor, far, near, 1 - at.core)
                arrived(place, core_sem, (group, kind, step), core_peer)
        keeps[group].wait()

    stores = []

    def store(source, target):
        copy = pltpu.make_async_copy(source, target, out_sem.at[len(stores)])
        copy.start()
        stores.append(copy)

    def vector(row, columns=slice(None)):
        return params[row : row + 1, columns]

    def norm_rows(source, target, first, size, shift, gain_row, shift_row):
        data = source[pl.ds(first, size), :]
        row_mean = jnp.mean(data, axis=-1, keepdims=True)
        centred = data - row_mean
        inv_std = lax.rsqrt(jnp.mean(centred * centred, axis=-1, keepdims=True) + eps)
        scaled = centred * inv_std * vector(gain_row) + vector(shift_row)
        target[pl.ds(first + shift, size), :] = scaled.astype(bf16)

    def first_norm():
        held = small_all[0].astype(f32)
        for device in range(1, small_all.shape[0]):
            held = held + small_all[device].astype(f32)
        params[...] = held
        x_load.wait()
        norm_rows(x_ref, ln1, rows - halo, halo, halo, 0, 1)
        send(ln1.at[pl.ds(rows, halo)], ln1.at[pl.ds(0, halo)], tail_sem, (), x_peer)

        def one(i):
            norm_rows(x_ref, ln1, pl.multiple_of(i * halo, halo), halo, halo, 0, 1)

        loop(rows // halo - 1, one)

    def masks():
        id_ref[:, :halo] = jnp.full((1, halo), -1, jnp.int32)
        id_ref[:, halo:] = ids_ref[...]
        window = 2 * halo
        row = lax.broadcasted_iota(jnp.int32, (halo, window), 0)
        column = lax.broadcasted_iota(jnp.int32, (halo, window), 1)
        causal = column <= row + halo
        for block in range(rows // halo):
            first = at.tensor * rows + block * halo
            keys = id_ref[:, lanes(first, window)]
            queries = jnp.broadcast_to(id_ref[:, lanes(first + halo, halo)], (halo, halo)).T
            same = jnp.concatenate([queries, queries], axis=1) == keys
            mask_ref[block] = jnp.where(same & causal, 1.0, 0.0)
        cot_load.wait()

        def one(i):
            part = pl.ds(pl.multiple_of(i * halo, halo), halo)
            cot_bf[part, :] = cot_ref[part, :].astype(bf16)

        loop(rows // halo, one)

    def project(lead, bias_row, first):
        def one(i):
            columns = lanes(lead * width + i * TILE)
            part = jnp.dot(ln1[first:, :], w_qkv[:, columns], preferred_element_type=f32)
            if bias_row is not None:
                part = part + params[bias_row : bias_row + 1, lanes(i * TILE)]
            qkv[first:, columns] = part.astype(bf16)

        loop(width // TILE, one)

    def attention(first_pair, pair_count):
        lane = lax.broadcasted_iota(jnp.int32, (halo, LANES), 1)

        def one(i):
            pair = first_pair + i
            q_at, k_at = lanes(pair * LANES, LANES), lanes(width + pair * LANES, LANES)
            v_at = lanes(2 * width + pair * LANES, LANES)
            for block in range(rows // halo):
                first = block * halo
                query = qkv[first + halo : first + 2 * halo, q_at]
                keys = qkv[first : first + 2 * halo, k_at]
                values = qkv[first : first + 2 * halo, v_at]
                allowed = mask_ref[block] > 0.5
                held = None
                for head in range(LANES // HD):
                    mine = (lane >= head * HD) & (lane < (head + 1) * HD)
                    query_head = jnp.where(mine, query, jnp.zeros_like(query))
                    scores = times_transposed(query_head, keys) * scale_factor
                    weight = jnp.where(allowed, jnp.exp(scores), 0.0)
                    probs = weight / jnp.sum(weight, axis=-1, keepdims=True)
                    part = jnp.dot(probs.astype(bf16), values, preferred_element_type=f32)
                    held = part if head == 0 else jnp.where(mine, part, held)
                mixed[first : first + halo, q_at] = held.astype(bf16)

        loop(pair_count, one)

    def project_out():
        def one(i):
            columns = lanes(i * TILE)
            out_rows = pl.ds(pl.multiple_of(i * TILE, TILE), TILE)
            part = x_ref[:, columns] + times_transposed(mixed[...], w_out[out_rows, :])
            part = part + params[2:3, columns]
            middle[:, columns] = part
            total[:, columns] = part + params[5:6, columns]

        loop(width // TILE, one)

    def second_norm():
        def one(i):
            norm_rows(middle, ln2, pl.multiple_of(i * halo, halo), halo, 0, 3, 4)

        loop(rows // halo, one)

    def go_up(half, tensor):
        base = tensor * hid + half * cut

        def one(i):
            columns = lanes(base + i * TILE)
            bias_row = UP_BIAS + base // width
            bias = params[bias_row : bias_row + 1, lanes(base % width + i * TILE)]
            u = jnp.dot(ln2[...], w_up[:, columns], preferred_element_type=f32) + bias
            square = u * u
            bent = jnp.tanh(GELU_C * (u + GELU_A * (u * square)))
            half_sum = 0.5 + 0.5 * bent
            hidden[:, columns] = (u * half_sum).astype(bf16)
            turn = (0.5 * GELU_C) * (1.0 + (3.0 * GELU_A) * square)
            slope[:, columns] = half_sum + u * (1.0 - bent * bent) * turn

        loop(cut // TILE, one)

    def go_down(half, tensor):
        base = tensor * hid + half * cut

        def one(i):
            columns = lanes(i * TILE)
            out_rows = pl.ds(pl.multiple_of(i * TILE, TILE), TILE)
            total[:, columns] += times_transposed(
                hidden[:, base : base + cut], w_down[out_rows, base : base + cut]
            )

        loop(width // TILE, one)

    def go_back(half, tensor):
        base = tensor * hid + half * cut

        def one(i):
            columns = lanes(base + i * TILE)
            part = jnp.dot(cot_bf[...], w_down[:, columns], preferred_element_type=f32)
            part = part * slope[:, columns]
            grad_pre[:, columns] = part.astype(bf16)
            up_grad[:, columns] = jnp.sum(part, axis=0, keepdims=True)

        loop(cut // TILE, one)

    def halo_here():
        tail = ln1.at[pl.ds(0, halo)]
        remote(tail, tail, tail_sem, (), x_peer).wait_recv()
        store(ln1.at[pl.ds(halo, rows)], ln1_out)

    pairs = width // LANES
    step_pairs = pairs // 3 if pairs % 3 == 0 else pairs
    work = {
        0: [first_norm, masks],
        1: [lambda: project(0, Q_BIAS, halo)],
        2: [lambda: (halo_here(), project(1, None, 0))],
        3: [lambda: (project(2, V_BIAS, 0), store(w_qkv, qkv_w_out), store(qkv, qkv_out))]
        + [
            functools.partial(attention, first, step_pairs)
            for first in range(0, pairs, step_pairs)
        ],
        4: [
            lambda: (project_out(), store(w_out, out_w_out), store(mixed, mixed_out)),
            lambda: (second_norm(), store(middle, middle_out), store(ln2, ln2_out)),
        ],
    }
    for half in range(2):
        work[5 + 2 * half] = [functools.partial(go_up, half, tensor) for tensor in range(2)]
        work[6 + 2 * half] = [functools.partial(go_down, half, tensor) for tensor in range(2)]
        work[6 + 2 * half] += [functools.partial(go_back, half, tensor) for tensor in range(2)]
    work[7].append(lambda: (store(w_up, up_w_out), store(hidden, hidden_out)))
    queue = []

    def tick():
        if queue:
            queue.pop(0)()

    ahead = 4
    for group in range(min(ahead, count)):
        own(group)
    for group in range(count):
        if group + ahead < count:
            own(group + ahead)
        relay(group, 0)
        tick()
        for step in range(1, far_count):
            spread(group, step)
            if group:
                corner(group - 1, step - 1)
            if step % 2 == 0:
                tick()
        if group:
            corner(group - 1, far_count - 1)
        for step in range(1, far_count):
            relay(group, step)
            if step % 2 == 0:
                tick()
        if group:
            finish(group - 1)
            queue += work[group - 1]
            tick()
    for step in range(far_count):
        corner(count - 1, step)
    while queue:
        tick()
    finish(count - 1)
    queue += work[count - 1]
    while queue:
        tick()
    store(total, layer_out)
    store(grad_pre, grad_pre_out)
    for copy in sent:
        copy.wait_send()
    for copy in stores:
        copy.wait()


def forward_pass(own_qkv, own_out, own_up, own_down, own_small, inputs, cot, ids, halo):
    f32, bf16 = jnp.float32, jnp.bfloat16
    dp_size = lax.axis_size("dp")
    far_count = dp_size // 4
    rows, width = inputs.shape
    hid = 2 * own_up.shape[1]
    ext = rows + halo
    count = 9
    dma = pltpu.SemaphoreType.DMA
    shape, vmem = jax.ShapeDtypeStruct, pltpu.VMEM
    any_spec, vmem_spec = pl.BlockSpec(memory_space=pl.ANY), pl.BlockSpec(memory_space=pltpu.VMEM)
    return pl.pallas_call(
        functools.partial(forward_kernel, far_count, halo),
        out_shape=[
            shape((width, 3 * width), bf16),
            shape((width, width), bf16),
            shape((width, hid), bf16),
            shape((rows, width), bf16),
            shape((ext, 3 * width), bf16),
            shape((rows, width), bf16),
            shape((rows, width), f32),
            shape((rows, width), bf16),
            shape((rows, hid), bf16),
            shape((rows, hid), bf16),
            shape((rows, width), f32),
            shape((SMALL_ROWS, width), f32),
            shape((1, hid), f32),
        ],
        in_specs=[any_spec] * 7 + [vmem_spec],
        out_specs=[any_spec] * 11 + [vmem_spec] * 2,
        scratch_shapes=[
            vmem((width, 3 * width), bf16),
            vmem((width, width), bf16),
            vmem((width, hid), bf16),
            vmem((width, hid), bf16),
            vmem((2 * dp_size, SMALL_ROWS, width), bf16),
            vmem((rows, width), f32),
            vmem((rows, width), f32),
            vmem((rows, width), bf16),
            vmem((ext, width), bf16),
            vmem((ext, 3 * width), bf16),
            vmem((rows, width), bf16),
            vmem((rows, width), f32),
            vmem((rows, width), f32),
            vmem((rows, width), bf16),
            vmem((rows, hid), bf16),
            vmem((rows, hid), f32),
            vmem((rows, hid), bf16),
            vmem((1, halo + 2 * rows), jnp.int32),
            vmem((rows // halo, halo, 2 * halo), f32),
            dma((2,)),
            dma((11,)),
            dma((count,)),
            dma((2,)),
            dma((2, count, far_count)),
            dma((2, count, far_count)),
            dma((2, count, far_count)),
            dma((2, count, far_count)),
            dma((2, count, 4, far_count)),
        ],
        compiler_params=pltpu.CompilerParams(
            collective_id=2, has_side_effects=True, vmem_limit_bytes=VMEM_BYTES
        ),
        name="forward_pass",
    )(own_qkv, own_out, own_up, own_down, own_small, inputs, cot, ids)


def placed_small(vectors, qv_bias, up_bias, width):
    dp_size, tensor_size = lax.axis_size("dp"), lax.axis_size("tensor")
    dp, tensor = lax.axis_index("dp"), lax.axis_index("tensor")
    mine = lax.broadcasted_iota(jnp.int32, (dp_size * tensor_size, 1), 0) == dp * tensor_size + tensor
    stacked = jnp.stack(vectors)
    zero = jnp.zeros((), stacked.dtype)
    placed = jnp.where(mine[None], stacked[:, None, :], zero).reshape(len(vectors), width)
    my_dp = lax.broadcasted_iota(jnp.int32, (1, 1, 1, dp_size, 1), 3) == dp
    my_tensor = lax.broadcasted_iota(jnp.int32, (1, tensor_size, 1, 1, 1), 1) == tensor
    spot = my_dp & my_tensor
    qv = jnp.where(spot, qv_bias[:, None, :, None, :], zero).reshape(2, width)
    up = jnp.where(spot, up_bias[None, None, :, None, :], zero).reshape(-1, width)
    parts = jnp.concatenate([placed, qv, up])
    return jnp.pad(parts, ((0, SMALL_ROWS - parts.shape[0]), (0, 0)))


def on_device_small(
    inputs,
    seq_ids,
    norm1_gain,
    norm1_shift,
    qkv_weight,
    qv_bias,
    out_weight,
    out_bias,
    norm2_gain,
    norm2_shift,
    up_weight,
    up_bias,
    down_weight,
    down_bias,
    out_cotangent,
):
    f32, bf16 = jnp.float32, jnp.bfloat16
    dp_size, tensor_size = lax.axis_size("dp"), lax.axis_size("tensor")
    tensor = lax.axis_index("tensor")
    local_rows, width = inputs.shape
    halo = min(SEQ_MAX, local_rows)
    rows = up_weight.shape[0]
    attn = qkv_weight.shape[2]
    hid = up_weight.shape[1]
    vec = norm1_gain.shape[0]
    heads = qv_bias.shape[1]
    bias_cols = qv_bias.shape[2]
    up_rows, up_cols = up_bias.shape

    vectors = [norm1_gain, norm1_shift, out_bias, norm2_gain, norm2_shift, down_bias]
    vectors += [qv_bias.reshape(-1), up_bias.reshape(-1)]
    small_rows = len(vectors)
    small = jnp.stack([jnp.pad(vector, (0, LANES - vector.shape[0])) for vector in vectors])
    small = jnp.pad(small, ((0, rows - small_rows), (0, 0)))
    full_qkv, full_out, full_up, full_down, small_all, halo_rows = gather_weights(
        [qkv_weight, out_weight.T, up_weight, down_weight.T, small], inputs[local_rows - halo :]
    )
    full_qkv = full_qkv.reshape(width, -1)
    full_up = full_up.reshape(width, -1)
    full_down = full_down.reshape(width, -1)
    full_out = full_out.reshape(width, -1)
    small_all = small_all[:, :small_rows].reshape(dp_size, small_rows, tensor_size, LANES)
    gain_one, shift_one, bias_out, gain_two, shift_two, bias_down = (
        small_all[:, i, :, :vec].reshape(-1) for i in range(6)
    )
    qv_full = (
        small_all[:, 6, :, : qv_bias.size]
        .reshape(dp_size, tensor_size, 2, heads, bias_cols)
        .transpose(2, 1, 3, 0, 4)
        .reshape(2, tensor_size, attn)
    )
    up_bias_full = (
        small_all[:, 7, :, : up_bias.size]
        .reshape(dp_size, tensor_size, up_rows, up_cols)
        .transpose(1, 2, 0, 3)
        .reshape(-1)
    )
    qkv_bias = jnp.stack([qv_full[0], jnp.zeros_like(qv_full[0]), qv_full[1]], axis=1)
    qkv_bias = qkv_bias.reshape(-1).astype(f32)

    first_row = tensor * local_rows
    padded_ids = jnp.concatenate([jnp.full((halo,), -1, jnp.int32), seq_ids[0]])
    ext_ids = lax.dynamic_slice_in_dim(padded_ids, first_row, local_rows + halo)
    id_row, id_col = ext_ids[None, :], ext_ids[halo:, None]

    normed_one, inv_one, ln_one = norm_forward(inputs, gain_one, shift_one)
    ln_halo = norm_forward(halo_rows, gain_one, shift_one)[2]
    ln_ext = jnp.concatenate([ln_halo, ln_one])
    qkv = (jnp.dot(ln_ext, full_qkv, preferred_element_type=f32) + qkv_bias).astype(bf16)
    mixed = attend(qkv, id_row, id_col, halo, tensor_size)
    middle = inputs + times_transposed(mixed, full_out) + bias_out.astype(f32)
    normed_two, inv_two, ln_two = norm_forward(middle, gain_two, shift_two)
    pre_act = jnp.dot(ln_two, full_up, preferred_element_type=f32) + up_bias_full.astype(f32)
    hidden = gelu_forward(pre_act).astype(bf16)
    layer_out = middle + times_transposed(hidden, full_down) + bias_down.astype(f32)

    cot_bf = out_cotangent.astype(bf16)
    down_grad = contract_rows(cot_bf, hidden).astype(bf16)
    grad_pre = gelu_backward(pre_act, jnp.dot(cot_bf, full_down, preferred_element_type=f32))
    grad_pre_bf = grad_pre.astype(bf16)
    up_grad = contract_rows(ln_two, grad_pre_bf).astype(bf16)
    up_bias_grad = jnp.sum(grad_pre, axis=0)
    grad_ln_two = times_transposed(grad_pre_bf, full_up)
    gain_two_grad = jnp.sum(grad_ln_two * normed_two, axis=0)
    shift_two_grad = jnp.sum(grad_ln_two, axis=0)
    grad_middle = out_cotangent + norm_backward(grad_ln_two, normed_two, inv_two, gain_two)
    bias_down_grad = jnp.sum(out_cotangent, axis=0)
    bias_out_grad = jnp.sum(grad_middle, axis=0)
    mid_bf = grad_middle.astype(bf16)
    out_grad = contract_rows(mid_bf, mixed).astype(bf16)
    grad_mixed = jnp.dot(mid_bf, full_out, preferred_element_type=f32).astype(bf16)
    query_grad, key_ext, value_ext = attend_back(
        qkv, id_row, id_col, mixed, grad_mixed, halo, tensor_size
    )
    lent = jnp.concatenate([key_ext[:halo], value_ext[:halo]], axis=1).astype(bf16)
    ring = [((i + 1) % tensor_size, i) for i in range(tensor_size)]
    back = lax.ppermute(lent, "tensor", ring).astype(f32)
    rest = local_rows - halo

    def returned(ext, part):
        own = ext[halo:]
        return jnp.concatenate([own[:rest], own[rest:] + part])

    key_grad = returned(key_ext, back[:, :width])
    value_grad = returned(value_ext, back[:, width:])
    pieces = []
    for t in range(tensor_size):
        for piece in (query_grad, key_grad, value_grad):
            pieces.append(piece[:, t * attn : (t + 1) * attn].astype(bf16))
    grad_qkv = jnp.concatenate(pieces, axis=1)
    qkv_grad = contract_rows(ln_one, grad_qkv).astype(bf16)
    qv_grad = jnp.stack([jnp.sum(query_grad, axis=0), jnp.sum(value_grad, axis=0)])
    grad_ln_one = times_transposed(grad_qkv, full_qkv)
    gain_one_grad = jnp.sum(grad_ln_one * normed_one, axis=0)
    shift_one_grad = jnp.sum(grad_ln_one, axis=0)
    input_grad = grad_middle + norm_backward(grad_ln_one, normed_one, inv_one, gain_one)

    vectors = [gain_one_grad, shift_one_grad, bias_out_grad]
    vectors += [gain_two_grad, shift_two_grad, bias_down_grad]
    vectors = [vector.reshape(dp_size, tensor_size, vec) for vector in vectors] + [
        qv_grad.reshape(2, tensor_size, heads, dp_size, bias_cols)
        .transpose(3, 1, 0, 2, 4)
        .reshape(dp_size, tensor_size, -1),
        up_bias_grad.reshape(tensor_size, up_rows, dp_size, up_cols)
        .transpose(2, 0, 1, 3)
        .reshape(dp_size, tensor_size, -1),
    ]
    small_grad = jnp.stack(
        [jnp.pad(one.astype(bf16), ((0, 0), (0, 0), (0, LANES - one.shape[2]))) for one in vectors],
        axis=1,
    ).reshape(dp_size, small_rows, tensor_size * LANES)
    small_grad = jnp.pad(small_grad, ((0, 0), (0, rows - small_rows), (0, 0)))

    parts = [qkv_grad, out_grad, up_grad, down_grad, small_grad]
    own_qkv, own_out, own_up, own_down, own_small = scatter_grads(
        [part.reshape(dp_size, rows, -1) for part in parts],
        [(3, rows, attn), (rows, attn), (rows, hid), (rows, hid), (rows, LANES)],
    )
    vectors = [own_small[i, :vec] for i in range(6)]
    gain_one_own, shift_one_own, bias_out_own, gain_two_own, shift_two_own, bias_down_own = vectors
    return (
        layer_out,
        input_grad,
        gain_one_own,
        shift_one_own,
        own_qkv,
        own_small[6, : qv_bias.size].reshape(qv_bias.shape),
        own_out.T,
        bias_out_own,
        gain_two_own,
        shift_two_own,
        own_up,
        own_small[7, : up_bias.size].reshape(up_bias.shape),
        own_down.T,
        bias_down_own,
    )


def on_device(
    inputs,
    seq_ids,
    norm1_gain,
    norm1_shift,
    qkv_weight,
    qv_bias,
    out_weight,
    out_bias,
    norm2_gain,
    norm2_shift,
    up_weight,
    up_bias,
    down_weight,
    down_bias,
    out_cotangent,
):
    rows = up_weight.shape[0]
    if rows % 16:
        return on_device_small(
            inputs,
            seq_ids,
            norm1_gain,
            norm1_shift,
            qkv_weight,
            qv_bias,
            out_weight,
            out_bias,
            norm2_gain,
            norm2_shift,
            up_weight,
            up_bias,
            down_weight,
            down_bias,
            out_cotangent,
        )
    f32, bf16 = jnp.float32, jnp.bfloat16
    dp_size, tensor_size = lax.axis_size("dp"), lax.axis_size("tensor")
    tensor = lax.axis_index("tensor")
    local_rows, width = inputs.shape
    halo = min(SEQ_MAX, local_rows)
    attn = qkv_weight.shape[2]
    hid = up_weight.shape[1]
    vec = norm1_gain.shape[0]
    heads = qv_bias.shape[1]
    bias_cols = qv_bias.shape[2]
    up_rows, up_cols = up_bias.shape

    small = placed_small(
        [norm1_gain, norm1_shift, out_bias, norm2_gain, norm2_shift, down_bias],
        qv_bias,
        up_bias,
        width,
    )
    (
        full_qkv,
        full_out,
        full_up,
        ln_one,
        qkv,
        mixed,
        middle,
        ln_two,
        hidden,
        grad_pre_bf,
        layer_out,
        params,
        up_bias_grad,
    ) = forward_pass(
        qkv_weight,
        out_weight.T,
        up_weight,
        down_weight.T,
        small,
        inputs,
        out_cotangent,
        seq_ids,
        halo,
    )
    gain_one, gain_two = params[0], params[3]
    first_row = tensor * local_rows
    padded_ids = jnp.concatenate([jnp.full((halo,), -1, jnp.int32), seq_ids[0]])
    ext_ids = lax.dynamic_slice_in_dim(padded_ids, first_row, local_rows + halo)
    id_row, id_col = ext_ids[None, :], ext_ids[halo:, None]
    normed_one, inv_one, _ = norm_forward(inputs, gain_one, gain_one)
    normed_two, inv_two, _ = norm_forward(middle, gain_two, gain_two)

    cot_bf = out_cotangent.astype(bf16)
    down_grad = contract_rows(cot_bf, hidden).astype(bf16)
    up_grad = contract_rows(ln_two, grad_pre_bf).astype(bf16)
    grad_ln_two = times_transposed(grad_pre_bf, full_up)
    gain_two_grad = jnp.sum(grad_ln_two * normed_two, axis=0)
    shift_two_grad = jnp.sum(grad_ln_two, axis=0)
    grad_middle = out_cotangent + norm_backward(grad_ln_two, normed_two, inv_two, gain_two)
    bias_down_grad = jnp.sum(out_cotangent, axis=0)
    bias_out_grad = jnp.sum(grad_middle, axis=0)
    mid_bf = grad_middle.astype(bf16)
    out_grad = contract_rows(mid_bf, mixed).astype(bf16)
    grad_mixed = jnp.dot(mid_bf, full_out, preferred_element_type=f32).astype(bf16)
    query_grad, key_ext, value_ext = attend_back(
        qkv, id_row, id_col, mixed, grad_mixed, halo, tensor_size, 1
    )
    lent = jnp.concatenate([key_ext[:halo], value_ext[:halo]], axis=1).astype(bf16)
    ring = [((i + 1) % tensor_size, i) for i in range(tensor_size)]
    back = lax.ppermute(lent, "tensor", ring).astype(f32)
    rest = local_rows - halo

    def returned(ext, part):
        own = ext[halo:]
        return jnp.concatenate([own[:rest], own[rest:] + part])

    key_grad = returned(key_ext, back[:, :width])
    value_grad = returned(value_ext, back[:, width:])
    grad_qkv = jnp.concatenate(
        [query_grad.astype(bf16), key_grad.astype(bf16), value_grad.astype(bf16)], axis=1
    )
    qkv_grad = [
        contract_rows(ln_one, grad_qkv[:, lead * width : (lead + 1) * width]).astype(bf16)
        for lead in range(3)
    ]
    qv_grad = jnp.stack([jnp.sum(query_grad, axis=0), jnp.sum(value_grad, axis=0)])
    grad_ln_one = times_transposed(grad_qkv, full_qkv)
    gain_one_grad = jnp.sum(grad_ln_one * normed_one, axis=0)
    shift_one_grad = jnp.sum(grad_ln_one, axis=0)
    input_grad = grad_middle + norm_backward(grad_ln_one, normed_one, inv_one, gain_one)

    vectors = [gain_one_grad, shift_one_grad, bias_out_grad]
    vectors += [gain_two_grad, shift_two_grad, bias_down_grad]
    vectors = [vector.reshape(dp_size, tensor_size, vec) for vector in vectors] + [
        qv_grad.reshape(2, tensor_size, heads, dp_size, bias_cols)
        .transpose(3, 1, 0, 2, 4)
        .reshape(dp_size, tensor_size, -1),
        up_bias_grad.reshape(tensor_size, up_rows, dp_size, up_cols)
        .transpose(2, 0, 1, 3)
        .reshape(dp_size, tensor_size, -1),
    ]
    small_rows = len(vectors)
    small_grad = jnp.stack(
        [jnp.pad(one.astype(bf16), ((0, 0), (0, 0), (0, LANES - one.shape[2]))) for one in vectors],
        axis=1,
    ).reshape(dp_size, small_rows, tensor_size * LANES)
    small_grad = jnp.pad(small_grad, ((0, 0), (0, rows - small_rows), (0, 0)))

    parts = qkv_grad + [out_grad, up_grad, down_grad, small_grad]
    *own_qkv, own_out, own_up, own_down, own_small = scatter_grads(
        [part.reshape(dp_size, rows, -1) for part in parts],
        [(rows, attn)] * 4 + [(rows, hid), (rows, hid), (rows, LANES)],
    )
    vectors = [own_small[i, :vec] for i in range(6)]
    gain_one_own, shift_one_own, bias_out_own, gain_two_own, shift_two_own, bias_down_own = vectors
    return (
        layer_out,
        input_grad,
        gain_one_own,
        shift_one_own,
        jnp.stack(own_qkv),
        own_small[6, : qv_bias.size].reshape(qv_bias.shape),
        own_out.T,
        bias_out_own,
        gain_two_own,
        shift_two_own,
        own_up,
        own_small[7, : up_bias.size].reshape(up_bias.shape),
        own_down.T,
        bias_down_own,
    )


def solution(mesh):
    placed = (
        P(("dp", "tensor"), None),
        P("dp", None),
        P(("dp", "tensor")),
        P(("dp", "tensor")),
        P(None, "dp", "tensor"),
        P(None, "tensor", "dp"),
        P("tensor", "dp"),
        P(("dp", "tensor")),
        P(("dp", "tensor")),
        P(("dp", "tensor")),
        P("dp", "tensor"),
        P("tensor", "dp"),
        P("tensor", "dp"),
        P(("dp", "tensor")),
        P(("dp", "tensor"), None),
    )
    return jax.shard_map(
        on_device,
        mesh=mesh,
        in_specs=placed,
        out_specs=(
            P(("dp", "tensor"), None),
            P(("dp", "tensor"), None),
            P(("dp", "tensor")),
            P(("dp", "tensor")),
            P(None, "dp", "tensor"),
            P(None, "tensor", "dp"),
            P("tensor", "dp"),
            P(("dp", "tensor")),
            P(("dp", "tensor")),
            P(("dp", "tensor")),
            P("dp", "tensor"),
            P("tensor", "dp"),
            P("tensor", "dp"),
            P(("dp", "tensor")),
        ),
        check_vma=False,
    )
```

```python
import functools

import jax
import jax.numpy as jnp
from jax import lax
from jax.experimental import pallas as pl
from jax.experimental.pallas import tpu as pltpu
from jax.sharding import PartitionSpec as P

HD = 64
SEQ_MAX = 128
LANES = 128
VMEM_BYTES = 60 * 1024 * 1024

eps = 1e-05
scale_factor = 0.125
MESH = pl.DeviceIdType.MESH


def gelu_forward(pre_act):
    return jax.nn.gelu(pre_act, approximate=True)


def gelu_backward(pre_act, cotangent):
    return jax.vjp(gelu_forward, pre_act)[1](cotangent)[0]


def norm_forward(row_data, gain_vec, shift_vec):
    row_mean = jnp.mean(row_data, axis=-1, keepdims=True)
    centred = row_data - row_mean
    inv_std = lax.rsqrt(jnp.mean(centred * centred, axis=-1, keepdims=True) + eps)
    normed = centred * inv_std
    scaled = normed * gain_vec.astype(jnp.float32) + shift_vec.astype(jnp.float32)
    return (normed, inv_std, scaled.astype(jnp.bfloat16))


def norm_backward(grad_norm, normed, inv_std, gain_vec):
    scaled = grad_norm * gain_vec.astype(jnp.float32)
    first_mean = jnp.mean(scaled, axis=-1, keepdims=True)
    second_mean = jnp.mean(scaled * normed, axis=-1, keepdims=True)
    return inv_std * (scaled - first_mean - normed * second_mean)


def contract_rows(left_mat, right_mat):
    return lax.dot_general(
        left_mat, right_mat, (((0,), (0,)), ((), ())), preferred_element_type=jnp.float32
    )


def times_transposed(left_mat, right_mat):
    return lax.dot_general(
        left_mat, right_mat, (((1,), (1,)), ((), ())), preferred_element_type=jnp.float32
    )


class Place:
    def __init__(self, far_count):
        index = lax.axis_index("dp")
        self.far_count = far_count
        self.tensor = lax.axis_index("tensor")
        self.core = lax.rem(index, 2)
        self.near = lax.rem(index // 2, 2)
        self.far = index // 4

    def index(self, far, near, core):
        return (far * 2 + near) * 2 + core

    def far_at(self, step):
        return lax.rem(self.far + step + self.far_count, self.far_count)

    def peer(self, kind, step=0):
        far, near, core, tensor = self.far, self.near, self.core, self.tensor
        if kind == "far":
            far = self.far_at(step)
        if kind == "near":
            near = 1 - near
        if kind == "core":
            core = 1 - core
        if kind == "tensor":
            tensor = 1 - tensor
        return {"dp": self.index(far, near, core), "tensor": tensor}

    def greet(self):
        barrier = pltpu.get_barrier_semaphore()
        peers = [self.peer("far", step) for step in range(1, self.far_count)]
        peers += [self.peer("near"), self.peer("core"), self.peer("tensor")]
        for peer in peers:
            pl.semaphore_signal(barrier, inc=1, device_id=peer, device_id_type=MESH)
        pl.semaphore_wait(barrier, len(peers))


def columns_at(tensor, width, start=0, size=None):
    return pl.ds(pl.multiple_of(tensor * width + start, LANES), width if size is None else size)


def gather_kernel(far_count, array_count, pieces, *refs):
    group_count = len(pieces)
    own_arrays = refs[:array_count]
    tail_ref = refs[array_count]
    full_refs = refs[array_count + 1 : 2 * array_count + 1]
    halo_ref = refs[2 * array_count + 1]
    local_sem, tail_sem, far_sem, x_sem, y_sem, diag_sem, core_sem = refs[2 * array_count + 2 :]
    own_refs = []
    for array, lead, first, _, size in pieces:
        own = own_arrays[array]
        own_refs.append(own.at[:, pl.ds(first, size)] if lead is None else own.at[lead])
    at = Place(far_count)
    at.greet()
    sent, arrivals = [], []

    def slot(group, tensor, far, near, core):
        array, _, _, start, size = pieces[group]
        block_width = full_refs[array].shape[2] // 2
        columns = columns_at(tensor, block_width, start, size)
        return full_refs[array].at[at.index(far, near, core), :, columns]

    def send(source, target, sems, place, peer):
        copy = pltpu.make_async_remote_copy(
            src_ref=source,
            dst_ref=target,
            send_sem=sems.at[(0,) + place],
            recv_sem=sems.at[(1,) + place],
            device_id=peer,
            device_id_type=MESH,
        )
        copy.start()
        sent.append(copy)

    def arrived(target, sems, place, peer):
        pltpu.make_async_remote_copy(
            src_ref=target,
            dst_ref=target,
            send_sem=sems.at[(0,) + place],
            recv_sem=sems.at[(1,) + place],
            device_id=peer,
            device_id_type=MESH,
        ).wait_recv()

    groups = range(group_count)
    x_first, loads = [], [0, 0]
    for piece in pieces:
        x_first.append(loads[0] <= loads[1])
        loads[0 if x_first[-1] else 1] += piece[4]
    x_peer, y_peer, core_peer = at.peer("tensor"), at.peer("near"), at.peer("core")
    local = []
    for group in groups:
        own_slot = slot(group, at.tensor, at.far, at.near, at.core)
        for step in range(1, far_count):
            send(own_refs[group], own_slot, far_sem, (group, step), at.peer("far", step))
        send(own_refs[group], own_slot, x_sem, (group, 0), x_peer)
        send(own_refs[group], own_slot, y_sem, (group, 0), y_peer)
        send(own_refs[group], own_slot, core_sem, (group, 0, 0), core_peer)
        if group == 0:
            copy = pltpu.make_async_remote_copy(
                src_ref=tail_ref,
                dst_ref=halo_ref,
                send_sem=tail_sem.at[0],
                recv_sem=tail_sem.at[1],
                device_id=x_peer,
                device_id_type=MESH,
            )
            copy.start()
            tail_copy = copy
        keep = pltpu.make_async_copy(own_refs[group], own_slot, local_sem.at[group])
        keep.start()
        local.append(keep)

    def spread(group, step):
        far = at.far_at(-step)
        here = slot(group, at.tensor, far, at.near, at.core)
        arrived(here, far_sem, (group, step), x_peer)
        send(here, here, x_sem, (group, step), x_peer)
        send(here, here, y_sem, (group, step), y_peer)
        send(here, here, core_sem, (group, 0, step), core_peer)

    def relay(group, step):
        far = at.far_at(-step)
        from_x = slot(group, 1 - at.tensor, far, at.near, at.core)
        arrived(from_x, x_sem, (group, step), x_peer)
        if x_first[group]:
            send(from_x, from_x, diag_sem, (group, step), y_peer)
        send(from_x, from_x, core_sem, (group, 1, step), core_peer)
        from_y = slot(group, at.tensor, far, 1 - at.near, at.core)
        arrived(from_y, y_sem, (group, step), y_peer)
        if not x_first[group]:
            send(from_y, from_y, diag_sem, (group, step), x_peer)
        send(from_y, from_y, core_sem, (group, 2, step), core_peer)

    def corner(group, step):
        far = at.far_at(-step)
        diag = slot(group, 1 - at.tensor, far, 1 - at.near, at.core)
        arrived(diag, diag_sem, (group, step), y_peer if x_first[group] else x_peer)
        send(diag, diag, core_sem, (group, 3, step), core_peer)

    for group in groups:
        relay(group, 0)
        for step in range(1, far_count):
            spread(group, step)
            if group:
                corner(group - 1, step - 1)
        if group:
            corner(group - 1, far_count - 1)
        for step in range(1, far_count):
            relay(group, step)
    for step in range(far_count):
        corner(group_count - 1, step)
    for group in groups:
        for step in range(far_count):
            far = at.far_at(-step)
            for kind, (flip_x, flip_y) in enumerate(((0, 0), (1, 0), (0, 1), (1, 1))):
                tensor = 1 - at.tensor if flip_x else at.tensor
                near = 1 - at.near if flip_y else at.near
                arrived(
                    slot(group, tensor, far, near, 1 - at.core),
                    core_sem,
                    (group, kind, step),
                    core_peer,
                )
    for copy in sent:
        copy.wait_send()
    tail_copy.wait()
    for keep in local:
        keep.wait()


def gather_weights(own_blocks, tail):
    dp_size, tensor_size = lax.axis_size("dp"), lax.axis_size("tensor")
    far_count = dp_size // 4
    array_count = len(own_blocks)
    shapes, pieces = [], []
    for array, own in enumerate(own_blocks):
        size = own.shape[-1]
        lead_count = own.shape[0] if own.ndim == 3 else 1
        block_width = lead_count * size
        shapes.append(
            jax.ShapeDtypeStruct((dp_size, own.shape[-2], tensor_size * block_width), own.dtype)
        )
        if own.ndim == 3:
            pieces += [(array, lead, 0, lead * size, size) for lead in range(lead_count)]
        elif size < 8 * LANES:
            pieces.append((array, None, 0, 0, size))
        else:
            cut = size // 2
            pieces += [(array, None, first, first, cut) for first in (0, cut)]
    shapes.append(jax.ShapeDtypeStruct(tail.shape, tail.dtype))
    count = len(pieces)
    dma = pltpu.SemaphoreType.DMA
    return pl.pallas_call(
        functools.partial(gather_kernel, far_count, array_count, tuple(pieces)),
        out_shape=shapes,
        in_specs=[pl.BlockSpec(memory_space=pltpu.VMEM)] * (array_count + 1),
        out_specs=[pl.BlockSpec(memory_space=pl.ANY)] * (array_count + 1),
        scratch_shapes=[
            dma((count,)),
            dma((2,)),
            dma((2, count, far_count)),
            dma((2, count, far_count)),
            dma((2, count, far_count)),
            dma((2, count, far_count)),
            dma((2, count, 4, far_count)),
        ],
        compiler_params=pltpu.CompilerParams(
            collective_id=0, has_side_effects=True, vmem_limit_bytes=VMEM_BYTES
        ),
        name="gather_weights",
    )(*own_blocks, tail)


def scatter_kernel(far_count, group_count, *refs):
    part_refs = refs[:group_count]
    out_refs = refs[group_count : 2 * group_count]
    (
        result,
        total,
        core_in,
        x_in,
        y_in,
        diag_in,
        far_in,
        core_sem,
        x_sem,
        y_sem,
        diag_x_sem,
        diag_y_sem,
        far_sem,
    ) = refs[2 * group_count :]
    at = Place(far_count)
    at.greet()
    sent = []
    tensor_size = 2
    widths = [ref.shape[2] // tensor_size for ref in part_refs]
    offsets = [sum(widths[:group]) for group in range(group_count)]
    all_columns = sum(widths)
    half = all_columns // 2 // LANES * LANES
    low, high = pl.ds(0, half), pl.ds(half, all_columns - half)
    x_peer, y_peer, core_peer = at.peer("tensor"), at.peer("near"), at.peer("core")
    order = list(range(1, far_count)) + [0]
    own, by_x, by_y, diag = range(4)
    flips = ((0, 0), (1, 0), (0, 1), (1, 1))

    def make(source, target, sems, place, peer):
        return pltpu.make_async_remote_copy(
            src_ref=source,
            dst_ref=target,
            send_sem=sems.at[(0,) + place],
            recv_sem=sems.at[(1,) + place],
            device_id=peer,
            device_id_type=MESH,
        )

    def send(*args):
        copy = make(*args)
        copy.start()
        sent.append(copy)

    def slot(group, kind, step, core):
        flip_x, flip_y = flips[kind]
        tensor = 1 - at.tensor if flip_x else at.tensor
        near = 1 - at.near if flip_y else at.near
        index = at.index(at.far_at(step), near, core)
        return part_refs[group].at[index, :, columns_at(tensor, widths[group])]

    def core_slot(group, kind, step):
        return core_in.at[kind, step, :, pl.ds(offsets[group], widths[group])]

    kinds = (diag, by_x, by_y, own)
    for step in order:
        for kind in kinds:
            for group in range(group_count):
                send(
                    slot(group, kind, step, 1 - at.core),
                    core_slot(group, kind, step),
                    core_sem,
                    (group, kind, step),
                    core_peer,
                )

    def meet(kind, step):
        for group in range(group_count):
            target = core_slot(group, kind, step)
            make(target, target, core_sem, (group, kind, step), core_peer).wait_recv()
            columns = pl.ds(offsets[group], widths[group])
            mine = slot(group, kind, step, at.core)
            total[kind, step, :, columns] = (
                mine[...].astype(jnp.float32) + target[...].astype(jnp.float32)
            ).astype(jnp.bfloat16)

    def add_to(kind, step, columns, source):
        total[kind, step, :, columns] = (
            total[kind, step, :, columns].astype(jnp.float32) + source[...].astype(jnp.float32)
        ).astype(jnp.bfloat16)

    for step in order:
        meet(diag, step)
        corner = total.at[diag, step]
        send(corner.at[:, low], diag_in.at[step, :, low], diag_y_sem, (step,), y_peer)
        send(corner.at[:, high], diag_in.at[step, :, high], diag_x_sem, (step,), x_peer)
        meet(by_x, step)
        meet(by_y, step)
        meet(own, step)

    for step in order:
        from_y = diag_in.at[step, :, low]
        make(from_y, from_y, diag_y_sem, (step,), y_peer).wait_recv()
        add_to(by_x, step, low, from_y)
        send(total.at[by_x, step], x_in.at[step], x_sem, (step,), x_peer)
        from_x = diag_in.at[step, :, high]
        make(from_x, from_x, diag_x_sem, (step,), x_peer).wait_recv()
        add_to(by_y, step, high, from_x)
        send(total.at[by_y, step], y_in.at[step], y_sem, (step,), y_peer)

    for step in order:
        make(x_in.at[step], x_in.at[step], x_sem, (step,), x_peer).wait_recv()
        make(y_in.at[step], y_in.at[step], y_sem, (step,), y_peer).wait_recv()
        merged = (
            total[own, step].astype(jnp.float32)
            + x_in[step].astype(jnp.float32)
            + y_in[step].astype(jnp.float32)
        )
        if step:
            total[own, step] = merged.astype(jnp.bfloat16)
            send(total.at[own, step], far_in.at[step], far_sem, (step,), at.peer("far", step))
        else:
            result[...] = merged
    for step in range(1, far_count):
        make(far_in.at[step], far_in.at[step], far_sem, (step,), at.peer("far", step)).wait_recv()
        if step < far_count - 1:
            result[...] += far_in[step].astype(jnp.float32)
    for group in range(group_count):
        out_ref = out_refs[group]
        width = out_ref.shape[-1]
        for lead in range(widths[group] // width):
            columns = pl.ds(offsets[group] + lead * width, width)
            held = result[:, columns]
            if far_count > 1:
                held += far_in[far_count - 1, :, columns].astype(jnp.float32)
            if len(out_ref.shape) == 3:
                out_ref[lead] = held
            else:
                out_ref[...] = held
    for copy in sent:
        copy.wait_send()


def scatter_grads(parts, out_shapes):
    dp_size, tensor_size = lax.axis_size("dp"), lax.axis_size("tensor")
    far_count = dp_size // 4
    count = len(parts)
    rows = parts[0].shape[1]
    all_columns = sum(part.shape[2] for part in parts) // tensor_size
    dma = pltpu.SemaphoreType.DMA
    block = (rows, all_columns)
    return pl.pallas_call(
        functools.partial(scatter_kernel, far_count, count),
        out_shape=[jax.ShapeDtypeStruct(shape, jnp.float32) for shape in out_shapes],
        in_specs=[pl.BlockSpec(memory_space=pltpu.VMEM)] * count,
        out_specs=[pl.BlockSpec(memory_space=pltpu.VMEM)] * count,
        scratch_shapes=[
            pltpu.VMEM(block, jnp.float32),
            pltpu.VMEM((4, far_count) + block, jnp.bfloat16),
            pltpu.VMEM((4, far_count) + block, jnp.bfloat16),
            pltpu.VMEM((far_count,) + block, jnp.bfloat16),
            pltpu.VMEM((far_count,) + block, jnp.bfloat16),
            pltpu.VMEM((far_count,) + block, jnp.bfloat16),
            pltpu.VMEM((far_count,) + block, jnp.bfloat16),
            dma((2, count, 4, far_count)),
            dma((2, far_count)),
            dma((2, far_count)),
            dma((2, far_count)),
            dma((2, far_count)),
            dma((2, far_count)),
        ],
        compiler_params=pltpu.CompilerParams(
            collective_id=1, has_side_effects=True, vmem_limit_bytes=VMEM_BYTES
        ),
        name="scatter_grads",
    )(*parts)


def head_blocks(q_ref, k_ref, v_ref, id_row, id_col, halo):
    query_rows = id_col.shape[0]
    lane = lax.broadcasted_iota(jnp.int32, (halo, LANES), 1)
    window = 2 * halo
    row = lax.broadcasted_iota(jnp.int32, (halo, window), 0)
    column = lax.broadcasted_iota(jnp.int32, (halo, window), 1)
    causal = column <= row + halo
    for block in range(query_rows // halo):
        first = block * halo
        query = q_ref[first + halo : first + 2 * halo, :]
        keys = k_ref[first : first + window, :]
        values = v_ref[first : first + window, :]
        same = id_col[first : first + halo, :] == id_row[:, first : first + window]
        allowed = causal & same
        for head in range(LANES // HD):
            mine = (lane >= head * HD) & (lane < (head + 1) * HD)
            query_head = jnp.where(mine, query, jnp.zeros_like(query))
            scores = times_transposed(query_head, keys) * scale_factor
            weight = jnp.where(allowed, jnp.exp(scores), 0.0)
            probs = weight / jnp.sum(weight, axis=-1, keepdims=True)
            yield first, head, mine, query_head, keys, values, probs


def attend_kernel(halo, q_ref, k_ref, v_ref, id_row, id_col, mixed_ref):
    held = None
    for first, head, mine, _, _, values, probs in head_blocks(
        q_ref, k_ref, v_ref, id_row, id_col, halo
    ):
        part = jnp.dot(probs.astype(jnp.bfloat16), values, preferred_element_type=jnp.float32)
        held = part if head == 0 else jnp.where(mine, part, held)
        if head == LANES // HD - 1:
            mixed_ref[first : first + halo, :] = held.astype(jnp.bfloat16)


def attend_back_kernel(
    halo, q_ref, k_ref, v_ref, id_row, id_col, mixed_ref, grad_ref, dq_ref, dk_ref, dv_ref
):
    dk_ref[...] = jnp.zeros_like(dk_ref)
    dv_ref[...] = jnp.zeros_like(dv_ref)
    for first, head, mine, query_head, keys, values, probs in head_blocks(
        q_ref, k_ref, v_ref, id_row, id_col, halo
    ):
        window = keys.shape[0]
        grad = grad_ref[first : first + halo, :]
        grad_head = jnp.where(mine, grad, jnp.zeros_like(grad))
        mixed = mixed_ref[first : first + halo, :]
        delta = jnp.sum(
            grad_head.astype(jnp.float32) * mixed.astype(jnp.float32), axis=-1, keepdims=True
        )
        grad_probs = times_transposed(grad_head, values)
        grad_scores = (probs * (grad_probs - delta) * scale_factor).astype(jnp.bfloat16)
        dv_ref[first : first + window, :] += contract_rows(probs.astype(jnp.bfloat16), grad_head)
        dk_ref[first : first + window, :] += contract_rows(grad_scores, query_head)
        part = jnp.dot(grad_scores, keys, preferred_element_type=jnp.float32)
        if head == 0:
            dq_ref[first : first + halo, :] = part
        else:
            dq_ref[first : first + halo, :] = jnp.where(
                mine, part, dq_ref[first : first + halo, :]
            )


def attend_specs(qkv, halo, tensor_size):
    ext_rows = qkv.shape[0]
    pairs = qkv.shape[1] // 3 // tensor_size // LANES

    def part_of(which):
        return pl.BlockSpec(
            (ext_rows, LANES), lambda pair: (0, pair // pairs * 3 * pairs + which * pairs + pair % pairs)
        )

    ids = [
        pl.BlockSpec((1, ext_rows), lambda pair: (0, 0)),
        pl.BlockSpec((ext_rows - halo, 1), lambda pair: (0, 0)),
    ]
    return pairs * tensor_size, [part_of(0), part_of(1), part_of(2)] + ids


def attend(qkv, id_row, id_col, halo, tensor_size):
    steps, specs = attend_specs(qkv, halo, tensor_size)
    rows = qkv.shape[0] - halo
    return pl.pallas_call(
        functools.partial(attend_kernel, halo),
        grid=(steps,),
        in_specs=specs,
        out_specs=pl.BlockSpec((rows, LANES), lambda pair: (0, pair)),
        out_shape=jax.ShapeDtypeStruct((rows, steps * LANES), jnp.bfloat16),
        name="attend",
    )(qkv, qkv, qkv, id_row, id_col)


def attend_back(qkv, id_row, id_col, mixed, grad_mixed, halo, tensor_size):
    steps, specs = attend_specs(qkv, halo, tensor_size)
    ext_rows = qkv.shape[0]
    rows = ext_rows - halo
    short = pl.BlockSpec((rows, LANES), lambda pair: (0, pair))
    tall = pl.BlockSpec((ext_rows, LANES), lambda pair: (0, pair))
    width = steps * LANES
    return pl.pallas_call(
        functools.partial(attend_back_kernel, halo),
        grid=(steps,),
        in_specs=specs + [short, short],
        out_specs=[short, tall, tall],
        out_shape=[
            jax.ShapeDtypeStruct((rows, width), jnp.float32),
            jax.ShapeDtypeStruct((ext_rows, width), jnp.float32),
            jax.ShapeDtypeStruct((ext_rows, width), jnp.float32),
        ],
        name="attend_back",
    )(qkv, qkv, qkv, id_row, id_col, mixed, grad_mixed)


GELU_C = 0.7978845608028654
GELU_A = 0.044715
ROWS_AT = {"gain_one": 0, "shift_one": 1, "out_bias": 2, "gain_two": 3, "shift_two": 4, "down_bias": 5}
Q_BIAS, V_BIAS, UP_BIAS = 6, 7, 8
SMALL_ROWS = 16
TILE = 256


def loop(count, body):
    lax.fori_loop(0, count, lambda i, carry: (body(i), carry)[1], 0)


def lanes(start, size=TILE):
    return pl.ds(pl.multiple_of(start, LANES), size)


def forward_kernel(far_count, halo, *refs):
    (
        own_qkv,
        own_out,
        own_up,
        own_down,
        own_small,
        x_hbm,
        cot_hbm,
        ids_ref,
        qkv_w_out,
        out_w_out,
        up_w_out,
        ln1_out,
        qkv_out,
        mixed_out,
        middle_out,
        ln2_out,
        hidden_out,
        grad_pre_out,
        layer_out,
        params,
        up_grad,
        w_qkv,
        w_out,
        w_up,
        w_down,
        small_all,
        x_ref,
        cot_ref,
        cot_bf,
        ln1,
        qkv,
        mixed,
        middle,
        total,
        ln2,
        hidden,
        slope,
        grad_pre,
        id_ref,
        mask_ref,
        load_sem,
        out_sem,
        local_sem,
        tail_sem,
        far_sem,
        x_sem,
        y_sem,
        diag_sem,
        core_sem,
    ) = refs
    f32, bf16 = jnp.float32, jnp.bfloat16
    rows, width = x_ref.shape
    own_rows = own_out.shape[0]
    attn = own_out.shape[1]
    hid = own_up.shape[1]
    cut = hid // 2
    at = Place(far_count)
    at.greet()
    sent, keeps = [], {}
    x_load = pltpu.make_async_copy(x_hbm, x_ref, load_sem.at[0])
    cot_load = pltpu.make_async_copy(cot_hbm, cot_ref, load_sem.at[1])
    x_load.start()
    cot_load.start()

    def block_of(full, width_of, start, size):
        def place(index, tensor):
            row = pl.multiple_of(index * own_rows, 16)
            return full.at[pl.ds(row, own_rows), lanes(tensor * width_of + start, size)]

        return place

    groups = [(own_small, lambda index, tensor: small_all.at[index * 2 + tensor], 0)]
    for lead in range(3):
        def place(index, tensor, lead=lead):
            row = pl.multiple_of(index * own_rows, 16)
            return w_qkv.at[pl.ds(row, own_rows), lanes(lead * width + tensor * attn, attn)]

        groups.append((own_qkv.at[lead], place, attn))
    groups.append((own_out, block_of(w_out, attn, 0, attn), attn))
    for half in range(2):
        columns = pl.ds(half * cut, cut)
        groups.append((own_up.at[:, columns], block_of(w_up, hid, half * cut, cut), cut))
        groups.append((own_down.at[:, columns], block_of(w_down, hid, half * cut, cut), cut))
    count = len(groups)
    x_first, loads = [], [attn, 0]
    for _, _, size in groups:
        x_first.append(loads[0] >= loads[1])
        loads[1 if x_first[-1] else 0] += size

    def slot(group, tensor, far, near, core):
        return groups[group][1](at.index(far, near, core), tensor)

    def remote(source, target, sems, place, peer):
        return pltpu.make_async_remote_copy(
            src_ref=source,
            dst_ref=target,
            send_sem=sems.at[(0,) + place],
            recv_sem=sems.at[(1,) + place],
            device_id=peer,
            device_id_type=MESH,
        )

    def send(*args):
        copy = remote(*args)
        copy.start()
        sent.append(copy)

    def arrived(target, sems, place, peer):
        remote(target, target, sems, place, peer).wait_recv()

    x_peer, y_peer, core_peer = at.peer("tensor"), at.peer("near"), at.peer("core")

    def own(group):
        source = groups[group][0]
        target = slot(group, at.tensor, at.far, at.near, at.core)
        for step in range(1, far_count):
            send(source, target, far_sem, (group, step), at.peer("far", step))
        send(source, target, x_sem, (group, 0), x_peer)
        send(source, target, y_sem, (group, 0), y_peer)
        send(source, target, core_sem, (group, 0, 0), core_peer)
        keep = pltpu.make_async_copy(source, target, local_sem.at[group])
        keep.start()
        keeps[group] = keep

    def spread(group, step):
        here = slot(group, at.tensor, at.far_at(-step), at.near, at.core)
        arrived(here, far_sem, (group, step), x_peer)
        send(here, here, x_sem, (group, step), x_peer)
        send(here, here, y_sem, (group, step), y_peer)
        send(here, here, core_sem, (group, 0, step), core_peer)

    def relay(group, step):
        far = at.far_at(-step)
        from_x = slot(group, 1 - at.tensor, far, at.near, at.core)
        arrived(from_x, x_sem, (group, step), x_peer)
        if x_first[group]:
            send(from_x, from_x, diag_sem, (group, step), y_peer)
        send(from_x, from_x, core_sem, (group, 1, step), core_peer)
        from_y = slot(group, at.tensor, far, 1 - at.near, at.core)
        arrived(from_y, y_sem, (group, step), y_peer)
        if not x_first[group]:
            send(from_y, from_y, diag_sem, (group, step), x_peer)
        send(from_y, from_y, core_sem, (group, 2, step), core_peer)

    def corner(group, step):
        diag = slot(group, 1 - at.tensor, at.far_at(-step), 1 - at.near, at.core)
        arrived(diag, diag_sem, (group, step), y_peer if x_first[group] else x_peer)
        send(diag, diag, core_sem, (group, 3, step), core_peer)

    def finish(group):
        for step in range(far_count):
            far = at.far_at(-step)
            for kind, (flip_x, flip_y) in enumerate(((0, 0), (1, 0), (0, 1), (1, 1))):
                tensor = 1 - at.tensor if flip_x else at.tensor
                near = 1 - at.near if flip_y else at.near
                place = slot(group, tensor, far, near, 1 - at.core)
                arrived(place, core_sem, (group, kind, step), core_peer)
        keeps[group].wait()

    stores = []

    def store(source, target):
        copy = pltpu.make_async_copy(source, target, out_sem.at[len(stores)])
        copy.start()
        stores.append(copy)

    def vector(row, columns=slice(None)):
        return params[row : row + 1, columns]

    def norm_rows(source, target, first, size, shift, gain_row, shift_row):
        data = source[pl.ds(first, size), :]
        row_mean = jnp.mean(data, axis=-1, keepdims=True)
        centred = data - row_mean
        inv_std = lax.rsqrt(jnp.mean(centred * centred, axis=-1, keepdims=True) + eps)
        scaled = centred * inv_std * vector(gain_row) + vector(shift_row)
        target[pl.ds(first + shift, size), :] = scaled.astype(bf16)

    def first_norm():
        held = small_all[0].astype(f32)
        for device in range(1, small_all.shape[0]):
            held = held + small_all[device].astype(f32)
        params[...] = held
        x_load.wait()
        norm_rows(x_ref, ln1, rows - halo, halo, halo, 0, 1)
        send(ln1.at[pl.ds(rows, halo)], ln1.at[pl.ds(0, halo)], tail_sem, (), x_peer)

        def one(i):
            norm_rows(x_ref, ln1, pl.multiple_of(i * halo, halo), halo, halo, 0, 1)

        loop(rows // halo - 1, one)

    def masks():
        id_ref[:, :halo] = jnp.full((1, halo), -1, jnp.int32)
        id_ref[:, halo:] = ids_ref[...]
        window = 2 * halo
        row = lax.broadcasted_iota(jnp.int32, (halo, window), 0)
        column = lax.broadcasted_iota(jnp.int32, (halo, window), 1)
        causal = column <= row + halo
        for block in range(rows // halo):
            first = at.tensor * rows + block * halo
            keys = id_ref[:, lanes(first, window)]
            queries = jnp.broadcast_to(id_ref[:, lanes(first + halo, halo)], (halo, halo)).T
            same = jnp.concatenate([queries, queries], axis=1) == keys
            mask_ref[block] = jnp.where(same & causal, 1.0, 0.0)
        cot_load.wait()

        def one(i):
            part = pl.ds(pl.multiple_of(i * halo, halo), halo)
            cot_bf[part, :] = cot_ref[part, :].astype(bf16)

        loop(rows // halo, one)

    def project(lead, bias_row, first):
        def one(i):
            columns = lanes(lead * width + i * TILE)
            part = jnp.dot(ln1[first:, :], w_qkv[:, columns], preferred_element_type=f32)
            if bias_row is not None:
                part = part + params[bias_row : bias_row + 1, lanes(i * TILE)]
            qkv[first:, columns] = part.astype(bf16)

        loop(width // TILE, one)

    def attention(first_pair, pair_count):
        lane = lax.broadcasted_iota(jnp.int32, (halo, LANES), 1)

        def one(i):
            pair = first_pair + i
            q_at, k_at = lanes(pair * LANES, LANES), lanes(width + pair * LANES, LANES)
            v_at = lanes(2 * width + pair * LANES, LANES)
            for block in range(rows // halo):
                first = block * halo
                query = qkv[first + halo : first + 2 * halo, q_at]
                keys = qkv[first : first + 2 * halo, k_at]
                values = qkv[first : first + 2 * halo, v_at]
                allowed = mask_ref[block] > 0.5
                held = None
                for head in range(LANES // HD):
                    mine = (lane >= head * HD) & (lane < (head + 1) * HD)
                    query_head = jnp.where(mine, query, jnp.zeros_like(query))
                    scores = times_transposed(query_head, keys) * scale_factor
                    weight = jnp.where(allowed, jnp.exp(scores), 0.0)
                    probs = weight / jnp.sum(weight, axis=-1, keepdims=True)
                    part = jnp.dot(probs.astype(bf16), values, preferred_element_type=f32)
                    held = part if head == 0 else jnp.where(mine, part, held)
                mixed[first : first + halo, q_at] = held.astype(bf16)

        loop(pair_count, one)

    def project_out():
        def one(i):
            columns = lanes(i * TILE)
            out_rows = pl.ds(pl.multiple_of(i * TILE, TILE), TILE)
            part = x_ref[:, columns] + times_transposed(mixed[...], w_out[out_rows, :])
            part = part + params[2:3, columns]
            middle[:, columns] = part
            total[:, columns] = part + params[5:6, columns]

        loop(width // TILE, one)

    def second_norm():
        def one(i):
            norm_rows(middle, ln2, pl.multiple_of(i * halo, halo), halo, 0, 3, 4)

        loop(rows // halo, one)

    def go_up(half, tensor):
        base = tensor * hid + half * cut

        def one(i):
            columns = lanes(base + i * TILE)
            bias_row = UP_BIAS + base // width
            bias = params[bias_row : bias_row + 1, lanes(base % width + i * TILE)]
            u = jnp.dot(ln2[...], w_up[:, columns], preferred_element_type=f32) + bias
            square = u * u
            bent = jnp.tanh(GELU_C * (u + GELU_A * (u * square)))
            half_sum = 0.5 + 0.5 * bent
            hidden[:, columns] = (u * half_sum).astype(bf16)
            turn = (0.5 * GELU_C) * (1.0 + (3.0 * GELU_A) * square)
            slope[:, columns] = half_sum + u * (1.0 - bent * bent) * turn

        loop(cut // TILE, one)

    def go_down(half, tensor):
        base = tensor * hid + half * cut

        def one(i):
            columns = lanes(i * TILE)
            out_rows = pl.ds(pl.multiple_of(i * TILE, TILE), TILE)
            total[:, columns] += times_transposed(
                hidden[:, base : base + cut], w_down[out_rows, base : base + cut]
            )

        loop(width // TILE, one)

    def go_back(half, tensor):
        base = tensor * hid + half * cut

        def one(i):
            columns = lanes(base + i * TILE)
            part = jnp.dot(cot_bf[...], w_down[:, columns], preferred_element_type=f32)
            part = part * slope[:, columns]
            grad_pre[:, columns] = part.astype(bf16)
            up_grad[:, columns] = jnp.sum(part, axis=0, keepdims=True)

        loop(cut // TILE, one)

    def halo_here():
        tail = ln1.at[pl.ds(0, halo)]
        remote(tail, tail, tail_sem, (), x_peer).wait_recv()
        store(ln1.at[pl.ds(halo, rows)], ln1_out)

    pairs = width // LANES
    step_pairs = pairs // 3 if pairs % 3 == 0 else pairs
    work = {
        0: [first_norm, masks],
        1: [lambda: project(0, Q_BIAS, halo)],
        2: [lambda: (halo_here(), project(1, None, 0))],
        3: [lambda: (project(2, V_BIAS, 0), store(w_qkv, qkv_w_out), store(qkv, qkv_out))]
        + [
            functools.partial(attention, first, step_pairs)
            for first in range(0, pairs, step_pairs)
        ],
        4: [
            lambda: (project_out(), store(w_out, out_w_out), store(mixed, mixed_out)),
            lambda: (second_norm(), store(middle, middle_out), store(ln2, ln2_out)),
        ],
    }
    for half in range(2):
        work[5 + 2 * half] = [functools.partial(go_up, half, tensor) for tensor in range(2)]
        work[6 + 2 * half] = [functools.partial(go_down, half, tensor) for tensor in range(2)]
        work[6 + 2 * half] += [functools.partial(go_back, half, tensor) for tensor in range(2)]
    work[7].append(lambda: (store(w_up, up_w_out), store(hidden, hidden_out)))
    queue = []

    def tick():
        if queue:
            queue.pop(0)()

    ahead = 4
    for group in range(min(ahead, count)):
        own(group)
    for group in range(count):
        if group + ahead < count:
            own(group + ahead)
        relay(group, 0)
        tick()
        for step in range(1, far_count):
            spread(group, step)
            if group:
                corner(group - 1, step - 1)
            if step % 2 == 0:
                tick()
        if group:
            corner(group - 1, far_count - 1)
        for step in range(1, far_count):
            relay(group, step)
            if step % 2 == 0:
                tick()
        if group:
            finish(group - 1)
            queue += work[group - 1]
            tick()
    for step in range(far_count):
        corner(count - 1, step)
    while queue:
        tick()
    finish(count - 1)
    queue += work[count - 1]
    while queue:
        tick()
    store(total, layer_out)
    store(grad_pre, grad_pre_out)
    for copy in sent:
        copy.wait_send()
    for copy in stores:
        copy.wait()


def forward_pass(own_qkv, own_out, own_up, own_down, own_small, inputs, cot, ids, halo):
    f32, bf16 = jnp.float32, jnp.bfloat16
    dp_size = lax.axis_size("dp")
    far_count = dp_size // 4
    rows, width = inputs.shape
    hid = 2 * own_up.shape[1]
    ext = rows + halo
    count = 9
    dma = pltpu.SemaphoreType.DMA
    shape, vmem = jax.ShapeDtypeStruct, pltpu.VMEM
    any_spec, vmem_spec = pl.BlockSpec(memory_space=pl.ANY), pl.BlockSpec(memory_space=pltpu.VMEM)
    return pl.pallas_call(
        functools.partial(forward_kernel, far_count, halo),
        out_shape=[
            shape((width, 3 * width), bf16),
            shape((width, width), bf16),
            shape((width, hid), bf16),
            shape((rows, width), bf16),
            shape((ext, 3 * width), bf16),
            shape((rows, width), bf16),
            shape((rows, width), f32),
            shape((rows, width), bf16),
            shape((rows, hid), bf16),
            shape((rows, hid), bf16),
            shape((rows, width), f32),
            shape((SMALL_ROWS, width), f32),
            shape((1, hid), f32),
        ],
        in_specs=[any_spec] * 7 + [vmem_spec],
        out_specs=[any_spec] * 11 + [vmem_spec] * 2,
        scratch_shapes=[
            vmem((width, 3 * width), bf16),
            vmem((width, width), bf16),
            vmem((width, hid), bf16),
            vmem((width, hid), bf16),
            vmem((2 * dp_size, SMALL_ROWS, width), bf16),
            vmem((rows, width), f32),
            vmem((rows, width), f32),
            vmem((rows, width), bf16),
            vmem((ext, width), bf16),
            vmem((ext, 3 * width), bf16),
            vmem((rows, width), bf16),
            vmem((rows, width), f32),
            vmem((rows, width), f32),
            vmem((rows, width), bf16),
            vmem((rows, hid), bf16),
            vmem((rows, hid), f32),
            vmem((rows, hid), bf16),
            vmem((1, halo + 2 * rows), jnp.int32),
            vmem((rows // halo, halo, 2 * halo), f32),
            dma((2,)),
            dma((11,)),
            dma((count,)),
            dma((2,)),
            dma((2, count, far_count)),
            dma((2, count, far_count)),
            dma((2, count, far_count)),
            dma((2, count, far_count)),
            dma((2, count, 4, far_count)),
        ],
        compiler_params=pltpu.CompilerParams(
            collective_id=2, has_side_effects=True, vmem_limit_bytes=VMEM_BYTES
        ),
        name="forward_pass",
    )(own_qkv, own_out, own_up, own_down, own_small, inputs, cot, ids)


def backward_kernel(far_count, halo, *refs):
    (
        hidden_hbm,
        cot_hbm,
        ln2_hbm,
        grad_pre_hbm,
        w_up_hbm,
        w_out_hbm,
        w_qkv_hbm,
        middle_hbm,
        x_hbm,
        mixed_hbm,
        qkv_hbm,
        ln1_hbm,
        ids_ref,
        params,
        up_sum,
        input_grad_out,
        own_qkv,
        own_out,
        own_up,
        own_down,
        sums,
        hidden,
        cot_ref,
        ln2,
        grad_pre,
        w_up,
        w_out,
        middle,
        mixed,
        qkv,
        ln1,
        turned,
        cot_bf,
        grad_ln,
        grad_mixed,
        grad_qkv,
        p_down,
        p_up,
        p_out,
        p_qkv,
        rest_k,
        rest_v,
        lent,
        back,
        id_ref,
        mask_ref,
        held,
        core_in,
        x_in,
        y_in,
        diag_in,
        far_in,
        sums_in,
        load_sem,
        halo_sem,
        sums_sem,
        core_sem,
        x_sem,
        y_sem,
        diag_x_sem,
        diag_y_sem,
        far_sem,
    ) = refs
    f32, bf16 = jnp.float32, jnp.bfloat16
    rows, width = cot_ref.shape
    own_rows, attn = own_out.shape
    hid = own_up.shape[1]
    cut = hid // 2
    at = Place(far_count)
    loads = {}

    def load(name, source, target):
        copy = pltpu.make_async_copy(source, target, load_sem.at[len(loads)])
        copy.start()
        loads[name] = copy

    load("cot", cot_hbm, cot_ref)
    load("hidden", hidden_hbm, hidden)
    load("ln2", ln2_hbm, ln2)
    load("grad_pre", grad_pre_hbm, grad_pre)
    load("w_up", w_up_hbm, w_up)
    load("middle", middle_hbm, middle)
    load("w_out", w_out_hbm, w_out)
    load("mixed", mixed_hbm, mixed)
    load("qkv", qkv_hbm, qkv)
    load("ln1", ln1_hbm, ln1)
    at.greet()
    sent = []
    x_peer, y_peer, core_peer = at.peer("tensor"), at.peer("near"), at.peer("core")
    order = list(range(1, far_count)) + [0]
    own, by_x, by_y, diag = range(4)
    flips = ((0, 0), (1, 0), (0, 1), (1, 1))

    groups = []

    def add_group(part, block, first, start, size, out):
        offset = groups[-1][5] + groups[-1][4] if groups else 0
        groups.append((part, block, first, start, size, offset, out))

    for half in range(2):
        columns = slice(half * cut, (half + 1) * cut)
        add_group(p_down, hid, 0, half * cut, cut, own_down.at[:, columns])
    for half in range(2):
        columns = slice(half * cut, (half + 1) * cut)
        add_group(p_up, hid, 0, half * cut, cut, own_up.at[:, columns])
    add_group(p_out, attn, 0, 0, attn, own_out)
    for lead in range(3):
        add_group(p_qkv, attn, lead * width, 0, attn, own_qkv.at[lead])

    def make(source, target, sems, place, peer):
        return pltpu.make_async_remote_copy(
            src_ref=source,
            dst_ref=target,
            send_sem=sems.at[(0,) + place],
            recv_sem=sems.at[(1,) + place],
            device_id=peer,
            device_id_type=MESH,
        )

    def send(*args):
        copy = make(*args)
        copy.start()
        sent.append(copy)

    def arrived(target, sems, place, peer):
        make(target, target, sems, place, peer).wait_recv()

    def slot(group, kind, step, core):
        part, block, first, start, size, _, _ = groups[group]
        flip_x, flip_y = flips[kind]
        tensor = 1 - at.tensor if flip_x else at.tensor
        near = 1 - at.near if flip_y else at.near
        row = pl.multiple_of(at.index(at.far_at(step), near, core) * own_rows, 16)
        return part.at[pl.ds(row, own_rows), lanes(first + tensor * block + start, size)]

    def columns_of(group):
        return pl.ds(groups[group][5], groups[group][4])

    def core_slot(group, kind, step):
        return core_in.at[kind, step, :, columns_of(group)]

    def parts_of(group):
        offset, size = groups[group][5], groups[group][4]
        half = size // 2 // LANES * LANES
        low, high = pl.ds(offset, half), pl.ds(offset + half, size - half)
        return (low, high) if group % 2 else (high, low)

    def stage_core(group):
        for step in order:
            for kind in (diag, by_x, by_y, own):
                source = slot(group, kind, step, 1 - at.core)
                target = core_slot(group, kind, step)
                send(source, target, core_sem, (group, kind, step), core_peer)

    def stage_meet(group):
        for step in order:
            for kind in (diag, by_x, by_y, own):
                target = core_slot(group, kind, step)
                arrived(target, core_sem, (group, kind, step), core_peer)
                mine = slot(group, kind, step, at.core)
                target[...] = (mine[...].astype(f32) + target[...].astype(f32)).astype(bf16)
                if kind == diag:
                    via_y, via_x = parts_of(group)
                    from_y, from_x = diag_in.at[step, :, via_y], diag_in.at[step, :, via_x]
                    corner = core_in.at[diag, step]
                    send(corner.at[:, via_y], from_y, diag_y_sem, (group, step), y_peer)
                    send(corner.at[:, via_x], from_x, diag_x_sem, (group, step), x_peer)

    def stage_corner(group):
        via_y, via_x = parts_of(group)
        columns = columns_of(group)
        for step in order:
            for kind, via, sem, diag_peer, into, into_sem, peer in (
                (by_x, via_y, diag_y_sem, y_peer, x_in, x_sem, x_peer),
                (by_y, via_x, diag_x_sem, x_peer, y_in, y_sem, y_peer),
            ):
                source = diag_in.at[step, :, via]
                arrived(source, sem, (group, step), diag_peer)
                target = core_in.at[kind, step, :, via]
                target[...] = (target[...].astype(f32) + source[...].astype(f32)).astype(bf16)
                place = into.at[step, :, columns]
                send(core_in.at[kind, step, :, columns], place, into_sem, (group, step), peer)

    def stage_merge(group):
        columns = columns_of(group)
        for step in order:
            arrived(x_in.at[step, :, columns], x_sem, (group, step), x_peer)
            arrived(y_in.at[step, :, columns], y_sem, (group, step), y_peer)
            merged = (
                core_in[own, step, :, columns].astype(f32)
                + x_in[step, :, columns].astype(f32)
                + y_in[step, :, columns].astype(f32)
            )
            if step:
                core_in[own, step, :, columns] = merged.astype(bf16)
                source, target = core_in.at[own, step, :, columns], far_in.at[step, :, columns]
                send(source, target, far_sem, (group, step), at.peer("far", step))
            else:
                groups[group][6][...] = merged

    def stage_far(group):
        columns = columns_of(group)
        out = groups[group][6]
        for step in range(1, far_count):
            place = far_in.at[step, :, columns]
            arrived(place, far_sem, (group, step), at.peer("far", step))
        total = out[...]
        for step in range(1, far_count):
            total = total + far_in[step, :, columns].astype(f32)
        out[...] = total

    def turn(source):
        def one(i):
            part = pl.multiple_of(i * halo, halo)
            turned[:, pl.ds(part, halo)] = source[pl.ds(part, halo), :].T

        loop(rows // halo, one)

    def contract(right, first, part, count):
        def one(i):
            columns = lanes(first + i * TILE)
            grad = jnp.dot(turned[...], right[:, columns], preferred_element_type=f32)
            part[:, columns] = grad.astype(bf16)

        loop(count // TILE, one)

    def contract_half(right, part, half):
        for tensor in range(2):
            contract(right, tensor * hid + half * cut, part, cut)

    def rows_at(i):
        return pl.ds(pl.multiple_of(i * halo, halo), halo)

    def start():
        loads["cot"].wait()

        def one(i):
            cot_bf[rows_at(i), :] = cot_ref[rows_at(i), :].astype(bf16)

        loop(rows // halo, one)
        turn(cot_bf)
        held[...] = jnp.zeros_like(held)
        for row in range(4):
            base = UP_BIAS + row
            held[base : base + 1, :] = up_sum[:, row * width : (row + 1) * width]

    def back_up():
        def one(i):
            out_rows = pl.ds(pl.multiple_of(i * TILE, TILE), TILE)
            grad_ln[:, lanes(i * TILE)] = times_transposed(grad_pre[...], w_up[out_rows, :])

        loop(width // TILE, one)

    def add_sum(row, value):
        held[row : row + 1, :] += jnp.sum(value, axis=0, keepdims=True)

    def normed_rows(source, i):
        data = source[rows_at(i), :]
        centred = data - jnp.mean(data, axis=-1, keepdims=True)
        inv_std = lax.rsqrt(jnp.mean(centred * centred, axis=-1, keepdims=True) + eps)
        return centred * inv_std, inv_std

    def back_second_norm():
        def one(i):
            normed, inv_std = normed_rows(middle, i)
            grad = grad_ln[rows_at(i), :]
            cot = cot_ref[rows_at(i), :]
            add_sum(3, grad * normed)
            add_sum(4, grad)
            grad_middle = cot + norm_backward(grad, normed, inv_std, params[3:4, :])
            add_sum(5, cot)
            add_sum(2, grad_middle)
            middle[rows_at(i), :] = grad_middle
            cot_bf[rows_at(i), :] = grad_middle.astype(bf16)

        loop(rows // halo, one)
        turn(cot_bf)

    def back_out():
        def one(i):
            columns = lanes(i * TILE)
            part = jnp.dot(cot_bf[...], w_out[:, columns], preferred_element_type=f32)
            grad_mixed[:, columns] = part.astype(bf16)

        loop(width // TILE, one)

    def masks():
        id_ref[:, :halo] = jnp.full((1, halo), -1, jnp.int32)
        id_ref[:, halo:] = ids_ref[...]
        window = 2 * halo
        row = lax.broadcasted_iota(jnp.int32, (halo, window), 0)
        column = lax.broadcasted_iota(jnp.int32, (halo, window), 1)
        causal = column <= row + halo
        for block in range(rows // halo):
            first = at.tensor * rows + block * halo
            keys = id_ref[:, lanes(first, window)]
            queries = jnp.broadcast_to(id_ref[:, lanes(first + halo, halo)], (halo, halo)).T
            same = jnp.concatenate([queries, queries], axis=1) == keys
            mask_ref[block] = jnp.where(same & causal, 1.0, 0.0)

    def back_attention(first_pair, pair_count):
        lane = lax.broadcasted_iota(jnp.int32, (halo, LANES), 1)

        def one(i):
            pair = first_pair + i
            q_at, k_at = lanes(pair * LANES, LANES), lanes(width + pair * LANES, LANES)
            v_at = lanes(2 * width + pair * LANES, LANES)
            carry_k = carry_v = None
            query_sum = jnp.zeros((1, LANES), f32)
            value_sum = jnp.zeros((1, LANES), f32)
            for block in range(rows // halo):
                first = block * halo
                query = qkv[first + halo : first + 2 * halo, q_at]
                keys = qkv[first : first + 2 * halo, k_at]
                values = qkv[first : first + 2 * halo, v_at]
                allowed = mask_ref[block] > 0.5
                grad = grad_mixed[first : first + halo, q_at]
                product = grad.astype(f32) * mixed[first : first + halo, q_at].astype(f32)
                query_grad = key_grad = value_grad = None
                for head in range(LANES // HD):
                    mine = (lane >= head * HD) & (lane < (head + 1) * HD)
                    query_head = jnp.where(mine, query, jnp.zeros_like(query))
                    grad_head = jnp.where(mine, grad, jnp.zeros_like(grad))
                    delta = jnp.sum(jnp.where(mine, product, 0.0), axis=-1, keepdims=True)
                    scores = times_transposed(query_head, keys) * scale_factor
                    weight = jnp.where(allowed, jnp.exp(scores), 0.0)
                    probs = weight / jnp.sum(weight, axis=-1, keepdims=True)
                    grad_probs = times_transposed(grad_head, values)
                    grad_scores = (probs * (grad_probs - delta) * scale_factor).astype(bf16)
                    value_part = contract_rows(probs.astype(bf16), grad_head)
                    key_part = contract_rows(grad_scores, query_head)
                    part = jnp.dot(grad_scores, keys, preferred_element_type=f32)
                    if head == 0:
                        query_grad, key_grad, value_grad = part, key_part, value_part
                    else:
                        query_grad = jnp.where(mine, part, query_grad)
                        key_grad, value_grad = key_grad + key_part, value_grad + value_part
                query_sum += jnp.sum(query_grad, axis=0, keepdims=True)
                grad_qkv[first : first + halo, q_at] = query_grad.astype(bf16)
                if block == 0:
                    lent[:, q_at] = key_grad[:halo].astype(bf16)
                    lent[:, k_at] = value_grad[:halo].astype(bf16)
                else:
                    done = pl.ds(first - halo, halo)
                    grad_qkv[done, k_at] = (carry_k + key_grad[:halo]).astype(bf16)
                    whole = carry_v + value_grad[:halo]
                    grad_qkv[done, v_at] = whole.astype(bf16)
                    value_sum += jnp.sum(whole, axis=0, keepdims=True)
                carry_k, carry_v = key_grad[halo:], value_grad[halo:]
            rest_k[:, q_at] = carry_k
            rest_v[:, q_at] = carry_v
            held[Q_BIAS : Q_BIAS + 1, q_at] = query_sum
            held[V_BIAS : V_BIAS + 1, q_at] = value_sum

        loop(pair_count, one)

    def lend():
        send(lent, back, halo_sem, (), x_peer)

    def returned():
        arrived(back, halo_sem, (), x_peer)
        last = pl.ds(rows - halo, halo)
        grad_qkv[last, width : 2 * width] = (rest_k[...] + back[:, :width].astype(f32)).astype(bf16)
        whole = rest_v[...] + back[:, width:].astype(f32)
        grad_qkv[last, 2 * width :] = whole.astype(bf16)
        add_sum(V_BIAS, whole)

    def back_project():
        loads["w_qkv"].wait()

        def one(i):
            out_rows = pl.ds(pl.multiple_of(i * TILE, TILE), TILE)
            weights = w_up[out_rows, : 3 * width]
            grad_ln[:, lanes(i * TILE)] = times_transposed(grad_qkv[...], weights)

        loop(width // TILE, one)

    def back_first_norm():
        loads["x"].wait()

        def one(i):
            normed, inv_std = normed_rows(cot_ref, i)
            grad = grad_ln[rows_at(i), :]
            add_sum(0, grad * normed)
            add_sum(1, grad)
            middle[rows_at(i), :] += norm_backward(grad, normed, inv_std, params[0:1, :])

        loop(rows // halo, one)

    d0, d1, u0, u1, o0, q0, k0, v0 = range(8)
    pairs = width // LANES

    def pair_of(index):
        first, last = index * pairs // 6, (index + 1) * pairs // 6
        if last > first:
            back_attention(first, last - first)

    start()
    loads["hidden"].wait()
    contract_half(hidden, p_down, 0)
    stage_core(d0)
    contract_half(hidden, p_down, 1)
    stage_core(d1)
    stage_meet(d0)
    loads["ln2"].wait()
    loads["grad_pre"].wait()
    turn(ln2)
    contract_half(grad_pre, p_up, 0)
    stage_core(u0)
    stage_meet(d1)
    stage_corner(d0)
    contract_half(grad_pre, p_up, 1)
    stage_core(u1)
    loads["w_up"].wait()
    back_up()
    load("w_qkv", w_qkv_hbm, w_up.at[:, : 3 * width])
    stage_meet(u0)
    stage_corner(d1)
    stage_merge(d0)
    loads["middle"].wait()
    back_second_norm()
    load("x", x_hbm, cot_ref)
    loads["mixed"].wait()
    contract(mixed, 0, p_out, width)
    stage_core(o0)
    stage_meet(u1)
    stage_corner(u0)
    stage_merge(d1)
    stage_far(d0)
    loads["w_out"].wait()
    back_out()
    stage_meet(o0)
    stage_corner(u1)
    masks()
    loads["qkv"].wait()
    pair_of(0)
    stage_merge(u0)
    stage_far(d1)
    pair_of(1)
    stage_corner(o0)
    pair_of(2)
    stage_merge(u1)
    stage_far(u0)
    pair_of(3)
    stage_merge(o0)
    pair_of(4)
    stage_far(u1)
    pair_of(5)
    lend()
    stage_far(o0)
    loads["ln1"].wait()
    turn(ln1)
    contract(grad_qkv, 0, p_qkv, width)
    stage_core(q0)
    returned()
    contract(grad_qkv, width, p_qkv, width)
    stage_core(k0)
    stage_meet(q0)
    contract(grad_qkv, 2 * width, p_qkv, width)
    stage_core(v0)
    stage_meet(k0)
    stage_corner(q0)
    stage_meet(v0)
    stage_corner(k0)
    back_project()
    stage_corner(v0)
    stage_merge(q0)
    back_first_norm()
    result = pltpu.make_async_copy(middle, input_grad_out, load_sem.at[len(loads)])
    result.start()
    sums[0] = held[...]
    send(sums.at[0], sums_in.at[0], sums_sem, (0,), core_peer)
    stage_merge(k0)
    arrived(sums_in.at[0], sums_sem, (0,), core_peer)
    sums[1] = sums[0] + sums_in[0]
    send(sums.at[1], sums_in.at[1], sums_sem, (1,), x_peer)
    stage_merge(v0)
    arrived(sums_in.at[1], sums_sem, (1,), x_peer)
    sums[2] = sums[1] + sums_in[1]
    send(sums.at[2], sums_in.at[2], sums_sem, (2,), y_peer)
    stage_far(q0)
    arrived(sums_in.at[2], sums_sem, (2,), y_peer)
    sums[3] = sums[2] + sums_in[2]
    for step in range(1, far_count):
        send(sums.at[3], sums_in.at[2 + step], sums_sem, (2 + step,), at.peer("far", step))
    stage_far(k0)
    stage_far(v0)
    total = sums[3]
    for step in range(1, far_count):
        arrived(sums_in.at[2 + step], sums_sem, (2 + step,), at.peer("far", step))
        total = total + sums_in[2 + step]
    sums[4] = total
    result.wait()
    for copy in sent:
        copy.wait_send()


def backward_pass(arrays, ids, params, up_sum, halo, own_rows, attn):
    f32, bf16 = jnp.float32, jnp.bfloat16
    hidden, cot = arrays[0], arrays[1]
    far_count = lax.axis_size("dp") // 4
    rows, width = cot.shape
    hid = hidden.shape[1]
    own_hid = hid // 2
    ext = rows + halo
    count = 8
    all_columns = 4 * attn + 2 * own_hid
    block = (far_count, own_rows, all_columns)
    dma = pltpu.SemaphoreType.DMA
    shape, vmem = jax.ShapeDtypeStruct, pltpu.VMEM
    any_spec, vmem_spec = pl.BlockSpec(memory_space=pl.ANY), pl.BlockSpec(memory_space=pltpu.VMEM)
    return pl.pallas_call(
        functools.partial(backward_kernel, far_count, halo),
        out_shape=[
            shape((rows, width), f32),
            shape((3, own_rows, attn), f32),
            shape((own_rows, attn), f32),
            shape((own_rows, own_hid), f32),
            shape((own_rows, own_hid), f32),
            shape((5, SMALL_ROWS, width), f32),
        ],
        in_specs=[any_spec] * 12 + [vmem_spec] * 3,
        out_specs=[any_spec] + [vmem_spec] * 5,
        scratch_shapes=[
            vmem((rows, hid), bf16),
            vmem((rows, width), f32),
            vmem((rows, width), bf16),
            vmem((rows, hid), bf16),
            vmem((width, hid), bf16),
            vmem((width, width), bf16),
            vmem((rows, width), f32),
            vmem((rows, width), bf16),
            vmem((ext, 3 * width), bf16),
            vmem((rows, width), bf16),
            vmem((width, rows), bf16),
            vmem((rows, width), bf16),
            vmem((rows, width), f32),
            vmem((rows, width), bf16),
            vmem((rows, 3 * width), bf16),
            vmem((width, hid), bf16),
            vmem((width, hid), bf16),
            vmem((width, width), bf16),
            vmem((width, 3 * width), bf16),
            vmem((halo, width), f32),
            vmem((halo, width), f32),
            vmem((halo, 2 * width), bf16),
            vmem((halo, 2 * width), bf16),
            vmem((1, halo + 2 * rows), jnp.int32),
            vmem((rows // halo, halo, 2 * halo), f32),
            vmem((SMALL_ROWS, width), f32),
            vmem((4,) + block, bf16),
            vmem(block, bf16),
            vmem(block, bf16),
            vmem(block, bf16),
            vmem(block, bf16),
            vmem((2 + far_count, SMALL_ROWS, width), f32),
            dma((13,)),
            dma((2,)),
            dma((2, 2 + far_count)),
            dma((2, count, 4, far_count)),
            dma((2, count, far_count)),
            dma((2, count, far_count)),
            dma((2, count, far_count)),
            dma((2, count, far_count)),
            dma((2, count, far_count)),
        ],
        compiler_params=pltpu.CompilerParams(
            collective_id=3, has_side_effects=True, vmem_limit_bytes=67043328
        ),
        name="backward_pass",
    )(*arrays, ids, params, up_sum)


def placed_small(vectors, qv_bias, up_bias, width):
    dp_size, tensor_size = lax.axis_size("dp"), lax.axis_size("tensor")
    dp, tensor = lax.axis_index("dp"), lax.axis_index("tensor")
    mine = lax.broadcasted_iota(jnp.int32, (dp_size * tensor_size, 1), 0) == dp * tensor_size + tensor
    stacked = jnp.stack(vectors)
    zero = jnp.zeros((), stacked.dtype)
    placed = jnp.where(mine[None], stacked[:, None, :], zero).reshape(len(vectors), width)
    my_dp = lax.broadcasted_iota(jnp.int32, (1, 1, 1, dp_size, 1), 3) == dp
    my_tensor = lax.broadcasted_iota(jnp.int32, (1, tensor_size, 1, 1, 1), 1) == tensor
    spot = my_dp & my_tensor
    qv = jnp.where(spot, qv_bias[:, None, :, None, :], zero).reshape(2, width)
    up = jnp.where(spot, up_bias[None, None, :, None, :], zero).reshape(-1, width)
    parts = jnp.concatenate([placed, qv, up])
    return jnp.pad(parts, ((0, SMALL_ROWS - parts.shape[0]), (0, 0)))


def on_device_small(
    inputs,
    seq_ids,
    norm1_gain,
    norm1_shift,
    qkv_weight,
    qv_bias,
    out_weight,
    out_bias,
    norm2_gain,
    norm2_shift,
    up_weight,
    up_bias,
    down_weight,
    down_bias,
    out_cotangent,
):
    f32, bf16 = jnp.float32, jnp.bfloat16
    dp_size, tensor_size = lax.axis_size("dp"), lax.axis_size("tensor")
    tensor = lax.axis_index("tensor")
    local_rows, width = inputs.shape
    halo = min(SEQ_MAX, local_rows)
    rows = up_weight.shape[0]
    attn = qkv_weight.shape[2]
    hid = up_weight.shape[1]
    vec = norm1_gain.shape[0]
    heads = qv_bias.shape[1]
    bias_cols = qv_bias.shape[2]
    up_rows, up_cols = up_bias.shape

    vectors = [norm1_gain, norm1_shift, out_bias, norm2_gain, norm2_shift, down_bias]
    vectors += [qv_bias.reshape(-1), up_bias.reshape(-1)]
    small_rows = len(vectors)
    small = jnp.stack([jnp.pad(vector, (0, LANES - vector.shape[0])) for vector in vectors])
    small = jnp.pad(small, ((0, rows - small_rows), (0, 0)))
    full_qkv, full_out, full_up, full_down, small_all, halo_rows = gather_weights(
        [qkv_weight, out_weight.T, up_weight, down_weight.T, small], inputs[local_rows - halo :]
    )
    full_qkv = full_qkv.reshape(width, -1)
    full_up = full_up.reshape(width, -1)
    full_down = full_down.reshape(width, -1)
    full_out = full_out.reshape(width, -1)
    small_all = small_all[:, :small_rows].reshape(dp_size, small_rows, tensor_size, LANES)
    gain_one, shift_one, bias_out, gain_two, shift_two, bias_down = (
        small_all[:, i, :, :vec].reshape(-1) for i in range(6)
    )
    qv_full = (
        small_all[:, 6, :, : qv_bias.size]
        .reshape(dp_size, tensor_size, 2, heads, bias_cols)
        .transpose(2, 1, 3, 0, 4)
        .reshape(2, tensor_size, attn)
    )
    up_bias_full = (
        small_all[:, 7, :, : up_bias.size]
        .reshape(dp_size, tensor_size, up_rows, up_cols)
        .transpose(1, 2, 0, 3)
        .reshape(-1)
    )
    qkv_bias = jnp.stack([qv_full[0], jnp.zeros_like(qv_full[0]), qv_full[1]], axis=1)
    qkv_bias = qkv_bias.reshape(-1).astype(f32)

    first_row = tensor * local_rows
    padded_ids = jnp.concatenate([jnp.full((halo,), -1, jnp.int32), seq_ids[0]])
    ext_ids = lax.dynamic_slice_in_dim(padded_ids, first_row, local_rows + halo)
    id_row, id_col = ext_ids[None, :], ext_ids[halo:, None]

    normed_one, inv_one, ln_one = norm_forward(inputs, gain_one, shift_one)
    ln_halo = norm_forward(halo_rows, gain_one, shift_one)[2]
    ln_ext = jnp.concatenate([ln_halo, ln_one])
    qkv = (jnp.dot(ln_ext, full_qkv, preferred_element_type=f32) + qkv_bias).astype(bf16)
    mixed = attend(qkv, id_row, id_col, halo, tensor_size)
    middle = inputs + times_transposed(mixed, full_out) + bias_out.astype(f32)
    normed_two, inv_two, ln_two = norm_forward(middle, gain_two, shift_two)
    pre_act = jnp.dot(ln_two, full_up, preferred_element_type=f32) + up_bias_full.astype(f32)
    hidden = gelu_forward(pre_act).astype(bf16)
    layer_out = middle + times_transposed(hidden, full_down) + bias_down.astype(f32)

    cot_bf = out_cotangent.astype(bf16)
    down_grad = contract_rows(cot_bf, hidden).astype(bf16)
    grad_pre = gelu_backward(pre_act, jnp.dot(cot_bf, full_down, preferred_element_type=f32))
    grad_pre_bf = grad_pre.astype(bf16)
    up_grad = contract_rows(ln_two, grad_pre_bf).astype(bf16)
    up_bias_grad = jnp.sum(grad_pre, axis=0)
    grad_ln_two = times_transposed(grad_pre_bf, full_up)
    gain_two_grad = jnp.sum(grad_ln_two * normed_two, axis=0)
    shift_two_grad = jnp.sum(grad_ln_two, axis=0)
    grad_middle = out_cotangent + norm_backward(grad_ln_two, normed_two, inv_two, gain_two)
    bias_down_grad = jnp.sum(out_cotangent, axis=0)
    bias_out_grad = jnp.sum(grad_middle, axis=0)
    mid_bf = grad_middle.astype(bf16)
    out_grad = contract_rows(mid_bf, mixed).astype(bf16)
    grad_mixed = jnp.dot(mid_bf, full_out, preferred_element_type=f32).astype(bf16)
    query_grad, key_ext, value_ext = attend_back(
        qkv, id_row, id_col, mixed, grad_mixed, halo, tensor_size
    )
    lent = jnp.concatenate([key_ext[:halo], value_ext[:halo]], axis=1).astype(bf16)
    ring = [((i + 1) % tensor_size, i) for i in range(tensor_size)]
    back = lax.ppermute(lent, "tensor", ring).astype(f32)
    rest = local_rows - halo

    def returned(ext, part):
        own = ext[halo:]
        return jnp.concatenate([own[:rest], own[rest:] + part])

    key_grad = returned(key_ext, back[:, :width])
    value_grad = returned(value_ext, back[:, width:])
    pieces = []
    for t in range(tensor_size):
        for piece in (query_grad, key_grad, value_grad):
            pieces.append(piece[:, t * attn : (t + 1) * attn].astype(bf16))
    grad_qkv = jnp.concatenate(pieces, axis=1)
    qkv_grad = contract_rows(ln_one, grad_qkv).astype(bf16)
    qv_grad = jnp.stack([jnp.sum(query_grad, axis=0), jnp.sum(value_grad, axis=0)])
    grad_ln_one = times_transposed(grad_qkv, full_qkv)
    gain_one_grad = jnp.sum(grad_ln_one * normed_one, axis=0)
    shift_one_grad = jnp.sum(grad_ln_one, axis=0)
    input_grad = grad_middle + norm_backward(grad_ln_one, normed_one, inv_one, gain_one)

    vectors = [gain_one_grad, shift_one_grad, bias_out_grad]
    vectors += [gain_two_grad, shift_two_grad, bias_down_grad]
    vectors = [vector.reshape(dp_size, tensor_size, vec) for vector in vectors] + [
        qv_grad.reshape(2, tensor_size, heads, dp_size, bias_cols)
        .transpose(3, 1, 0, 2, 4)
        .reshape(dp_size, tensor_size, -1),
        up_bias_grad.reshape(tensor_size, up_rows, dp_size, up_cols)
        .transpose(2, 0, 1, 3)
        .reshape(dp_size, tensor_size, -1),
    ]
    small_grad = jnp.stack(
        [jnp.pad(one.astype(bf16), ((0, 0), (0, 0), (0, LANES - one.shape[2]))) for one in vectors],
        axis=1,
    ).reshape(dp_size, small_rows, tensor_size * LANES)
    small_grad = jnp.pad(small_grad, ((0, 0), (0, rows - small_rows), (0, 0)))

    parts = [qkv_grad, out_grad, up_grad, down_grad, small_grad]
    own_qkv, own_out, own_up, own_down, own_small = scatter_grads(
        [part.reshape(dp_size, rows, -1) for part in parts],
        [(3, rows, attn), (rows, attn), (rows, hid), (rows, hid), (rows, LANES)],
    )
    vectors = [own_small[i, :vec] for i in range(6)]
    gain_one_own, shift_one_own, bias_out_own, gain_two_own, shift_two_own, bias_down_own = vectors
    return (
        layer_out,
        input_grad,
        gain_one_own,
        shift_one_own,
        own_qkv,
        own_small[6, : qv_bias.size].reshape(qv_bias.shape),
        own_out.T,
        bias_out_own,
        gain_two_own,
        shift_two_own,
        own_up,
        own_small[7, : up_bias.size].reshape(up_bias.shape),
        own_down.T,
        bias_down_own,
    )


def on_device(
    inputs,
    seq_ids,
    norm1_gain,
    norm1_shift,
    qkv_weight,
    qv_bias,
    out_weight,
    out_bias,
    norm2_gain,
    norm2_shift,
    up_weight,
    up_bias,
    down_weight,
    down_bias,
    out_cotangent,
):
    rows = up_weight.shape[0]
    if rows % 16:
        return on_device_small(
            inputs,
            seq_ids,
            norm1_gain,
            norm1_shift,
            qkv_weight,
            qv_bias,
            out_weight,
            out_bias,
            norm2_gain,
            norm2_shift,
            up_weight,
            up_bias,
            down_weight,
            down_bias,
            out_cotangent,
        )
    f32, bf16 = jnp.float32, jnp.bfloat16
    dp_size, tensor_size = lax.axis_size("dp"), lax.axis_size("tensor")
    tensor = lax.axis_index("tensor")
    local_rows, width = inputs.shape
    halo = min(SEQ_MAX, local_rows)
    attn = qkv_weight.shape[2]
    hid = up_weight.shape[1]
    vec = norm1_gain.shape[0]
    heads = qv_bias.shape[1]
    bias_cols = qv_bias.shape[2]
    up_rows, up_cols = up_bias.shape

    small = placed_small(
        [norm1_gain, norm1_shift, out_bias, norm2_gain, norm2_shift, down_bias],
        qv_bias,
        up_bias,
        width,
    )
    (
        full_qkv,
        full_out,
        full_up,
        ln_one,
        qkv,
        mixed,
        middle,
        ln_two,
        hidden,
        grad_pre_bf,
        layer_out,
        params,
        up_bias_grad,
    ) = forward_pass(
        qkv_weight,
        out_weight.T,
        up_weight,
        down_weight.T,
        small,
        inputs,
        out_cotangent,
        seq_ids,
        halo,
    )
    input_grad, own_qkv, own_out, own_up, own_down, sums = backward_pass(
        [
            hidden,
            out_cotangent,
            ln_two,
            grad_pre_bf,
            full_up,
            full_out,
            full_qkv,
            middle,
            inputs,
            mixed,
            qkv,
            ln_one,
        ],
        seq_ids,
        params,
        up_bias_grad,
        halo,
        rows,
        attn,
    )
    dp = lax.axis_index("dp")
    sums = sums[4]
    vectors = lax.dynamic_slice_in_dim(sums[:6], (dp * tensor_size + tensor) * vec, vec, axis=1)
    qv_sums = sums[Q_BIAS : V_BIAS + 1].reshape(2, tensor_size, heads, dp_size, bias_cols)
    qv_own = lax.dynamic_slice(
        qv_sums, (0, tensor, 0, dp, 0), (2, 1, heads, 1, bias_cols)
    ).reshape(qv_bias.shape)
    up_sums = sums[UP_BIAS : UP_BIAS + 4].reshape(tensor_size, up_rows, dp_size, up_cols)
    up_own = lax.dynamic_slice(up_sums, (tensor, 0, dp, 0), (1, up_rows, 1, up_cols)).reshape(
        up_bias.shape
    )
    return (
        layer_out,
        input_grad,
        vectors[0],
        vectors[1],
        own_qkv,
        qv_own,
        own_out.T,
        vectors[2],
        vectors[3],
        vectors[4],
        own_up,
        up_own,
        own_down.T,
        vectors[5],
    )


def solution(mesh):
    placed = (
        P(("dp", "tensor"), None),
        P("dp", None),
        P(("dp", "tensor")),
        P(("dp", "tensor")),
        P(None, "dp", "tensor"),
        P(None, "tensor", "dp"),
        P("tensor", "dp"),
        P(("dp", "tensor")),
        P(("dp", "tensor")),
        P(("dp", "tensor")),
        P("dp", "tensor"),
        P("tensor", "dp"),
        P("tensor", "dp"),
        P(("dp", "tensor")),
        P(("dp", "tensor"), None),
    )
    return jax.shard_map(
        on_device,
        mesh=mesh,
        in_specs=placed,
        out_specs=(
            P(("dp", "tensor"), None),
            P(("dp", "tensor"), None),
            P(("dp", "tensor")),
            P(("dp", "tensor")),
            P(None, "dp", "tensor"),
            P(None, "tensor", "dp"),
            P("tensor", "dp"),
            P(("dp", "tensor")),
            P(("dp", "tensor")),
            P(("dp", "tensor")),
            P("dp", "tensor"),
            P("tensor", "dp"),
            P("tensor", "dp"),
            P(("dp", "tensor")),
        ),
        check_vma=False,
    )
```

```python
import functools

import jax
import jax.numpy as jnp
from jax import lax
from jax.experimental import pallas as pl
from jax.experimental.pallas import tpu as pltpu
from jax.sharding import PartitionSpec as P

HD = 64
SEQ_MAX = 128
LANES = 128
VMEM_BYTES = 60 * 1024 * 1024

eps = 1e-05
scale_factor = 0.125
MESH = pl.DeviceIdType.MESH


def gelu_forward(pre_act):
    return jax.nn.gelu(pre_act, approximate=True)


def gelu_backward(pre_act, cotangent):
    return jax.vjp(gelu_forward, pre_act)[1](cotangent)[0]


def norm_forward(row_data, gain_vec, shift_vec):
    row_mean = jnp.mean(row_data, axis=-1, keepdims=True)
    centred = row_data - row_mean
    inv_std = lax.rsqrt(jnp.mean(centred * centred, axis=-1, keepdims=True) + eps)
    normed = centred * inv_std
    scaled = normed * gain_vec.astype(jnp.float32) + shift_vec.astype(jnp.float32)
    return (normed, inv_std, scaled.astype(jnp.bfloat16))


def norm_backward(grad_norm, normed, inv_std, gain_vec):
    scaled = grad_norm * gain_vec.astype(jnp.float32)
    first_mean = jnp.mean(scaled, axis=-1, keepdims=True)
    second_mean = jnp.mean(scaled * normed, axis=-1, keepdims=True)
    return inv_std * (scaled - first_mean - normed * second_mean)


def contract_rows(left_mat, right_mat):
    return lax.dot_general(
        left_mat, right_mat, (((0,), (0,)), ((), ())), preferred_element_type=jnp.float32
    )


def times_transposed(left_mat, right_mat):
    return lax.dot_general(
        left_mat, right_mat, (((1,), (1,)), ((), ())), preferred_element_type=jnp.float32
    )


class Place:
    def __init__(self, far_count):
        index = lax.axis_index("dp")
        self.far_count = far_count
        self.tensor = lax.axis_index("tensor")
        self.core = lax.rem(index, 2)
        self.near = lax.rem(index // 2, 2)
        self.far = index // 4

    def index(self, far, near, core):
        return (far * 2 + near) * 2 + core

    def far_at(self, step):
        return lax.rem(self.far + step + self.far_count, self.far_count)

    def peer(self, kind, step=0):
        far, near, core, tensor = self.far, self.near, self.core, self.tensor
        if kind == "far":
            far = self.far_at(step)
        if kind == "near":
            near = 1 - near
        if kind == "core":
            core = 1 - core
        if kind == "tensor":
            tensor = 1 - tensor
        return {"dp": self.index(far, near, core), "tensor": tensor}

    def greet(self):
        barrier = pltpu.get_barrier_semaphore()
        peers = [self.peer("far", step) for step in range(1, self.far_count)]
        peers += [self.peer("near"), self.peer("core"), self.peer("tensor")]
        for peer in peers:
            pl.semaphore_signal(barrier, inc=1, device_id=peer, device_id_type=MESH)
        pl.semaphore_wait(barrier, len(peers))


def columns_at(tensor, width, start=0, size=None):
    return pl.ds(pl.multiple_of(tensor * width + start, LANES), width if size is None else size)


def gather_kernel(far_count, array_count, pieces, *refs):
    group_count = len(pieces)
    own_arrays = refs[:array_count]
    tail_ref = refs[array_count]
    full_refs = refs[array_count + 1 : 2 * array_count + 1]
    halo_ref = refs[2 * array_count + 1]
    local_sem, tail_sem, far_sem, x_sem, y_sem, diag_sem, core_sem = refs[2 * array_count + 2 :]
    own_refs = []
    for array, lead, first, _, size in pieces:
        own = own_arrays[array]
        own_refs.append(own.at[:, pl.ds(first, size)] if lead is None else own.at[lead])
    at = Place(far_count)
    at.greet()
    sent, arrivals = [], []

    def slot(group, tensor, far, near, core):
        array, _, _, start, size = pieces[group]
        block_width = full_refs[array].shape[2] // 2
        columns = columns_at(tensor, block_width, start, size)
        return full_refs[array].at[at.index(far, near, core), :, columns]

    def send(source, target, sems, place, peer):
        copy = pltpu.make_async_remote_copy(
            src_ref=source,
            dst_ref=target,
            send_sem=sems.at[(0,) + place],
            recv_sem=sems.at[(1,) + place],
            device_id=peer,
            device_id_type=MESH,
        )
        copy.start()
        sent.append(copy)

    def arrived(target, sems, place, peer):
        pltpu.make_async_remote_copy(
            src_ref=target,
            dst_ref=target,
            send_sem=sems.at[(0,) + place],
            recv_sem=sems.at[(1,) + place],
            device_id=peer,
            device_id_type=MESH,
        ).wait_recv()

    groups = range(group_count)
    x_first, loads = [], [0, 0]
    for piece in pieces:
        x_first.append(loads[0] <= loads[1])
        loads[0 if x_first[-1] else 1] += piece[4]
    x_peer, y_peer, core_peer = at.peer("tensor"), at.peer("near"), at.peer("core")
    local = []
    for group in groups:
        own_slot = slot(group, at.tensor, at.far, at.near, at.core)
        for step in range(1, far_count):
            send(own_refs[group], own_slot, far_sem, (group, step), at.peer("far", step))
        send(own_refs[group], own_slot, x_sem, (group, 0), x_peer)
        send(own_refs[group], own_slot, y_sem, (group, 0), y_peer)
        send(own_refs[group], own_slot, core_sem, (group, 0, 0), core_peer)
        if group == 0:
            copy = pltpu.make_async_remote_copy(
                src_ref=tail_ref,
                dst_ref=halo_ref,
                send_sem=tail_sem.at[0],
                recv_sem=tail_sem.at[1],
                device_id=x_peer,
                device_id_type=MESH,
            )
            copy.start()
            tail_copy = copy
        keep = pltpu.make_async_copy(own_refs[group], own_slot, local_sem.at[group])
        keep.start()
        local.append(keep)

    def spread(group, step):
        far = at.far_at(-step)
        here = slot(group, at.tensor, far, at.near, at.core)
        arrived(here, far_sem, (group, step), x_peer)
        send(here, here, x_sem, (group, step), x_peer)
        send(here, here, y_sem, (group, step), y_peer)
        send(here, here, core_sem, (group, 0, step), core_peer)

    def relay(group, step):
        far = at.far_at(-step)
        from_x = slot(group, 1 - at.tensor, far, at.near, at.core)
        arrived(from_x, x_sem, (group, step), x_peer)
        if x_first[group]:
            send(from_x, from_x, diag_sem, (group, step), y_peer)
        send(from_x, from_x, core_sem, (group, 1, step), core_peer)
        from_y = slot(group, at.tensor, far, 1 - at.near, at.core)
        arrived(from_y, y_sem, (group, step), y_peer)
        if not x_first[group]:
            send(from_y, from_y, diag_sem, (group, step), x_peer)
        send(from_y, from_y, core_sem, (group, 2, step), core_peer)

    def corner(group, step):
        far = at.far_at(-step)
        diag = slot(group, 1 - at.tensor, far, 1 - at.near, at.core)
        arrived(diag, diag_sem, (group, step), y_peer if x_first[group] else x_peer)
        send(diag, diag, core_sem, (group, 3, step), core_peer)

    for group in groups:
        relay(group, 0)
        for step in range(1, far_count):
            spread(group, step)
            if group:
                corner(group - 1, step - 1)
        if group:
            corner(group - 1, far_count - 1)
        for step in range(1, far_count):
            relay(group, step)
    for step in range(far_count):
        corner(group_count - 1, step)
    for group in groups:
        for step in range(far_count):
            far = at.far_at(-step)
            for kind, (flip_x, flip_y) in enumerate(((0, 0), (1, 0), (0, 1), (1, 1))):
                tensor = 1 - at.tensor if flip_x else at.tensor
                near = 1 - at.near if flip_y else at.near
                arrived(
                    slot(group, tensor, far, near, 1 - at.core),
                    core_sem,
                    (group, kind, step),
                    core_peer,
                )
    for copy in sent:
        copy.wait_send()
    tail_copy.wait()
    for keep in local:
        keep.wait()


def gather_weights(own_blocks, tail):
    dp_size, tensor_size = lax.axis_size("dp"), lax.axis_size("tensor")
    far_count = dp_size // 4
    array_count = len(own_blocks)
    shapes, pieces = [], []
    for array, own in enumerate(own_blocks):
        size = own.shape[-1]
        lead_count = own.shape[0] if own.ndim == 3 else 1
        block_width = lead_count * size
        shapes.append(
            jax.ShapeDtypeStruct((dp_size, own.shape[-2], tensor_size * block_width), own.dtype)
        )
        if own.ndim == 3:
            pieces += [(array, lead, 0, lead * size, size) for lead in range(lead_count)]
        elif size < 8 * LANES:
            pieces.append((array, None, 0, 0, size))
        else:
            cut = size // 2
            pieces += [(array, None, first, first, cut) for first in (0, cut)]
    shapes.append(jax.ShapeDtypeStruct(tail.shape, tail.dtype))
    count = len(pieces)
    dma = pltpu.SemaphoreType.DMA
    return pl.pallas_call(
        functools.partial(gather_kernel, far_count, array_count, tuple(pieces)),
        out_shape=shapes,
        in_specs=[pl.BlockSpec(memory_space=pltpu.VMEM)] * (array_count + 1),
        out_specs=[pl.BlockSpec(memory_space=pl.ANY)] * (array_count + 1),
        scratch_shapes=[
            dma((count,)),
            dma((2,)),
            dma((2, count, far_count)),
            dma((2, count, far_count)),
            dma((2, count, far_count)),
            dma((2, count, far_count)),
            dma((2, count, 4, far_count)),
        ],
        compiler_params=pltpu.CompilerParams(
            collective_id=0, has_side_effects=True, vmem_limit_bytes=VMEM_BYTES
        ),
        name="gather_weights",
    )(*own_blocks, tail)


def scatter_kernel(far_count, group_count, *refs):
    part_refs = refs[:group_count]
    out_refs = refs[group_count : 2 * group_count]
    (
        result,
        total,
        core_in,
        x_in,
        y_in,
        diag_in,
        far_in,
        core_sem,
        x_sem,
        y_sem,
        diag_x_sem,
        diag_y_sem,
        far_sem,
    ) = refs[2 * group_count :]
    at = Place(far_count)
    at.greet()
    sent = []
    tensor_size = 2
    widths = [ref.shape[2] // tensor_size for ref in part_refs]
    offsets = [sum(widths[:group]) for group in range(group_count)]
    all_columns = sum(widths)
    half = all_columns // 2 // LANES * LANES
    low, high = pl.ds(0, half), pl.ds(half, all_columns - half)
    x_peer, y_peer, core_peer = at.peer("tensor"), at.peer("near"), at.peer("core")
    order = list(range(1, far_count)) + [0]
    own, by_x, by_y, diag = range(4)
    flips = ((0, 0), (1, 0), (0, 1), (1, 1))

    def make(source, target, sems, place, peer):
        return pltpu.make_async_remote_copy(
            src_ref=source,
            dst_ref=target,
            send_sem=sems.at[(0,) + place],
            recv_sem=sems.at[(1,) + place],
            device_id=peer,
            device_id_type=MESH,
        )

    def send(*args):
        copy = make(*args)
        copy.start()
        sent.append(copy)

    def slot(group, kind, step, core):
        flip_x, flip_y = flips[kind]
        tensor = 1 - at.tensor if flip_x else at.tensor
        near = 1 - at.near if flip_y else at.near
        index = at.index(at.far_at(step), near, core)
        return part_refs[group].at[index, :, columns_at(tensor, widths[group])]

    def core_slot(group, kind, step):
        return core_in.at[kind, step, :, pl.ds(offsets[group], widths[group])]

    kinds = (diag, by_x, by_y, own)
    for step in order:
        for kind in kinds:
            for group in range(group_count):
                send(
                    slot(group, kind, step, 1 - at.core),
                    core_slot(group, kind, step),
                    core_sem,
                    (group, kind, step),
                    core_peer,
                )

    def meet(kind, step):
        for group in range(group_count):
            target = core_slot(group, kind, step)
            make(target, target, core_sem, (group, kind, step), core_peer).wait_recv()
            columns = pl.ds(offsets[group], widths[group])
            mine = slot(group, kind, step, at.core)
            total[kind, step, :, columns] = (
                mine[...].astype(jnp.float32) + target[...].astype(jnp.float32)
            ).astype(jnp.bfloat16)

    def add_to(kind, step, columns, source):
        total[kind, step, :, columns] = (
            total[kind, step, :, columns].astype(jnp.float32) + source[...].astype(jnp.float32)
        ).astype(jnp.bfloat16)

    for step in order:
        meet(diag, step)
        corner = total.at[diag, step]
        send(corner.at[:, low], diag_in.at[step, :, low], diag_y_sem, (step,), y_peer)
        send(corner.at[:, high], diag_in.at[step, :, high], diag_x_sem, (step,), x_peer)
        meet(by_x, step)
        meet(by_y, step)
        meet(own, step)

    for step in order:
        from_y = diag_in.at[step, :, low]
        make(from_y, from_y, diag_y_sem, (step,), y_peer).wait_recv()
        add_to(by_x, step, low, from_y)
        send(total.at[by_x, step], x_in.at[step], x_sem, (step,), x_peer)
        from_x = diag_in.at[step, :, high]
        make(from_x, from_x, diag_x_sem, (step,), x_peer).wait_recv()
        add_to(by_y, step, high, from_x)
        send(total.at[by_y, step], y_in.at[step], y_sem, (step,), y_peer)

    for step in order:
        make(x_in.at[step], x_in.at[step], x_sem, (step,), x_peer).wait_recv()
        make(y_in.at[step], y_in.at[step], y_sem, (step,), y_peer).wait_recv()
        merged = (
            total[own, step].astype(jnp.float32)
            + x_in[step].astype(jnp.float32)
            + y_in[step].astype(jnp.float32)
        )
        if step:
            total[own, step] = merged.astype(jnp.bfloat16)
            send(total.at[own, step], far_in.at[step], far_sem, (step,), at.peer("far", step))
        else:
            result[...] = merged
    for step in range(1, far_count):
        make(far_in.at[step], far_in.at[step], far_sem, (step,), at.peer("far", step)).wait_recv()
        if step < far_count - 1:
            result[...] += far_in[step].astype(jnp.float32)
    for group in range(group_count):
        out_ref = out_refs[group]
        width = out_ref.shape[-1]
        for lead in range(widths[group] // width):
            columns = pl.ds(offsets[group] + lead * width, width)
            held = result[:, columns]
            if far_count > 1:
                held += far_in[far_count - 1, :, columns].astype(jnp.float32)
            if len(out_ref.shape) == 3:
                out_ref[lead] = held
            else:
                out_ref[...] = held
    for copy in sent:
        copy.wait_send()


def scatter_grads(parts, out_shapes):
    dp_size, tensor_size = lax.axis_size("dp"), lax.axis_size("tensor")
    far_count = dp_size // 4
    count = len(parts)
    rows = parts[0].shape[1]
    all_columns = sum(part.shape[2] for part in parts) // tensor_size
    dma = pltpu.SemaphoreType.DMA
    block = (rows, all_columns)
    return pl.pallas_call(
        functools.partial(scatter_kernel, far_count, count),
        out_shape=[jax.ShapeDtypeStruct(shape, jnp.float32) for shape in out_shapes],
        in_specs=[pl.BlockSpec(memory_space=pltpu.VMEM)] * count,
        out_specs=[pl.BlockSpec(memory_space=pltpu.VMEM)] * count,
        scratch_shapes=[
            pltpu.VMEM(block, jnp.float32),
            pltpu.VMEM((4, far_count) + block, jnp.bfloat16),
            pltpu.VMEM((4, far_count) + block, jnp.bfloat16),
            pltpu.VMEM((far_count,) + block, jnp.bfloat16),
            pltpu.VMEM((far_count,) + block, jnp.bfloat16),
            pltpu.VMEM((far_count,) + block, jnp.bfloat16),
            pltpu.VMEM((far_count,) + block, jnp.bfloat16),
            dma((2, count, 4, far_count)),
            dma((2, far_count)),
            dma((2, far_count)),
            dma((2, far_count)),
            dma((2, far_count)),
            dma((2, far_count)),
        ],
        compiler_params=pltpu.CompilerParams(
            collective_id=1, has_side_effects=True, vmem_limit_bytes=VMEM_BYTES
        ),
        name="scatter_grads",
    )(*parts)


def head_blocks(q_ref, k_ref, v_ref, id_row, id_col, halo):
    query_rows = id_col.shape[0]
    lane = lax.broadcasted_iota(jnp.int32, (halo, LANES), 1)
    window = 2 * halo
    row = lax.broadcasted_iota(jnp.int32, (halo, window), 0)
    column = lax.broadcasted_iota(jnp.int32, (halo, window), 1)
    causal = column <= row + halo
    for block in range(query_rows // halo):
        first = block * halo
        query = q_ref[first + halo : first + 2 * halo, :]
        keys = k_ref[first : first + window, :]
        values = v_ref[first : first + window, :]
        same = id_col[first : first + halo, :] == id_row[:, first : first + window]
        allowed = causal & same
        for head in range(LANES // HD):
            mine = (lane >= head * HD) & (lane < (head + 1) * HD)
            query_head = jnp.where(mine, query, jnp.zeros_like(query))
            scores = times_transposed(query_head, keys) * scale_factor
            weight = jnp.where(allowed, jnp.exp(scores), 0.0)
            probs = weight / jnp.sum(weight, axis=-1, keepdims=True)
            yield first, head, mine, query_head, keys, values, probs


def attend_kernel(halo, q_ref, k_ref, v_ref, id_row, id_col, mixed_ref):
    held = None
    for first, head, mine, _, _, values, probs in head_blocks(
        q_ref, k_ref, v_ref, id_row, id_col, halo
    ):
        part = jnp.dot(probs.astype(jnp.bfloat16), values, preferred_element_type=jnp.float32)
        held = part if head == 0 else jnp.where(mine, part, held)
        if head == LANES // HD - 1:
            mixed_ref[first : first + halo, :] = held.astype(jnp.bfloat16)


def attend_back_kernel(
    halo, q_ref, k_ref, v_ref, id_row, id_col, mixed_ref, grad_ref, dq_ref, dk_ref, dv_ref
):
    dk_ref[...] = jnp.zeros_like(dk_ref)
    dv_ref[...] = jnp.zeros_like(dv_ref)
    for first, head, mine, query_head, keys, values, probs in head_blocks(
        q_ref, k_ref, v_ref, id_row, id_col, halo
    ):
        window = keys.shape[0]
        grad = grad_ref[first : first + halo, :]
        grad_head = jnp.where(mine, grad, jnp.zeros_like(grad))
        mixed = mixed_ref[first : first + halo, :]
        delta = jnp.sum(
            grad_head.astype(jnp.float32) * mixed.astype(jnp.float32), axis=-1, keepdims=True
        )
        grad_probs = times_transposed(grad_head, values)
        grad_scores = (probs * (grad_probs - delta) * scale_factor).astype(jnp.bfloat16)
        dv_ref[first : first + window, :] += contract_rows(probs.astype(jnp.bfloat16), grad_head)
        dk_ref[first : first + window, :] += contract_rows(grad_scores, query_head)
        part = jnp.dot(grad_scores, keys, preferred_element_type=jnp.float32)
        if head == 0:
            dq_ref[first : first + halo, :] = part
        else:
            dq_ref[first : first + halo, :] = jnp.where(
                mine, part, dq_ref[first : first + halo, :]
            )


def attend_specs(qkv, halo, tensor_size):
    ext_rows = qkv.shape[0]
    pairs = qkv.shape[1] // 3 // tensor_size // LANES

    def part_of(which):
        return pl.BlockSpec(
            (ext_rows, LANES), lambda pair: (0, pair // pairs * 3 * pairs + which * pairs + pair % pairs)
        )

    ids = [
        pl.BlockSpec((1, ext_rows), lambda pair: (0, 0)),
        pl.BlockSpec((ext_rows - halo, 1), lambda pair: (0, 0)),
    ]
    return pairs * tensor_size, [part_of(0), part_of(1), part_of(2)] + ids


def attend(qkv, id_row, id_col, halo, tensor_size):
    steps, specs = attend_specs(qkv, halo, tensor_size)
    rows = qkv.shape[0] - halo
    return pl.pallas_call(
        functools.partial(attend_kernel, halo),
        grid=(steps,),
        in_specs=specs,
        out_specs=pl.BlockSpec((rows, LANES), lambda pair: (0, pair)),
        out_shape=jax.ShapeDtypeStruct((rows, steps * LANES), jnp.bfloat16),
        name="attend",
    )(qkv, qkv, qkv, id_row, id_col)


def attend_back(qkv, id_row, id_col, mixed, grad_mixed, halo, tensor_size):
    steps, specs = attend_specs(qkv, halo, tensor_size)
    ext_rows = qkv.shape[0]
    rows = ext_rows - halo
    short = pl.BlockSpec((rows, LANES), lambda pair: (0, pair))
    tall = pl.BlockSpec((ext_rows, LANES), lambda pair: (0, pair))
    width = steps * LANES
    return pl.pallas_call(
        functools.partial(attend_back_kernel, halo),
        grid=(steps,),
        in_specs=specs + [short, short],
        out_specs=[short, tall, tall],
        out_shape=[
            jax.ShapeDtypeStruct((rows, width), jnp.float32),
            jax.ShapeDtypeStruct((ext_rows, width), jnp.float32),
            jax.ShapeDtypeStruct((ext_rows, width), jnp.float32),
        ],
        name="attend_back",
    )(qkv, qkv, qkv, id_row, id_col, mixed, grad_mixed)


GELU_C = 0.7978845608028654
GELU_A = 0.044715
ROWS_AT = {"gain_one": 0, "shift_one": 1, "out_bias": 2, "gain_two": 3, "shift_two": 4, "down_bias": 5}
Q_BIAS, V_BIAS, UP_BIAS = 6, 7, 8
SMALL_ROWS = 16
TILE = 256


def loop(count, body):
    lax.fori_loop(0, count, lambda i, carry: (body(i), carry)[1], 0)


def lanes(start, size=TILE):
    return pl.ds(pl.multiple_of(start, LANES), size)


def forward_kernel(far_count, halo, *refs):
    (
        own_qkv,
        own_out,
        own_up,
        own_down,
        own_small,
        x_hbm,
        cot_hbm,
        ids_ref,
        qkv_w_out,
        out_w_out,
        up_w_out,
        ln1_out,
        qkv_out,
        mixed_out,
        middle_out,
        ln2_out,
        hidden_out,
        grad_pre_out,
        layer_out,
        params,
        up_grad,
        w_qkv,
        w_out,
        w_up,
        w_down,
        small_all,
        x_ref,
        cot_ref,
        cot_bf,
        ln1,
        qkv,
        mixed,
        middle,
        total,
        ln2,
        hidden,
        slope,
        grad_pre,
        id_ref,
        mask_ref,
        load_sem,
        out_sem,
        local_sem,
        tail_sem,
        far_sem,
        x_sem,
        y_sem,
        diag_sem,
        core_sem,
    ) = refs
    f32, bf16 = jnp.float32, jnp.bfloat16
    rows, width = x_ref.shape
    own_rows = own_out.shape[0]
    attn = own_out.shape[1]
    hid = own_up.shape[1]
    cut = hid // 2
    at = Place(far_count)
    at.greet()
    sent, keeps = [], {}
    x_load = pltpu.make_async_copy(x_hbm, x_ref, load_sem.at[0])
    cot_load = pltpu.make_async_copy(cot_hbm, cot_ref, load_sem.at[1])
    x_load.start()
    cot_load.start()

    def block_of(full, width_of, start, size):
        def place(index, tensor):
            row = pl.multiple_of(index * own_rows, 16)
            return full.at[pl.ds(row, own_rows), lanes(tensor * width_of + start, size)]

        return place

    groups = [(own_small, lambda index, tensor: small_all.at[index * 2 + tensor], 0)]
    for lead in range(3):
        def place(index, tensor, lead=lead):
            row = pl.multiple_of(index * own_rows, 16)
            return w_qkv.at[pl.ds(row, own_rows), lanes(lead * width + tensor * attn, attn)]

        groups.append((own_qkv.at[lead], place, attn))
    groups.append((own_out, block_of(w_out, attn, 0, attn), attn))
    for half in range(2):
        columns = pl.ds(half * cut, cut)
        groups.append((own_up.at[:, columns], block_of(w_up, hid, half * cut, cut), cut))
        groups.append((own_down.at[:, columns], block_of(w_down, hid, half * cut, cut), cut))
    count = len(groups)
    x_first, loads = [], [attn, 0]
    for _, _, size in groups:
        x_first.append(loads[0] >= loads[1])
        loads[1 if x_first[-1] else 0] += size

    def slot(group, tensor, far, near, core):
        return groups[group][1](at.index(far, near, core), tensor)

    def remote(source, target, sems, place, peer):
        return pltpu.make_async_remote_copy(
            src_ref=source,
            dst_ref=target,
            send_sem=sems.at[(0,) + place],
            recv_sem=sems.at[(1,) + place],
            device_id=peer,
            device_id_type=MESH,
        )

    def send(*args):
        copy = remote(*args)
        copy.start()
        sent.append(copy)

    def arrived(target, sems, place, peer):
        remote(target, target, sems, place, peer).wait_recv()

    x_peer, y_peer, core_peer = at.peer("tensor"), at.peer("near"), at.peer("core")

    def own(group):
        source = groups[group][0]
        target = slot(group, at.tensor, at.far, at.near, at.core)
        for step in range(1, far_count):
            send(source, target, far_sem, (group, step), at.peer("far", step))
        send(source, target, x_sem, (group, 0), x_peer)
        send(source, target, y_sem, (group, 0), y_peer)
        send(source, target, core_sem, (group, 0, 0), core_peer)
        keep = pltpu.make_async_copy(source, target, local_sem.at[group])
        keep.start()
        keeps[group] = keep

    def spread(group, step):
        here = slot(group, at.tensor, at.far_at(-step), at.near, at.core)
        arrived(here, far_sem, (group, step), x_peer)
        send(here, here, x_sem, (group, step), x_peer)
        send(here, here, y_sem, (group, step), y_peer)
        send(here, here, core_sem, (group, 0, step), core_peer)

    def relay(group, step):
        far = at.far_at(-step)
        from_x = slot(group, 1 - at.tensor, far, at.near, at.core)
        arrived(from_x, x_sem, (group, step), x_peer)
        if x_first[group]:
            send(from_x, from_x, diag_sem, (group, step), y_peer)
        send(from_x, from_x, core_sem, (group, 1, step), core_peer)
        from_y = slot(group, at.tensor, far, 1 - at.near, at.core)
        arrived(from_y, y_sem, (group, step), y_peer)
        if not x_first[group]:
            send(from_y, from_y, diag_sem, (group, step), x_peer)
        send(from_y, from_y, core_sem, (group, 2, step), core_peer)

    def corner(group, step):
        diag = slot(group, 1 - at.tensor, at.far_at(-step), 1 - at.near, at.core)
        arrived(diag, diag_sem, (group, step), y_peer if x_first[group] else x_peer)
        send(diag, diag, core_sem, (group, 3, step), core_peer)

    def finish(group):
        for step in range(far_count):
            far = at.far_at(-step)
            for kind, (flip_x, flip_y) in enumerate(((0, 0), (1, 0), (0, 1), (1, 1))):
                tensor = 1 - at.tensor if flip_x else at.tensor
                near = 1 - at.near if flip_y else at.near
                place = slot(group, tensor, far, near, 1 - at.core)
                arrived(place, core_sem, (group, kind, step), core_peer)
        keeps[group].wait()

    stores = []

    def store(source, target):
        copy = pltpu.make_async_copy(source, target, out_sem.at[len(stores)])
        copy.start()
        stores.append(copy)

    def vector(row, columns=slice(None)):
        return params[row : row + 1, columns]

    def norm_rows(source, target, first, size, shift, gain_row, shift_row):
        data = source[pl.ds(first, size), :]
        row_mean = jnp.mean(data, axis=-1, keepdims=True)
        centred = data - row_mean
        inv_std = lax.rsqrt(jnp.mean(centred * centred, axis=-1, keepdims=True) + eps)
        scaled = centred * inv_std * vector(gain_row) + vector(shift_row)
        target[pl.ds(first + shift, size), :] = scaled.astype(bf16)

    def first_norm():
        held = small_all[0].astype(f32)
        for device in range(1, small_all.shape[0]):
            held = held + small_all[device].astype(f32)
        params[...] = held
        x_load.wait()
        norm_rows(x_ref, ln1, rows - halo, halo, halo, 0, 1)
        send(ln1.at[pl.ds(rows, halo)], ln1.at[pl.ds(0, halo)], tail_sem, (), x_peer)

        def one(i):
            norm_rows(x_ref, ln1, pl.multiple_of(i * halo, halo), halo, halo, 0, 1)

        loop(rows // halo - 1, one)

    def masks():
        id_ref[:, :halo] = jnp.full((1, halo), -1, jnp.int32)
        id_ref[:, halo:] = ids_ref[...]
        window = 2 * halo
        row = lax.broadcasted_iota(jnp.int32, (halo, window), 0)
        column = lax.broadcasted_iota(jnp.int32, (halo, window), 1)
        causal = column <= row + halo
        for block in range(rows // halo):
            first = at.tensor * rows + block * halo
            keys = id_ref[:, lanes(first, window)]
            queries = jnp.broadcast_to(id_ref[:, lanes(first + halo, halo)], (halo, halo)).T
            same = jnp.concatenate([queries, queries], axis=1) == keys
            mask_ref[block] = jnp.where(same & causal, 1.0, 0.0)
        cot_load.wait()

        def one(i):
            part = pl.ds(pl.multiple_of(i * halo, halo), halo)
            cot_bf[part, :] = cot_ref[part, :].astype(bf16)

        loop(rows // halo, one)

    def project(lead, bias_row, first):
        def one(i):
            columns = lanes(lead * width + i * TILE)
            part = jnp.dot(ln1[first:, :], w_qkv[:, columns], preferred_element_type=f32)
            if bias_row is not None:
                part = part + params[bias_row : bias_row + 1, lanes(i * TILE)]
            qkv[first:, columns] = part.astype(bf16)

        loop(width // TILE, one)

    def attention(first_pair, pair_count):
        lane = lax.broadcasted_iota(jnp.int32, (halo, LANES), 1)

        def one(i):
            pair = first_pair + i
            q_at, k_at = lanes(pair * LANES, LANES), lanes(width + pair * LANES, LANES)
            v_at = lanes(2 * width + pair * LANES, LANES)
            for block in range(rows // halo):
                first = block * halo
                query = qkv[first + halo : first + 2 * halo, q_at]
                keys = qkv[first : first + 2 * halo, k_at]
                values = qkv[first : first + 2 * halo, v_at]
                allowed = mask_ref[block] > 0.5
                held = None
                for head in range(LANES // HD):
                    mine = (lane >= head * HD) & (lane < (head + 1) * HD)
                    query_head = jnp.where(mine, query, jnp.zeros_like(query))
                    scores = times_transposed(query_head, keys) * scale_factor
                    weight = jnp.where(allowed, jnp.exp(scores), 0.0)
                    probs = weight / jnp.sum(weight, axis=-1, keepdims=True)
                    part = jnp.dot(probs.astype(bf16), values, preferred_element_type=f32)
                    held = part if head == 0 else jnp.where(mine, part, held)
                mixed[first : first + halo, q_at] = held.astype(bf16)

        loop(pair_count, one)

    def project_out():
        def one(i):
            columns = lanes(i * TILE)
            out_rows = pl.ds(pl.multiple_of(i * TILE, TILE), TILE)
            part = x_ref[:, columns] + times_transposed(mixed[...], w_out[out_rows, :])
            part = part + params[2:3, columns]
            middle[:, columns] = part
            total[:, columns] = part + params[5:6, columns]

        loop(width // TILE, one)

    def second_norm():
        def one(i):
            norm_rows(middle, ln2, pl.multiple_of(i * halo, halo), halo, 0, 3, 4)

        loop(rows // halo, one)

    def go_up(half, tensor):
        base = tensor * hid + half * cut

        def one(i):
            columns = lanes(base + i * TILE)
            bias_row = UP_BIAS + base // width
            bias = params[bias_row : bias_row + 1, lanes(base % width + i * TILE)]
            u = jnp.dot(ln2[...], w_up[:, columns], preferred_element_type=f32) + bias
            square = u * u
            bent = jnp.tanh(GELU_C * (u + GELU_A * (u * square)))
            half_sum = 0.5 + 0.5 * bent
            hidden[:, columns] = (u * half_sum).astype(bf16)
            turn = (0.5 * GELU_C) * (1.0 + (3.0 * GELU_A) * square)
            slope[:, columns] = half_sum + u * (1.0 - bent * bent) * turn

        loop(cut // TILE, one)

    def go_down(half, tensor):
        base = tensor * hid + half * cut

        def one(i):
            columns = lanes(i * TILE)
            out_rows = pl.ds(pl.multiple_of(i * TILE, TILE), TILE)
            total[:, columns] += times_transposed(
                hidden[:, base : base + cut], w_down[out_rows, base : base + cut]
            )

        loop(width // TILE, one)

    def go_back(half, tensor):
        base = tensor * hid + half * cut

        def one(i):
            columns = lanes(base + i * TILE)
            part = jnp.dot(cot_bf[...], w_down[:, columns], preferred_element_type=f32)
            part = part * slope[:, columns]
            grad_pre[:, columns] = part.astype(bf16)
            up_grad[:, columns] = jnp.sum(part, axis=0, keepdims=True)

        loop(cut // TILE, one)

    def halo_here():
        tail = ln1.at[pl.ds(0, halo)]
        remote(tail, tail, tail_sem, (), x_peer).wait_recv()
        store(ln1.at[pl.ds(halo, rows)], ln1_out)

    pairs = width // LANES
    step_pairs = pairs // 3 if pairs % 3 == 0 else pairs
    work = {
        0: [first_norm, masks],
        1: [lambda: project(0, Q_BIAS, halo)],
        2: [lambda: (halo_here(), project(1, None, 0))],
        3: [lambda: (project(2, V_BIAS, 0), store(w_qkv, qkv_w_out), store(qkv, qkv_out))]
        + [
            functools.partial(attention, first, step_pairs)
            for first in range(0, pairs, step_pairs)
        ],
        4: [
            lambda: (project_out(), store(w_out, out_w_out), store(mixed, mixed_out)),
            lambda: (second_norm(), store(middle, middle_out), store(ln2, ln2_out)),
        ],
    }
    for half in range(2):
        work[5 + 2 * half] = [functools.partial(go_up, half, tensor) for tensor in range(2)]
        work[6 + 2 * half] = [functools.partial(go_down, half, tensor) for tensor in range(2)]
        work[6 + 2 * half] += [functools.partial(go_back, half, tensor) for tensor in range(2)]
    work[7].append(lambda: (store(w_up, up_w_out), store(hidden, hidden_out)))
    queue = []

    def tick():
        if queue:
            queue.pop(0)()

    ahead = 5
    for group in range(min(ahead, count)):
        own(group)
    for step in range(1, far_count):
        spread(0, step)
    for group in range(count):
        if group + ahead < count:
            own(group + ahead)
        if group + 1 < count:
            for step in range(1, far_count):
                spread(group + 1, step)
        tick()
        for step in range(far_count):
            relay(group, step)
            if step % 2:
                tick()
        if group:
            for step in range(far_count):
                corner(group - 1, step)
            finish(group - 1)
            queue += work[group - 1]
            tick()
    for step in range(far_count):
        corner(count - 1, step)
    while queue:
        tick()
    finish(count - 1)
    queue += work[count - 1]
    while queue:
        tick()
    store(total, layer_out)
    store(grad_pre, grad_pre_out)
    for copy in sent:
        copy.wait_send()
    for copy in stores:
        copy.wait()


def forward_pass(own_qkv, own_out, own_up, own_down, own_small, inputs, cot, ids, halo):
    f32, bf16 = jnp.float32, jnp.bfloat16
    dp_size = lax.axis_size("dp")
    far_count = dp_size // 4
    rows, width = inputs.shape
    hid = 2 * own_up.shape[1]
    ext = rows + halo
    count = 9
    dma = pltpu.SemaphoreType.DMA
    shape, vmem = jax.ShapeDtypeStruct, pltpu.VMEM
    any_spec, vmem_spec = pl.BlockSpec(memory_space=pl.ANY), pl.BlockSpec(memory_space=pltpu.VMEM)
    return pl.pallas_call(
        functools.partial(forward_kernel, far_count, halo),
        out_shape=[
            shape((width, 3 * width), bf16),
            shape((width, width), bf16),
            shape((width, hid), bf16),
            shape((rows, width), bf16),
            shape((ext, 3 * width), bf16),
            shape((rows, width), bf16),
            shape((rows, width), f32),
            shape((rows, width), bf16),
            shape((rows, hid), bf16),
            shape((rows, hid), bf16),
            shape((rows, width), f32),
            shape((SMALL_ROWS, width), f32),
            shape((1, hid), f32),
        ],
        in_specs=[any_spec] * 7 + [vmem_spec],
        out_specs=[any_spec] * 11 + [vmem_spec] * 2,
        scratch_shapes=[
            vmem((width, 3 * width), bf16),
            vmem((width, width), bf16),
            vmem((width, hid), bf16),
            vmem((width, hid), bf16),
            vmem((2 * dp_size, SMALL_ROWS, width), bf16),
            vmem((rows, width), f32),
            vmem((rows, width), f32),
            vmem((rows, width), bf16),
            vmem((ext, width), bf16),
            vmem((ext, 3 * width), bf16),
            vmem((rows, width), bf16),
            vmem((rows, width), f32),
            vmem((rows, width), f32),
            vmem((rows, width), bf16),
            vmem((rows, hid), bf16),
            vmem((rows, hid), f32),
            vmem((rows, hid), bf16),
            vmem((1, halo + 2 * rows), jnp.int32),
            vmem((rows // halo, halo, 2 * halo), f32),
            dma((2,)),
            dma((11,)),
            dma((count,)),
            dma((2,)),
            dma((2, count, far_count)),
            dma((2, count, far_count)),
            dma((2, count, far_count)),
            dma((2, count, far_count)),
            dma((2, count, 4, far_count)),
        ],
        compiler_params=pltpu.CompilerParams(
            collective_id=2, has_side_effects=True, vmem_limit_bytes=VMEM_BYTES
        ),
        name="forward_pass",
    )(own_qkv, own_out, own_up, own_down, own_small, inputs, cot, ids)


def backward_kernel(far_count, halo, *refs):
    (
        hidden_hbm,
        cot_hbm,
        ln2_hbm,
        grad_pre_hbm,
        w_up_hbm,
        w_out_hbm,
        w_qkv_hbm,
        middle_hbm,
        x_hbm,
        mixed_hbm,
        qkv_hbm,
        ln1_hbm,
        ids_ref,
        params,
        up_sum,
        input_grad_out,
        own_qkv,
        own_out,
        own_up,
        own_down,
        sums,
        hidden,
        cot_ref,
        ln2,
        grad_pre,
        w_up,
        w_out,
        middle,
        mixed,
        qkv,
        ln1,
        turned,
        cot_bf,
        grad_ln,
        grad_mixed,
        grad_qkv,
        p_down,
        p_up,
        p_out,
        p_qkv,
        rest_k,
        rest_v,
        lent,
        back,
        id_ref,
        mask_ref,
        held,
        core_in,
        x_in,
        y_in,
        diag_in,
        far_in,
        sums_in,
        load_sem,
        halo_sem,
        sums_sem,
        core_sem,
        x_sem,
        y_sem,
        diag_x_sem,
        diag_y_sem,
        far_sem,
    ) = refs
    f32, bf16 = jnp.float32, jnp.bfloat16
    rows, width = cot_ref.shape
    own_rows, attn = own_out.shape
    hid = own_up.shape[1]
    cut = hid // 2
    at = Place(far_count)
    loads = {}

    def load(name, source, target):
        copy = pltpu.make_async_copy(source, target, load_sem.at[len(loads)])
        copy.start()
        loads[name] = copy

    load("cot", cot_hbm, cot_ref)
    load("hidden", hidden_hbm, hidden)
    load("ln2", ln2_hbm, ln2)
    load("grad_pre", grad_pre_hbm, grad_pre)
    load("w_up", w_up_hbm, w_up)
    load("middle", middle_hbm, middle)
    load("w_out", w_out_hbm, w_out)
    load("mixed", mixed_hbm, mixed)
    load("qkv", qkv_hbm, qkv)
    load("ln1", ln1_hbm, ln1)
    at.greet()
    sent = []
    x_peer, y_peer, core_peer = at.peer("tensor"), at.peer("near"), at.peer("core")
    order = list(range(1, far_count)) + [0]
    own, by_x, by_y, diag = range(4)
    flips = ((0, 0), (1, 0), (0, 1), (1, 1))

    groups = []

    def add_group(part, block, first, start, size, out):
        offset = groups[-1][5] + groups[-1][4] if groups else 0
        groups.append((part, block, first, start, size, offset, out))

    for half in range(2):
        columns = slice(half * cut, (half + 1) * cut)
        add_group(p_down, hid, 0, half * cut, cut, own_down.at[:, columns])
    for half in range(2):
        columns = slice(half * cut, (half + 1) * cut)
        add_group(p_up, hid, 0, half * cut, cut, own_up.at[:, columns])
    add_group(p_out, attn, 0, 0, attn, own_out)
    per = attn // LANES
    third = 3 * LANES
    for j in range(per):
        add_group(p_qkv, third, 2 * j * third, 0, third, own_qkv.at[j])

    def make(source, target, sems, place, peer):
        return pltpu.make_async_remote_copy(
            src_ref=source,
            dst_ref=target,
            send_sem=sems.at[(0,) + place],
            recv_sem=sems.at[(1,) + place],
            device_id=peer,
            device_id_type=MESH,
        )

    def send(*args):
        copy = make(*args)
        copy.start()
        sent.append(copy)

    def arrived(target, sems, place, peer):
        make(target, target, sems, place, peer).wait_recv()

    def slot(group, kind, step, core):
        part, block, first, start, size, _, _ = groups[group]
        flip_x, flip_y = flips[kind]
        tensor = 1 - at.tensor if flip_x else at.tensor
        near = 1 - at.near if flip_y else at.near
        row = pl.multiple_of(at.index(at.far_at(step), near, core) * own_rows, 16)
        return part.at[pl.ds(row, own_rows), lanes(first + tensor * block + start, size)]

    def columns_of(group):
        return pl.ds(groups[group][5], groups[group][4])

    def core_slot(group, kind, step):
        return core_in.at[kind, step, :, columns_of(group)]

    def parts_of(group):
        offset, size = groups[group][5], groups[group][4]
        half = size // 2 // LANES * LANES
        low, high = pl.ds(offset, half), pl.ds(offset + half, size - half)
        return (low, high) if group % 2 else (high, low)

    def stage_core(group):
        for step in order:
            for kind in (diag, by_x, by_y, own):
                source = slot(group, kind, step, 1 - at.core)
                target = core_slot(group, kind, step)
                send(source, target, core_sem, (group, kind, step), core_peer)

    def stage_meet(group):
        for step in order:
            for kind in (diag, by_x, by_y, own):
                target = core_slot(group, kind, step)
                arrived(target, core_sem, (group, kind, step), core_peer)
                mine = slot(group, kind, step, at.core)
                target[...] = (mine[...].astype(f32) + target[...].astype(f32)).astype(bf16)
                if kind == diag:
                    via_y, via_x = parts_of(group)
                    from_y, from_x = diag_in.at[step, :, via_y], diag_in.at[step, :, via_x]
                    corner = core_in.at[diag, step]
                    send(corner.at[:, via_y], from_y, diag_y_sem, (group, step), y_peer)
                    send(corner.at[:, via_x], from_x, diag_x_sem, (group, step), x_peer)

    def stage_corner(group):
        via_y, via_x = parts_of(group)
        columns = columns_of(group)
        for step in order:
            for kind, via, sem, diag_peer, into, into_sem, peer in (
                (by_x, via_y, diag_y_sem, y_peer, x_in, x_sem, x_peer),
                (by_y, via_x, diag_x_sem, x_peer, y_in, y_sem, y_peer),
            ):
                source = diag_in.at[step, :, via]
                arrived(source, sem, (group, step), diag_peer)
                target = core_in.at[kind, step, :, via]
                target[...] = (target[...].astype(f32) + source[...].astype(f32)).astype(bf16)
                place = into.at[step, :, columns]
                send(core_in.at[kind, step, :, columns], place, into_sem, (group, step), peer)

    def stage_merge(group):
        columns = columns_of(group)
        for step in order:
            arrived(x_in.at[step, :, columns], x_sem, (group, step), x_peer)
            arrived(y_in.at[step, :, columns], y_sem, (group, step), y_peer)
            merged = (
                core_in[own, step, :, columns].astype(f32)
                + x_in[step, :, columns].astype(f32)
                + y_in[step, :, columns].astype(f32)
            )
            if step:
                core_in[own, step, :, columns] = merged.astype(bf16)
                source, target = core_in.at[own, step, :, columns], far_in.at[step, :, columns]
                send(source, target, far_sem, (group, step), at.peer("far", step))
            else:
                groups[group][6][...] = merged

    def stage_far(group):
        columns = columns_of(group)
        out = groups[group][6]
        for step in range(1, far_count):
            place = far_in.at[step, :, columns]
            arrived(place, far_sem, (group, step), at.peer("far", step))
        total = out[...]
        for step in range(1, far_count):
            total = total + far_in[step, :, columns].astype(f32)
        out[...] = total

    def turn(source):
        def one(i):
            part = pl.multiple_of(i * halo, halo)
            turned[:, pl.ds(part, halo)] = source[pl.ds(part, halo), :].T

        loop(rows // halo, one)

    def contract(right, first, part, count):
        def one(i):
            columns = lanes(first + i * TILE)
            grad = jnp.dot(turned[...], right[:, columns], preferred_element_type=f32)
            part[:, columns] = grad.astype(bf16)

        loop(count // TILE, one)

    def contract_half(right, part, half):
        for tensor in range(2):
            contract(right, tensor * hid + half * cut, part, cut)

    def rows_at(i):
        return pl.ds(pl.multiple_of(i * halo, halo), halo)

    def start():
        loads["cot"].wait()

        def one(i):
            cot_bf[rows_at(i), :] = cot_ref[rows_at(i), :].astype(bf16)

        loop(rows // halo, one)
        turn(cot_bf)
        held[...] = jnp.zeros_like(held)
        for row in range(4):
            base = UP_BIAS + row
            held[base : base + 1, :] = up_sum[:, row * width : (row + 1) * width]

    def back_up():
        def one(i):
            out_rows = pl.ds(pl.multiple_of(i * TILE, TILE), TILE)
            grad_ln[:, lanes(i * TILE)] = times_transposed(grad_pre[...], w_up[out_rows, :])

        loop(width // TILE, one)

    def add_sum(row, value):
        held[row : row + 1, :] += jnp.sum(value, axis=0, keepdims=True)

    def normed_rows(source, i):
        data = source[rows_at(i), :]
        centred = data - jnp.mean(data, axis=-1, keepdims=True)
        inv_std = lax.rsqrt(jnp.mean(centred * centred, axis=-1, keepdims=True) + eps)
        return centred * inv_std, inv_std

    def back_second_norm():
        def one(i):
            normed, inv_std = normed_rows(middle, i)
            grad = grad_ln[rows_at(i), :]
            cot = cot_ref[rows_at(i), :]
            add_sum(3, grad * normed)
            add_sum(4, grad)
            grad_middle = cot + norm_backward(grad, normed, inv_std, params[3:4, :])
            add_sum(5, cot)
            add_sum(2, grad_middle)
            middle[rows_at(i), :] = grad_middle
            cot_bf[rows_at(i), :] = grad_middle.astype(bf16)

        loop(rows // halo, one)
        turn(cot_bf)

    def back_out():
        def one(i):
            columns = lanes(i * TILE)
            part = jnp.dot(cot_bf[...], w_out[:, columns], preferred_element_type=f32)
            grad_mixed[:, columns] = part.astype(bf16)

        loop(width // TILE, one)

    def masks():
        id_ref[:, :halo] = jnp.full((1, halo), -1, jnp.int32)
        id_ref[:, halo:] = ids_ref[...]
        window = 2 * halo
        row = lax.broadcasted_iota(jnp.int32, (halo, window), 0)
        column = lax.broadcasted_iota(jnp.int32, (halo, window), 1)
        causal = column <= row + halo
        for block in range(rows // halo):
            first = at.tensor * rows + block * halo
            keys = id_ref[:, lanes(first, window)]
            queries = jnp.broadcast_to(id_ref[:, lanes(first + halo, halo)], (halo, halo)).T
            same = jnp.concatenate([queries, queries], axis=1) == keys
            mask_ref[block] = jnp.where(same & causal, 1.0, 0.0)

    def back_attention(j):
        lane = lax.broadcasted_iota(jnp.int32, (halo, LANES), 1)

        def one(i):
            pair = i * per + j
            grad_at = 2 * j * third + i * third
            dq_at, dk_at = lanes(grad_at, LANES), lanes(grad_at + LANES, LANES)
            dv_at = lanes(grad_at + 2 * LANES, LANES)
            rest_at = lanes((2 * j + i) * LANES, LANES)
            lent_k, lent_v = (lanes((4 * j + 2 * i + c) * LANES, LANES) for c in range(2))
            q_at, k_at = lanes(pair * LANES, LANES), lanes(width + pair * LANES, LANES)
            v_at = lanes(2 * width + pair * LANES, LANES)
            carry_k = carry_v = None
            query_sum = jnp.zeros((1, LANES), f32)
            value_sum = jnp.zeros((1, LANES), f32)
            for block in range(rows // halo):
                first = block * halo
                query = qkv[first + halo : first + 2 * halo, q_at]
                keys = qkv[first : first + 2 * halo, k_at]
                values = qkv[first : first + 2 * halo, v_at]
                allowed = mask_ref[block] > 0.5
                grad = grad_mixed[first : first + halo, q_at]
                product = grad.astype(f32) * mixed[first : first + halo, q_at].astype(f32)
                query_grad = key_grad = value_grad = None
                for head in range(LANES // HD):
                    mine = (lane >= head * HD) & (lane < (head + 1) * HD)
                    query_head = jnp.where(mine, query, jnp.zeros_like(query))
                    grad_head = jnp.where(mine, grad, jnp.zeros_like(grad))
                    delta = jnp.sum(jnp.where(mine, product, 0.0), axis=-1, keepdims=True)
                    scores = times_transposed(query_head, keys) * scale_factor
                    weight = jnp.where(allowed, jnp.exp(scores), 0.0)
                    probs = weight / jnp.sum(weight, axis=-1, keepdims=True)
                    grad_probs = times_transposed(grad_head, values)
                    grad_scores = (probs * (grad_probs - delta) * scale_factor).astype(bf16)
                    value_part = contract_rows(probs.astype(bf16), grad_head)
                    key_part = contract_rows(grad_scores, query_head)
                    part = jnp.dot(grad_scores, keys, preferred_element_type=f32)
                    if head == 0:
                        query_grad, key_grad, value_grad = part, key_part, value_part
                    else:
                        query_grad = jnp.where(mine, part, query_grad)
                        key_grad, value_grad = key_grad + key_part, value_grad + value_part
                query_sum += jnp.sum(query_grad, axis=0, keepdims=True)
                grad_qkv[first : first + halo, dq_at] = query_grad.astype(bf16)
                if block == 0:
                    lent[:, lent_k] = key_grad[:halo].astype(bf16)
                    lent[:, lent_v] = value_grad[:halo].astype(bf16)
                else:
                    done = pl.ds(first - halo, halo)
                    grad_qkv[done, dk_at] = (carry_k + key_grad[:halo]).astype(bf16)
                    whole = carry_v + value_grad[:halo]
                    grad_qkv[done, dv_at] = whole.astype(bf16)
                    value_sum += jnp.sum(whole, axis=0, keepdims=True)
                carry_k, carry_v = key_grad[halo:], value_grad[halo:]
            rest_k[:, rest_at] = carry_k
            rest_v[:, rest_at] = carry_v
            held[Q_BIAS : Q_BIAS + 1, q_at] = query_sum
            held[V_BIAS : V_BIAS + 1, q_at] = value_sum

        loop(2, one)

    def lent_at(j):
        return pl.ds(4 * j * LANES, 4 * LANES)

    def lend(j):
        send(lent.at[:, lent_at(j)], back.at[:, lent_at(j)], halo_sem, (j,), x_peer)

    def returned(j):
        arrived(back.at[:, lent_at(j)], halo_sem, (j,), x_peer)
        last = pl.ds(rows - halo, halo)
        for i in range(2):
            grad_at = 2 * j * third + i * third
            base, rest_at = (4 * j + 2 * i) * LANES, pl.ds((2 * j + i) * LANES, LANES)
            key_grad = rest_k[:, rest_at] + back[:, base : base + LANES].astype(f32)
            whole = rest_v[:, rest_at] + back[:, base + LANES : base + 2 * LANES].astype(f32)
            grad_qkv[last, grad_at + LANES : grad_at + 2 * LANES] = key_grad.astype(bf16)
            grad_qkv[last, grad_at + 2 * LANES : grad_at + third] = whole.astype(bf16)
            v_at = pl.ds((i * per + j) * LANES, LANES)
            held[V_BIAS : V_BIAS + 1, v_at] += jnp.sum(whole, axis=0, keepdims=True)

    def back_project():
        for j, i, lead in qkv_blocks:
            loads["w_qkv", j, i, lead].wait()

        def one(i):
            out_rows = pl.ds(pl.multiple_of(i * TILE, TILE), TILE)
            weights = w_up[out_rows, : 3 * width]
            grad_ln[:, lanes(i * TILE)] = times_transposed(grad_qkv[...], weights)

        loop(width // TILE, one)

    def back_first_norm():
        loads["x"].wait()

        def one(i):
            normed, inv_std = normed_rows(cot_ref, i)
            grad = grad_ln[rows_at(i), :]
            add_sum(0, grad * normed)
            add_sum(1, grad)
            middle[rows_at(i), :] += norm_backward(grad, normed, inv_std, params[0:1, :])

        loop(rows // halo, one)

    d0, d1, u0, u1, o0 = range(5)
    qkv_blocks = [(j, i, lead) for j in range(per) for i in range(2) for lead in range(3)]

    def qkv_grads(j):
        returned(j)
        contract(grad_qkv, 2 * j * third, p_qkv, 2 * third)
        stage_core(o0 + 1 + j)

    last = o0 + per
    early = [
        lambda: (stage_merge(u0), stage_far(d1), stage_corner(o0)),
        lambda: (stage_merge(u1), stage_far(u0)),
        lambda: (stage_merge(o0), stage_far(u1)),
    ]

    start()
    loads["hidden"].wait()
    contract_half(hidden, p_down, 0)
    stage_core(d0)
    contract_half(hidden, p_down, 1)
    stage_core(d1)
    stage_meet(d0)
    loads["ln2"].wait()
    loads["grad_pre"].wait()
    turn(ln2)
    contract_half(grad_pre, p_up, 0)
    stage_core(u0)
    stage_meet(d1)
    stage_corner(d0)
    contract_half(grad_pre, p_up, 1)
    stage_core(u1)
    loads["w_up"].wait()
    back_up()
    for j, i, lead in qkv_blocks:
        source = pl.ds(lead * width + i * attn + j * LANES, LANES)
        target = pl.ds((2 * j + i) * third + lead * LANES, LANES)
        load(("w_qkv", j, i, lead), w_qkv_hbm.at[:, source], w_up.at[:, target])
    stage_meet(u0)
    stage_corner(d1)
    stage_merge(d0)
    loads["middle"].wait()
    back_second_norm()
    load("x", x_hbm, cot_ref)
    loads["mixed"].wait()
    contract(mixed, 0, p_out, width)
    stage_core(o0)
    stage_meet(u1)
    stage_corner(u0)
    stage_merge(d1)
    stage_far(d0)
    loads["w_out"].wait()
    back_out()
    stage_meet(o0)
    stage_corner(u1)
    masks()
    loads["qkv"].wait()
    loads["ln1"].wait()
    turn(ln1)
    for j in range(per):
        back_attention(j)
        lend(j)
        if early:
            early.pop(0)()
        if j:
            qkv_grads(j - 1)
        if j > 1:
            stage_meet(o0 + j - 1)
    for extra in early:
        extra()
    qkv_grads(per - 1)
    if per > 1:
        stage_meet(last - 1)
    for group in range(o0 + 1, last - 1):
        stage_corner(group)
    stage_far(o0)
    stage_meet(last)
    if per > 1:
        stage_corner(last - 1)
    back_project()
    stage_corner(last)
    for group in range(o0 + 1, last - 1):
        stage_merge(group)
    back_first_norm()
    result = pltpu.make_async_copy(middle, input_grad_out, load_sem.at[len(loads)])
    result.start()
    sums[0] = held[...]
    send(sums.at[0], sums_in.at[0], sums_sem, (0,), core_peer)
    if per > 1:
        stage_merge(last - 1)
    arrived(sums_in.at[0], sums_sem, (0,), core_peer)
    sums[1] = sums[0] + sums_in[0]
    send(sums.at[1], sums_in.at[1], sums_sem, (1,), x_peer)
    stage_merge(last)
    arrived(sums_in.at[1], sums_sem, (1,), x_peer)
    sums[2] = sums[1] + sums_in[1]
    send(sums.at[2], sums_in.at[2], sums_sem, (2,), y_peer)
    for group in range(o0 + 1, last - 1):
        stage_far(group)
    arrived(sums_in.at[2], sums_sem, (2,), y_peer)
    sums[3] = sums[2] + sums_in[2]
    for step in range(1, far_count):
        send(sums.at[3], sums_in.at[2 + step], sums_sem, (2 + step,), at.peer("far", step))
    for group in range(max(o0 + 1, last - 1), last + 1):
        stage_far(group)
    total = sums[3]
    for step in range(1, far_count):
        arrived(sums_in.at[2 + step], sums_sem, (2 + step,), at.peer("far", step))
        total = total + sums_in[2 + step]
    sums[4] = total
    result.wait()
    for copy in sent:
        copy.wait_send()


def backward_pass(arrays, ids, params, up_sum, halo, own_rows, attn):
    f32, bf16 = jnp.float32, jnp.bfloat16
    hidden, cot = arrays[0], arrays[1]
    far_count = lax.axis_size("dp") // 4
    rows, width = cot.shape
    hid = hidden.shape[1]
    own_hid = hid // 2
    ext = rows + halo
    per = attn // LANES
    count = 5 + per
    all_columns = 4 * attn + 2 * own_hid
    block = (far_count, own_rows, all_columns)
    dma = pltpu.SemaphoreType.DMA
    shape, vmem = jax.ShapeDtypeStruct, pltpu.VMEM
    any_spec, vmem_spec = pl.BlockSpec(memory_space=pl.ANY), pl.BlockSpec(memory_space=pltpu.VMEM)
    return pl.pallas_call(
        functools.partial(backward_kernel, far_count, halo),
        out_shape=[
            shape((rows, width), f32),
            shape((per, own_rows, 3 * LANES), f32),
            shape((own_rows, attn), f32),
            shape((own_rows, own_hid), f32),
            shape((own_rows, own_hid), f32),
            shape((5, SMALL_ROWS, width), f32),
        ],
        in_specs=[any_spec] * 12 + [vmem_spec] * 3,
        out_specs=[any_spec] + [vmem_spec] * 5,
        scratch_shapes=[
            vmem((rows, hid), bf16),
            vmem((rows, width), f32),
            vmem((rows, width), bf16),
            vmem((rows, hid), bf16),
            vmem((width, hid), bf16),
            vmem((width, width), bf16),
            vmem((rows, width), f32),
            vmem((rows, width), bf16),
            vmem((ext, 3 * width), bf16),
            vmem((rows, width), bf16),
            vmem((width, rows), bf16),
            vmem((rows, width), bf16),
            vmem((rows, width), f32),
            vmem((rows, width), bf16),
            vmem((rows, 3 * width), bf16),
            vmem((width, hid), bf16),
            vmem((width, hid), bf16),
            vmem((width, width), bf16),
            vmem((width, 3 * width), bf16),
            vmem((halo, width), f32),
            vmem((halo, width), f32),
            vmem((halo, 2 * width), bf16),
            vmem((halo, 2 * width), bf16),
            vmem((1, halo + 2 * rows), jnp.int32),
            vmem((rows // halo, halo, 2 * halo), f32),
            vmem((SMALL_ROWS, width), f32),
            vmem((4,) + block, bf16),
            vmem(block, bf16),
            vmem(block, bf16),
            vmem(block, bf16),
            vmem(block, bf16),
            vmem((2 + far_count, SMALL_ROWS, width), f32),
            dma((12 + 6 * per,)),
            dma((2, per)),
            dma((2, 2 + far_count)),
            dma((2, count, 4, far_count)),
            dma((2, count, far_count)),
            dma((2, count, far_count)),
            dma((2, count, far_count)),
            dma((2, count, far_count)),
            dma((2, count, far_count)),
        ],
        compiler_params=pltpu.CompilerParams(
            collective_id=3, has_side_effects=True, vmem_limit_bytes=67043328
        ),
        name="backward_pass",
    )(*arrays, ids, params, up_sum)


def placed_small(vectors, qv_bias, up_bias, width):
    dp_size, tensor_size = lax.axis_size("dp"), lax.axis_size("tensor")
    dp, tensor = lax.axis_index("dp"), lax.axis_index("tensor")
    mine = lax.broadcasted_iota(jnp.int32, (dp_size * tensor_size, 1), 0) == dp * tensor_size + tensor
    stacked = jnp.stack(vectors)
    zero = jnp.zeros((), stacked.dtype)
    placed = jnp.where(mine[None], stacked[:, None, :], zero).reshape(len(vectors), width)
    my_dp = lax.broadcasted_iota(jnp.int32, (1, 1, 1, dp_size, 1), 3) == dp
    my_tensor = lax.broadcasted_iota(jnp.int32, (1, tensor_size, 1, 1, 1), 1) == tensor
    spot = my_dp & my_tensor
    qv = jnp.where(spot, qv_bias[:, None, :, None, :], zero).reshape(2, width)
    up = jnp.where(spot, up_bias[None, None, :, None, :], zero).reshape(-1, width)
    parts = jnp.concatenate([placed, qv, up])
    return jnp.pad(parts, ((0, SMALL_ROWS - parts.shape[0]), (0, 0)))


def on_device_small(
    inputs,
    seq_ids,
    norm1_gain,
    norm1_shift,
    qkv_weight,
    qv_bias,
    out_weight,
    out_bias,
    norm2_gain,
    norm2_shift,
    up_weight,
    up_bias,
    down_weight,
    down_bias,
    out_cotangent,
):
    f32, bf16 = jnp.float32, jnp.bfloat16
    dp_size, tensor_size = lax.axis_size("dp"), lax.axis_size("tensor")
    tensor = lax.axis_index("tensor")
    local_rows, width = inputs.shape
    halo = min(SEQ_MAX, local_rows)
    rows = up_weight.shape[0]
    attn = qkv_weight.shape[2]
    hid = up_weight.shape[1]
    vec = norm1_gain.shape[0]
    heads = qv_bias.shape[1]
    bias_cols = qv_bias.shape[2]
    up_rows, up_cols = up_bias.shape

    vectors = [norm1_gain, norm1_shift, out_bias, norm2_gain, norm2_shift, down_bias]
    vectors += [qv_bias.reshape(-1), up_bias.reshape(-1)]
    small_rows = len(vectors)
    small = jnp.stack([jnp.pad(vector, (0, LANES - vector.shape[0])) for vector in vectors])
    small = jnp.pad(small, ((0, rows - small_rows), (0, 0)))
    full_qkv, full_out, full_up, full_down, small_all, halo_rows = gather_weights(
        [qkv_weight, out_weight.T, up_weight, down_weight.T, small], inputs[local_rows - halo :]
    )
    full_qkv = full_qkv.reshape(width, -1)
    full_up = full_up.reshape(width, -1)
    full_down = full_down.reshape(width, -1)
    full_out = full_out.reshape(width, -1)
    small_all = small_all[:, :small_rows].reshape(dp_size, small_rows, tensor_size, LANES)
    gain_one, shift_one, bias_out, gain_two, shift_two, bias_down = (
        small_all[:, i, :, :vec].reshape(-1) for i in range(6)
    )
    qv_full = (
        small_all[:, 6, :, : qv_bias.size]
        .reshape(dp_size, tensor_size, 2, heads, bias_cols)
        .transpose(2, 1, 3, 0, 4)
        .reshape(2, tensor_size, attn)
    )
    up_bias_full = (
        small_all[:, 7, :, : up_bias.size]
        .reshape(dp_size, tensor_size, up_rows, up_cols)
        .transpose(1, 2, 0, 3)
        .reshape(-1)
    )
    qkv_bias = jnp.stack([qv_full[0], jnp.zeros_like(qv_full[0]), qv_full[1]], axis=1)
    qkv_bias = qkv_bias.reshape(-1).astype(f32)

    first_row = tensor * local_rows
    padded_ids = jnp.concatenate([jnp.full((halo,), -1, jnp.int32), seq_ids[0]])
    ext_ids = lax.dynamic_slice_in_dim(padded_ids, first_row, local_rows + halo)
    id_row, id_col = ext_ids[None, :], ext_ids[halo:, None]

    normed_one, inv_one, ln_one = norm_forward(inputs, gain_one, shift_one)
    ln_halo = norm_forward(halo_rows, gain_one, shift_one)[2]
    ln_ext = jnp.concatenate([ln_halo, ln_one])
    qkv = (jnp.dot(ln_ext, full_qkv, preferred_element_type=f32) + qkv_bias).astype(bf16)
    mixed = attend(qkv, id_row, id_col, halo, tensor_size)
    middle = inputs + times_transposed(mixed, full_out) + bias_out.astype(f32)
    normed_two, inv_two, ln_two = norm_forward(middle, gain_two, shift_two)
    pre_act = jnp.dot(ln_two, full_up, preferred_element_type=f32) + up_bias_full.astype(f32)
    hidden = gelu_forward(pre_act).astype(bf16)
    layer_out = middle + times_transposed(hidden, full_down) + bias_down.astype(f32)

    cot_bf = out_cotangent.astype(bf16)
    down_grad = contract_rows(cot_bf, hidden).astype(bf16)
    grad_pre = gelu_backward(pre_act, jnp.dot(cot_bf, full_down, preferred_element_type=f32))
    grad_pre_bf = grad_pre.astype(bf16)
    up_grad = contract_rows(ln_two, grad_pre_bf).astype(bf16)
    up_bias_grad = jnp.sum(grad_pre, axis=0)
    grad_ln_two = times_transposed(grad_pre_bf, full_up)
    gain_two_grad = jnp.sum(grad_ln_two * normed_two, axis=0)
    shift_two_grad = jnp.sum(grad_ln_two, axis=0)
    grad_middle = out_cotangent + norm_backward(grad_ln_two, normed_two, inv_two, gain_two)
    bias_down_grad = jnp.sum(out_cotangent, axis=0)
    bias_out_grad = jnp.sum(grad_middle, axis=0)
    mid_bf = grad_middle.astype(bf16)
    out_grad = contract_rows(mid_bf, mixed).astype(bf16)
    grad_mixed = jnp.dot(mid_bf, full_out, preferred_element_type=f32).astype(bf16)
    query_grad, key_ext, value_ext = attend_back(
        qkv, id_row, id_col, mixed, grad_mixed, halo, tensor_size
    )
    lent = jnp.concatenate([key_ext[:halo], value_ext[:halo]], axis=1).astype(bf16)
    ring = [((i + 1) % tensor_size, i) for i in range(tensor_size)]
    back = lax.ppermute(lent, "tensor", ring).astype(f32)
    rest = local_rows - halo

    def returned(ext, part):
        own = ext[halo:]
        return jnp.concatenate([own[:rest], own[rest:] + part])

    key_grad = returned(key_ext, back[:, :width])
    value_grad = returned(value_ext, back[:, width:])
    pieces = []
    for t in range(tensor_size):
        for piece in (query_grad, key_grad, value_grad):
            pieces.append(piece[:, t * attn : (t + 1) * attn].astype(bf16))
    grad_qkv = jnp.concatenate(pieces, axis=1)
    qkv_grad = contract_rows(ln_one, grad_qkv).astype(bf16)
    qv_grad = jnp.stack([jnp.sum(query_grad, axis=0), jnp.sum(value_grad, axis=0)])
    grad_ln_one = times_transposed(grad_qkv, full_qkv)
    gain_one_grad = jnp.sum(grad_ln_one * normed_one, axis=0)
    shift_one_grad = jnp.sum(grad_ln_one, axis=0)
    input_grad = grad_middle + norm_backward(grad_ln_one, normed_one, inv_one, gain_one)

    vectors = [gain_one_grad, shift_one_grad, bias_out_grad]
    vectors += [gain_two_grad, shift_two_grad, bias_down_grad]
    vectors = [vector.reshape(dp_size, tensor_size, vec) for vector in vectors] + [
        qv_grad.reshape(2, tensor_size, heads, dp_size, bias_cols)
        .transpose(3, 1, 0, 2, 4)
        .reshape(dp_size, tensor_size, -1),
        up_bias_grad.reshape(tensor_size, up_rows, dp_size, up_cols)
        .transpose(2, 0, 1, 3)
        .reshape(dp_size, tensor_size, -1),
    ]
    small_grad = jnp.stack(
        [jnp.pad(one.astype(bf16), ((0, 0), (0, 0), (0, LANES - one.shape[2]))) for one in vectors],
        axis=1,
    ).reshape(dp_size, small_rows, tensor_size * LANES)
    small_grad = jnp.pad(small_grad, ((0, 0), (0, rows - small_rows), (0, 0)))

    parts = [qkv_grad, out_grad, up_grad, down_grad, small_grad]
    own_qkv, own_out, own_up, own_down, own_small = scatter_grads(
        [part.reshape(dp_size, rows, -1) for part in parts],
        [(3, rows, attn), (rows, attn), (rows, hid), (rows, hid), (rows, LANES)],
    )
    vectors = [own_small[i, :vec] for i in range(6)]
    gain_one_own, shift_one_own, bias_out_own, gain_two_own, shift_two_own, bias_down_own = vectors
    return (
        layer_out,
        input_grad,
        gain_one_own,
        shift_one_own,
        own_qkv,
        own_small[6, : qv_bias.size].reshape(qv_bias.shape),
        own_out.T,
        bias_out_own,
        gain_two_own,
        shift_two_own,
        own_up,
        own_small[7, : up_bias.size].reshape(up_bias.shape),
        own_down.T,
        bias_down_own,
    )


def on_device(
    inputs,
    seq_ids,
    norm1_gain,
    norm1_shift,
    qkv_weight,
    qv_bias,
    out_weight,
    out_bias,
    norm2_gain,
    norm2_shift,
    up_weight,
    up_bias,
    down_weight,
    down_bias,
    out_cotangent,
):
    rows = up_weight.shape[0]
    if rows % 16 or lax.axis_size("tensor") != 2:
        return on_device_small(
            inputs,
            seq_ids,
            norm1_gain,
            norm1_shift,
            qkv_weight,
            qv_bias,
            out_weight,
            out_bias,
            norm2_gain,
            norm2_shift,
            up_weight,
            up_bias,
            down_weight,
            down_bias,
            out_cotangent,
        )
    f32, bf16 = jnp.float32, jnp.bfloat16
    dp_size, tensor_size = lax.axis_size("dp"), lax.axis_size("tensor")
    tensor = lax.axis_index("tensor")
    local_rows, width = inputs.shape
    halo = min(SEQ_MAX, local_rows)
    attn = qkv_weight.shape[2]
    hid = up_weight.shape[1]
    vec = norm1_gain.shape[0]
    heads = qv_bias.shape[1]
    bias_cols = qv_bias.shape[2]
    up_rows, up_cols = up_bias.shape

    small = placed_small(
        [norm1_gain, norm1_shift, out_bias, norm2_gain, norm2_shift, down_bias],
        qv_bias,
        up_bias,
        width,
    )
    (
        full_qkv,
        full_out,
        full_up,
        ln_one,
        qkv,
        mixed,
        middle,
        ln_two,
        hidden,
        grad_pre_bf,
        layer_out,
        params,
        up_bias_grad,
    ) = forward_pass(
        qkv_weight,
        out_weight.T,
        up_weight,
        down_weight.T,
        small,
        inputs,
        out_cotangent,
        seq_ids,
        halo,
    )
    input_grad, own_qkv, own_out, own_up, own_down, sums = backward_pass(
        [
            hidden,
            out_cotangent,
            ln_two,
            grad_pre_bf,
            full_up,
            full_out,
            full_qkv,
            middle,
            inputs,
            mixed,
            qkv,
            ln_one,
        ],
        seq_ids,
        params,
        up_bias_grad,
        halo,
        rows,
        attn,
    )
    dp = lax.axis_index("dp")
    sums = sums[4]
    vectors = lax.dynamic_slice_in_dim(sums[:6], (dp * tensor_size + tensor) * vec, vec, axis=1)
    qv_sums = sums[Q_BIAS : V_BIAS + 1].reshape(2, tensor_size, heads, dp_size, bias_cols)
    qv_own = lax.dynamic_slice(
        qv_sums, (0, tensor, 0, dp, 0), (2, 1, heads, 1, bias_cols)
    ).reshape(qv_bias.shape)
    up_sums = sums[UP_BIAS : UP_BIAS + 4].reshape(tensor_size, up_rows, dp_size, up_cols)
    up_own = lax.dynamic_slice(up_sums, (tensor, 0, dp, 0), (1, up_rows, 1, up_cols)).reshape(
        up_bias.shape
    )
    return (
        layer_out,
        input_grad,
        vectors[0],
        vectors[1],
        own_qkv.reshape(-1, rows, 3, LANES).transpose(2, 1, 0, 3).reshape(3, rows, attn),
        qv_own,
        own_out.T,
        vectors[2],
        vectors[3],
        vectors[4],
        own_up,
        up_own,
        own_down.T,
        vectors[5],
    )


def solution(mesh):
    placed = (
        P(("dp", "tensor"), None),
        P("dp", None),
        P(("dp", "tensor")),
        P(("dp", "tensor")),
        P(None, "dp", "tensor"),
        P(None, "tensor", "dp"),
        P("tensor", "dp"),
        P(("dp", "tensor")),
        P(("dp", "tensor")),
        P(("dp", "tensor")),
        P("dp", "tensor"),
        P("tensor", "dp"),
        P("tensor", "dp"),
        P(("dp", "tensor")),
        P(("dp", "tensor"), None),
    )
    return jax.shard_map(
        on_device,
        mesh=mesh,
        in_specs=placed,
        out_specs=(
            P(("dp", "tensor"), None),
            P(("dp", "tensor"), None),
            P(("dp", "tensor")),
            P(("dp", "tensor")),
            P(None, "dp", "tensor"),
            P(None, "tensor", "dp"),
            P("tensor", "dp"),
            P(("dp", "tensor")),
            P(("dp", "tensor")),
            P(("dp", "tensor")),
            P("dp", "tensor"),
            P("tensor", "dp"),
            P("tensor", "dp"),
            P(("dp", "tensor")),
        ),
        check_vma=False,
    )
```
